32 devices in a mesh: dp: 8 (over z, core), tensor: 4 (over y, x).
Axes of the slice: x: 2, y: 2, z: 4, core: 2. Of those that a mesh axis runs over, the one named last changes fastest.
Arguments:
- tokens: bfloat16 [32768, 1024], P(('dp', 'tensor')), may hold values from -6 to 6
- lengths: int32 [16], P('dp'), may hold values from 512 to 2048, as said below
- out_grad: bfloat16 [32768, 1024], P(('dp', 'tensor')), may hold values from -6 to 6
- ln1_gain: float32 [1024], replicated, may hold values from 0.5 to 1.5
- ln2_gain: float32 [1024], replicated, may hold values from 0.5 to 1.5
- onorm_gain: float32 [128], replicated, may hold values from 0.5 to 1.5
- a_log: float32 [8], replicated, may hold values from -6 to 0.5
- dt_bias: float32 [8], replicated, may hold values from -4 to 0
- w_query: bfloat16 [1024, 1024], P('dp', 'tensor'), may hold values from -0.1875 to 0.1875
- w_key: bfloat16 [1024, 2048], P('dp', 'tensor'), may hold values from -0.1875 to 0.1875
- w_value: bfloat16 [1024, 2048], P('dp', 'tensor'), may hold values from -0.1875 to 0.1875
- w_rates: bfloat16 [1024, 24], P('dp', 'tensor'), may hold values from -0.1875 to 0.1875
- w_outgate: bfloat16 [1024, 1024], P('dp', 'tensor'), may hold values from -0.1875 to 0.1875
- w_out: bfloat16 [1024, 1024], P('tensor', 'dp'), may hold values from -0.375 to 0.375
- w_gate: bfloat16 [1024, 2816], P('dp', 'tensor'), may hold values from -0.1875 to 0.1875
- w_up: bfloat16 [1024, 2816], P('dp', 'tensor'), may hold values from -0.1875 to 0.1875
- w_down: bfloat16 [2816, 1024], P('tensor', 'dp'), may hold values from -0.21875 to 0.21875
Outputs:
- block_out: bfloat16 [32768, 1024], P(('dp', 'tensor'))
- tokens_grad: bfloat16 [32768, 1024], P(('dp', 'tensor'))
- ln1_gain_grad: float32 [1024], replicated
- ln2_gain_grad: float32 [1024], replicated
- onorm_gain_grad: float32 [128], replicated
- a_log_grad: float32 [8], replicated
- dt_bias_grad: float32 [8], replicated
- w_query_grad: float32 [1024, 1024], P('dp', 'tensor')
- w_key_grad: float32 [1024, 2048], P('dp', 'tensor')
- w_value_grad: float32 [1024, 2048], P('dp', 'tensor')
- w_rates_grad: float32 [1024, 24], P('dp', 'tensor')
- w_outgate_grad: float32 [1024, 1024], P('dp', 'tensor')
- w_out_grad: float32 [1024, 1024], P('tensor', 'dp')
- w_gate_grad: float32 [1024, 2816], P('dp', 'tensor')
- w_up_grad: float32 [1024, 2816], P('dp', 'tensor')
- w_down_grad: float32 [2816, 1024], P('tensor', 'dp')
The draws below stay inside these ranges and needn't reach their ends.
Inputs may be any that keep to these rules, and one draw needn't show every extreme that they name: `lengths`: valid positions of each sequence; the positions after them are padding; in every draw some sequence has all 2048 positions valid.
All inputs are finite; a program needn't handle non-finite values.
Results may differ from the reference program's by a relative error of at most 0.017.
Values may be sent and summed in bfloat16 or wider, within the bound.
No kernel may reach another device: no remote copies, remote signals or barrier semaphores. Data moves between devices by JAX's collectives and lax.ppermute only.
A program may use at most 448 MiB of HBM per device.

```python
import jax
import jax.numpy as jnp
from jax import lax

D = 1024
H = 8
HEAD = 128
NH = 2
FF = 2816
CT = 64
LEN = 2048
SEQS = 16
TOKENS = 32768


def draw_lengths(key, part):
    first_key, second_key = jax.random.split(jax.random.fold_in(key, 11))
    ragged = jax.random.randint(first_key, (SEQS,), LEN // 4, LEN + 1)
    chosen = jax.random.randint(second_key, (), 0, SEQS)
    return jnp.where(jnp.arange(SEQS) == chosen, LEN, ragged).astype(jnp.int32)


def level_of(key, dims, shards, smallest, top_value):
    level, own = 1.0, jax.random.fold_in(key, 6)
    for position, blocks in shards:
        draws = jnp.exp(jax.random.uniform(jax.random.fold_in(own, position), (blocks,), jnp.float32, smallest / len(shards), top_value / len(shards)))
        level = level * jnp.repeat(draws, dims[position] // blocks).reshape([-1 if axis == position else 1 for axis in range(len(dims))])
    return level


def normal_values(own_key, dims, scale, reach, cuts=(), held_as=jnp.bfloat16):
    level = level_of(own_key, dims, cuts, -0.22, 0.18) if cuts else 1.0
    drawn = jax.random.normal(own_key, dims, jnp.float32) * scale * level
    return jnp.minimum(jnp.maximum(drawn, -reach), reach).astype(held_as)


def setup_inputs(seed: int = 0) -> dict:
    splits = jax.random.split(jax.random.key(seed), 18)
    tokens = normal_values(splits[0], (TOKENS, D), 1.0, 6.0, ((0, 32),))
    lengths = draw_lengths(jax.random.fold_in(splits[17], 71), 0)
    out_grad = normal_values(splits[2], (TOKENS, D), 1.0, 6.0, ((0, 32),))
    ln1_gain = jnp.clip(1.0 + 0.1 * jax.random.normal(splits[3], (D,), jnp.float32), 0.5, 1.5)
    ln2_gain = jnp.clip(1.0 + 0.1 * jax.random.normal(splits[4], (D,), jnp.float32), 0.5, 1.5)
    onorm_gain = jnp.clip(1.0 + 0.1 * jax.random.normal(splits[5], (HEAD,), jnp.float32), 0.5, 1.5)
    a_log = jnp.clip(jax.random.uniform(splits[6], (H,), jnp.float32, -6.0, 0.5), -6.0, 0.5)
    dt_bias = jnp.clip(jax.random.uniform(splits[7], (H,), jnp.float32, -4.0, 0.0), -4.0, 0.0)
    w_query = normal_values(splits[8], (D, H * HEAD), D ** -0.5, 0.1875, ((0, 8), (1, 4)))
    w_key = normal_values(splits[9], (D, H * NH * HEAD), D ** -0.5, 0.1875, ((0, 8), (1, 4)))
    w_value = normal_values(splits[10], (D, H * NH * HEAD), D ** -0.5, 0.1875, ((0, 8), (1, 4)))
    w_rates = normal_values(splits[11], (D, H * (NH + 1)), D ** -0.5, 0.1875, ((0, 8), (1, 4)))
    w_outgate = normal_values(splits[12], (D, H * HEAD), D ** -0.5, 0.1875, ((0, 8), (1, 4)))
    w_out = normal_values(splits[13], (H * HEAD, D), (H * HEAD // 4) ** -0.5, 0.375, ((0, 4), (1, 8)))
    w_gate = normal_values(splits[14], (D, FF), D ** -0.5, 0.1875, ((0, 8), (1, 4)))
    w_up = normal_values(splits[15], (D, FF), D ** -0.5, 0.1875, ((0, 8), (1, 4)))
    w_down = normal_values(splits[16], (FF, D), (FF // 4) ** -0.5, 0.21875, ((0, 4), (1, 8)))
    return dict(tokens=tokens, lengths=lengths, out_grad=out_grad, ln1_gain=ln1_gain, ln2_gain=ln2_gain, onorm_gain=onorm_gain, a_log=a_log, dt_bias=dt_bias, w_query=w_query, w_key=w_key, w_value=w_value, w_rates=w_rates, w_outgate=w_outgate, w_out=w_out, w_gate=w_gate, w_up=w_up, w_down=w_down)


@jax.custom_vjp
def low(v):
    return lax.optimization_barrier(v.astype(jnp.bfloat16)).astype(jnp.float32)

@jax.custom_vjp
def low_back(v):
    return v

def low_keep(v):
    return (low(v), None)

def low_pass(kept, grad):
    return (grad,)

def back_keep(v):
    return (v, None)

def back_low(kept, grad):
    return (low(grad),)
low.defvjp(low_keep, low_pass)
low_back.defvjp(back_keep, back_low)
HIGH = lax.Precision.HIGHEST
EPS = 1e-06

def matmul(left, right):
    return jnp.einsum('...i,ij->...j', left, right, precision=HIGH)

def rms_scale(values, gain):
    return values * lax.rsqrt(lax.optimization_barrier(jnp.mean(values * values, axis=-1, keepdims=True)) + EPS) * gain

def unit_rows(values):
    return values * lax.rsqrt(lax.optimization_barrier(jnp.sum(values * values, axis=-1, keepdims=True)) + EPS)

def token_recurrence(query, keys, values, betas, decays):
    groups, length, heads, width = query.shape
    vwidth = values.shape[-1]
    nblock = length // CT

    def blockwise(array):
        return jnp.moveaxis(array.reshape((groups, nblock, CT) + array.shape[2:]), 1, 0)
    blocks = tuple((blockwise(array) for array in (query, keys, values, betas, decays)))

    def one_block(carried, block_in):

        def one_token(inner, token):
            tok_query, tok_keys, tok_values, tok_betas, tok_decay = token
            inner = inner * jnp.exp(tok_decay)[:, :, None, None]
            for step in range(NH):
                predicted = jnp.einsum('ghkv,ghk->ghv', inner, tok_keys[:, :, step], precision=HIGH)
                inner = inner + tok_betas[:, :, step, None, None] * tok_keys[:, :, step, :, None] * (tok_values[:, :, step] - predicted)[:, :, None, :]
            return (inner, jnp.einsum('ghkv,ghk->ghv', inner, tok_query, precision=HIGH))
        carried, outputs = lax.scan(one_token, carried, tuple((jnp.moveaxis(array, 1, 0) for array in block_in)))
        return (carried, jnp.moveaxis(outputs, 0, 1))
    initial = jnp.zeros((groups, heads, width, vwidth), jnp.float32)
    last_state, outputs = lax.scan(jax.checkpoint(one_block), initial, blocks)
    return jnp.moveaxis(outputs, 0, 1).reshape(groups, length, heads, vwidth)

def mixer(query_pre, key_pre, value_pre, rates_pre, outgate_pre, a_log, dt_bias, onorm_gain):
    lead_dims = query_pre.shape[:-1]
    heads = a_log.shape[0]
    query = unit_rows(jax.nn.silu(query_pre).reshape(lead_dims + (heads, HEAD)))
    keys = unit_rows(jax.nn.silu(key_pre).reshape(lead_dims + (heads, NH, HEAD)))
    values = jax.nn.silu(value_pre).reshape(lead_dims + (heads, NH, HEAD))
    rates = rates_pre.reshape(lead_dims + (heads, NH + 1))
    betas = jax.nn.sigmoid(rates[..., :NH])
    decays = -jnp.exp(a_log) * jax.nn.softplus(rates[..., NH] + dt_bias)
    mixed = token_recurrence(query, keys, values, betas, decays)
    gate = jax.nn.silu(outgate_pre.reshape(lead_dims + (heads, HEAD)))
    normed = rms_scale(mixed, onorm_gain) * gate
    return normed.reshape(lead_dims + (heads * HEAD,))

def forward(xin, mask, params):
    ln1, ln2, onorm, a_log, dt_bias, w_query, w_key, w_value, w_rates, w_outgate, w_out, w_gate, w_up, w_down = params
    first = low(rms_scale(xin, ln1))
    query_pre = low_back(matmul(first, w_query))
    key_pre = low_back(matmul(first, w_key))
    value_pre = low_back(matmul(first, w_value))
    rates_pre = low_back(matmul(first, w_rates))
    outgate_pre = low_back(matmul(first, w_outgate))
    mixed = low(mixer(query_pre, key_pre, value_pre, rates_pre, outgate_pre, a_log, dt_bias, onorm))
    middle = xin + low_back(matmul(mixed, w_out))
    second = low(rms_scale(middle, ln2))
    gate_pre = low_back(matmul(second, w_gate))
    up_pre = low_back(matmul(second, w_up))
    hidden = low(jax.nn.silu(gate_pre) * up_pre)
    result = middle + low_back(matmul(hidden, w_down))
    return result * mask

def reference(tokens, lengths, out_grad, ln1_gain, ln2_gain, onorm_gain, a_log, dt_bias, w_query, w_key, w_value, w_rates, w_outgate, w_out, w_gate, w_up, w_down):
    params = tuple((item.astype(jnp.float32) for item in (ln1_gain, ln2_gain, onorm_gain, a_log, dt_bias, w_query, w_key, w_value, w_rates, w_outgate, w_out, w_gate, w_up, w_down)))
    group = 2 if SEQS % 2 == 0 else 1
    count = SEQS // group
    inputs = tokens.astype(jnp.float32).reshape(count, group, LEN, D)
    cotangents = out_grad.astype(jnp.float32).reshape(count, group, LEN, D)
    group_lengths = lengths.reshape(count, group)

    def per_group(totals, item):
        xin, grad_in, lens_in = item
        mask = (jnp.arange(LEN)[None, :] < lens_in[:, None]).astype(jnp.float32)[:, :, None]
        outputs, pull = jax.vjp(lambda first_arg, second_arg: forward(first_arg, mask, second_arg), xin, params)
        input_grad, param_grads = pull(grad_in)
        return (jax.tree.map(lambda left, right: left + right, totals, param_grads), (outputs, input_grad))
    zeros = tuple((jnp.zeros_like(item) for item in params))
    totals, (outputs, input_grads) = lax.scan(per_group, zeros, (inputs, cotangents, group_lengths))
    return (outputs.reshape(TOKENS, D).astype(jnp.bfloat16), input_grads.reshape(TOKENS, D).astype(jnp.bfloat16), totals[0], totals[1], totals[2], totals[3], totals[4], totals[5], totals[6], totals[7], totals[8], totals[9], totals[10], totals[11], totals[12], totals[13])
```

```python
import functools
import jax
import jax.numpy as jnp
import numpy as np
from jax import lax
from jax.experimental import pallas as pl
from jax.experimental.pallas import tpu as pltpu
from jax.sharding import Mesh
from jax.sharding import PartitionSpec as P

HEAD = 128
NH = 2
CT = 64
ROWS = CT * NH
EPS = 1e-06
HIGH = lax.Precision.HIGHEST
BF = jnp.bfloat16
F32 = jnp.float32


def dot_nn(left, right):
    return jnp.dot(left, right, preferred_element_type=F32)


def dot_nt(left, right):
    return lax.dot_general(left, right, (((1,), (1,)), ((), ())), preferred_element_type=F32)


def dot_tn(left, right):
    return lax.dot_general(left, right, (((0,), (0,)), ((), ())), preferred_element_type=F32)


def mixer_tables():
    row = np.arange(ROWS)
    tok, step = row % CT, row // CT
    order = tok * NH + step
    later = order[:, None] > order[None, :]
    barred = np.where(later, 0.0, -1e30).astype(np.float32)
    levels = []
    for size in (1, 4, 16):
        near = (tok[:, None] // (4 * size)) == (tok[None, :] // (4 * size))
        apart = (tok[:, None] // size) != (tok[None, :] // size)
        levels.append((near & apart).astype(np.float32))
    own = ((tok[:, None] == tok[None, :]) & later).astype(np.float32)
    eye = np.eye(ROWS, dtype=np.float32)
    read = np.zeros((CT, ROWS), np.float32)
    read[np.arange(CT), CT + np.arange(CT)] = 1.0
    sums = (np.arange(CT)[:, None] <= tok[None, :]).astype(np.float32)
    square = np.stack([barred, eye, own] + levels)
    thin = np.stack([read, sums])
    return square, thin


def sigm(values):
    return jax.nn.sigmoid(values)


class Layout:
    def __init__(self, heads):
        self.q = 0
        self.k = heads * HEAD
        self.v = self.k + heads * NH * HEAD
        self.g = self.v + heads * NH * HEAD
        self.r = self.g + heads * HEAD
        self.width = self.r + 128


def piece(ref, s, c, start):
    return ref[s, c * CT : (c + 1) * CT, start : start + HEAD]


def unit_silu(raw):
    sig = sigm(raw)
    act = raw * sig
    norm = lax.rsqrt(jnp.sum(act * act, axis=-1, keepdims=True) + EPS)
    return act * norm, norm, sig


def rates_of(pre_ref, par_ref, thin_ref, s, c, lay):
    raw = pre_ref[s, c * CT : (c + 1) * CT, lay.r : lay.r + 128]
    shifted = raw + par_ref[s, 1:2, :]
    soft = jnp.maximum(shifted, 0.0) + jnp.log1p(jnp.exp(-jnp.abs(shifted)))
    decay = par_ref[s, 0:1, :] * soft
    sums = thin_ref[1]
    cum_col = lax.dot_general(
        sums, decay, (((0,), (0,)), ((), ())), preferred_element_type=F32, precision=HIGH
    )
    cum_row = lax.dot_general(
        decay, sums, (((0,), (0,)), ((), ())), preferred_element_type=F32, precision=HIGH
    )
    return raw, shifted, decay, cum_col, cum_row


def chunk_parts(pre_ref, s, h, c, lay, raw, cum_col, cum_row, square_ref, thin_ref):
    query, nq, sq = unit_silu(piece(pre_ref, s, c, lay.q + h * HEAD))
    key0, nk0, sk0 = unit_silu(piece(pre_ref, s, c, lay.k + (2 * h) * HEAD))
    key1, nk1, sk1 = unit_silu(piece(pre_ref, s, c, lay.k + (2 * h + 1) * HEAD))
    keys = jnp.concatenate([key0, key1], axis=0)
    beta = jnp.concatenate([sigm(raw[:, 3 * h : 3 * h + 1]), sigm(raw[:, 3 * h + 1 : 3 * h + 2])], axis=0)
    scaled = keys * beta
    at = 3 * h + 2
    gcol = cum_col[:, at : at + 1]
    grow = cum_row[at : at + 1, :]
    weights = jnp.exp(gcol - grow + square_ref[0])
    tail = gcol[CT - 1 : CT, :]
    grown = jnp.exp(gcol)
    left = jnp.exp(tail - gcol)
    return dict(
        query=query, keys=keys, beta=beta, scaled=scaled, weights=weights, grown=grown, left=left,
        tail=jnp.exp(tail), nq=nq, sq=sq, nk=(nk0, nk1), sk=(sk0, sk1),
    )


def forward_kernel(lay, nsq, heads, nb, _, pre_ref, par_ref, gain_ref, square_ref, thin_ref,
                   mixed_ref, tinv_ref, state_ref, delta_ref, o_ref, carry):
    @pl.when(pl.program_id(0) == 0)
    def _():
        carry[...] = jnp.zeros_like(carry)

    which = [(c, s, h) for c in range(nb) for s in range(nsq) for h in range(heads)]
    rates = {}
    for c in range(nb):
        for s in range(nsq):
            rates[c, s] = rates_of(pre_ref, par_ref, thin_ref, s, c, lay)
    parts = {}
    for c, s, h in which:
        raw, _, _, cum_col, cum_row = rates[c, s]
        parts[c, s, h] = chunk_parts(pre_ref, s, h, c, lay, raw, cum_col, cum_row, square_ref, thin_ref)
    lam, scores = {}, {}
    for key in which:
        p = parts[key]
        keys_low, scaled_low, query_low = p["keys"].astype(BF), p["scaled"].astype(BF), p["query"].astype(BF)
        both = dot_nt(jnp.concatenate([keys_low, query_low], axis=0), scaled_low)
        lam[key] = both[:ROWS] * p["weights"]
        scores[key] = (both[ROWS:] * (p["weights"][CT:] + thin_ref[0])).astype(BF)
    tinv = {key: square_ref[1] - lam[key] * square_ref[2] for key in which}
    for level in range(3):
        low = {key: tinv[key].astype(BF) for key in which}
        step = {key: dot_nn(low[key], (lam[key] * square_ref[3 + level]).astype(BF)).astype(BF) for key in which}
        twice = {key: dot_nn(step[key], step[key]).astype(BF) for key in which}
        half = {key: tinv[key] - dot_nn(step[key], low[key]) for key in which}
        tinv = {key: half[key] + dot_nn(twice[key], half[key].astype(BF)) for key in which}
    for c in range(nb):
        for s in range(nsq):
            for h in range(heads):
                p = parts[c, s, h]
                at = s * heads + h
                state = carry[at]
                state_low = state.astype(BF)
                t_low = tinv[c, s, h].astype(BF)
                tinv_ref[c, at] = t_low
                state_ref[c, at] = state_low
                kg = (p["keys"] * p["grown"]).astype(BF)
                qg = (p["query"] * p["grown"][:CT]).astype(BF)
                both = dot_nn(jnp.concatenate([kg, qg], axis=0), state_low)
                raw0 = piece(pre_ref, s, c, lay.v + (2 * h) * HEAD)
                raw1 = piece(pre_ref, s, c, lay.v + (2 * h + 1) * HEAD)
                values = jnp.concatenate([raw0 * sigm(raw0), raw1 * sigm(raw1)], axis=0)
                delta = dot_nn(t_low, (values - both[:ROWS]).astype(BF)).astype(BF)
                delta_ref[c, at] = delta
                kout = (p["scaled"] * p["left"]).astype(BF)
                carry[at] = p["tail"] * state + dot_tn(kout, delta)
                out = both[ROWS:] + dot_nn(scores[c, s, h], delta)
                o_ref[s, c * CT : (c + 1) * CT, h * HEAD : (h + 1) * HEAD] = out
                scale = lax.rsqrt(jnp.mean(out * out, axis=-1, keepdims=True) + EPS)
                gate = piece(pre_ref, s, c, lay.g + h * HEAD)
                mixed = out * scale * gain_ref[0:1, :] * (gate * sigm(gate))
                mixed_ref[s, c * CT : (c + 1) * CT, h * HEAD : (h + 1) * HEAD] = mixed.astype(BF)


def silu_slope(raw, sig):
    return sig * (1.0 + raw * (1.0 - sig))


def backward_kernel(lay, nsq, heads, nb, _, pre_ref, par_ref, gain_ref, square_ref, thin_ref,
                    tinv_ref, state_ref, delta_ref, o_ref, dm_ref,
                    dpre_ref, small_ref, carry, acc):
    @pl.when(pl.program_id(0) == 0)
    def _():
        carry[...] = jnp.zeros_like(carry)
        acc[...] = jnp.zeros_like(acc)

    lane = lax.broadcasted_iota(jnp.int32, (CT, 128), 1)
    sub8 = lax.broadcasted_iota(jnp.int32, (8, 128), 0)
    lane_rows = lax.broadcasted_iota(jnp.int32, (ROWS, 128), 1)
    rates = {}
    for c in range(nb):
        for s in range(nsq):
            rates[c, s] = rates_of(pre_ref, par_ref, thin_ref, s, c, lay)
    for c in reversed(range(nb)):
        span = slice(c * CT, (c + 1) * CT)
        for s in range(nsq):
            raw, shifted, decay, cum_col, cum_row = rates[c, s]
            dg_all = jnp.zeros((ROWS, 128), F32)
            dq_all = jnp.zeros((CT, 128), F32)
            dtail_all = jnp.zeros((1, 128), F32)
            dbeta_all = jnp.zeros((CT, 128), F32)
            dcol_all = jnp.zeros((8, 128), F32)
            for h in range(heads):
                at = s * heads + h
                cols = slice(h * HEAD, (h + 1) * HEAD)
                p = chunk_parts(pre_ref, s, h, c, lay, raw, cum_col, cum_row, square_ref, thin_ref)
                out = o_ref[s, span, cols]
                dm = dm_ref[s, span, cols].astype(F32)
                graw = piece(pre_ref, s, c, lay.g + h * HEAD)
                gsig = sigm(graw)
                gate = graw * gsig
                scale = lax.rsqrt(jnp.mean(out * out, axis=-1, keepdims=True) + EPS)
                normed = out * scale
                gain = gain_ref[0:1, :]
                dgate = dm * normed * gain
                dpre_ref[s, span, lay.g + h * HEAD : lay.g + (h + 1) * HEAD] = (
                    dgate * silu_slope(graw, gsig)
                ).astype(BF)
                dn = dm * gate
                acc[0:1, :] += jnp.sum(dn * normed, axis=0, keepdims=True)
                scaled_dn = dn * gain
                dout = scale * (scaled_dn - normed * jnp.mean(scaled_dn * normed, axis=-1, keepdims=True))
                dout_low = dout.astype(BF)
                keys_low, scaled_low, query_low = p["keys"].astype(BF), p["scaled"].astype(BF), p["query"].astype(BF)
                read_w = p["weights"][CT:] + thin_ref[0]
                both_low = jnp.concatenate([keys_low, query_low], axis=0)
                w_all = jnp.concatenate([p["weights"], read_w], axis=0)
                weighted = dot_nt(both_low, scaled_low) * w_all
                scores = weighted[ROWS:].astype(BF)
                dstate = carry[at]
                dstate_low = dstate.astype(BF)
                kout = (p["scaled"] * p["left"]).astype(BF)
                ddelta = dot_tn(scores, dout_low) + dot_nn(kout, dstate_low)
                dpv = dot_tn(tinv_ref[c, at], ddelta.astype(BF))
                kg = (p["keys"] * p["grown"]).astype(BF)
                qg = (p["query"] * p["grown"][:CT]).astype(BF)
                joint = jnp.concatenate([(-dpv).astype(BF), dout_low], axis=0)
                carry[at] = p["tail"] * dstate + dot_tn(jnp.concatenate([kg, qg], axis=0), joint)
                delta = delta_ref[c, at]
                state_low = state_ref[c, at]
                inner = dot_nt(joint, delta)
                inner_low = (inner * w_all).astype(BF)
                pairs = inner * weighted
                grown_all = jnp.concatenate([p["grown"], p["grown"][:CT]], axis=0)
                entered = grown_all * dot_nt(joint, state_low)
                left_out = p["left"] * dot_nt(delta, dstate_low)
                direct = dot_nn(inner_low, scaled_low) + entered
                dscaled = dot_tn(inner_low, both_low) + left_out
                both_rows = jnp.concatenate([p["keys"], p["query"]], axis=0)
                row_part = jnp.sum(pairs + both_rows * entered, axis=-1, keepdims=True)
                col_part = jnp.sum(pairs, axis=0, keepdims=True)
                out_part = jnp.sum(p["scaled"] * left_out, axis=-1, keepdims=True)
                dtail = p["tail"] * jnp.sum(
                    jnp.sum(state_low.astype(F32) * dstate, axis=0, keepdims=True), axis=1, keepdims=True
                ) + jnp.sum(out_part, axis=0, keepdims=True)
                dkeys, dquery = direct[:ROWS], direct[ROWS:]
                dbeta = jnp.sum(p["keys"] * dscaled, axis=-1, keepdims=True)
                kdot = jnp.sum(p["keys"] * dkeys, axis=-1, keepdims=True)
                qdot = jnp.sum(p["query"] * dquery, axis=-1, keepdims=True)
                dg = row_part[:ROWS] - out_part
                kfull = kdot + p["beta"] * dbeta
                here = 3 * h + 2
                dg_all = jnp.where(lane_rows == here, dg, dg_all)
                dq_all = jnp.where(lane == here, row_part[ROWS:], dq_all)
                dcol_all = jnp.where(sub8 == here, col_part, dcol_all)
                dtail_all = jnp.where(lane[0:1] == here, dtail, dtail_all)
                dbp = dbeta * p["beta"] * (1.0 - p["beta"])
                dbeta_all = jnp.where(lane == 3 * h, dbp[:CT], dbeta_all)
                dbeta_all = jnp.where(lane == 3 * h + 1, dbp[CT:], dbeta_all)
                dk = dkeys + p["beta"] * dscaled
                dk = dk - p["keys"] * kfull
                for j in range(NH):
                    part = slice(j * CT, (j + 1) * CT)
                    start = lay.k + (2 * h + j) * HEAD
                    kraw = piece(pre_ref, s, c, start)
                    dpre_ref[s, span, start : start + HEAD] = (
                        dk[part] * p["nk"][j] * silu_slope(kraw, p["sk"][j])
                    ).astype(BF)
                    start = lay.v + (2 * h + j) * HEAD
                    vraw = piece(pre_ref, s, c, start)
                    dpre_ref[s, span, start : start + HEAD] = (
                        dpv[part] * silu_slope(vraw, sigm(vraw))
                    ).astype(BF)
                start = lay.q + h * HEAD
                qraw = piece(pre_ref, s, c, start)
                dq = (dquery - p["query"] * qdot) * p["nq"]
                dpre_ref[s, span, start : start + HEAD] = (dq * silu_slope(qraw, p["sq"])).astype(BF)
            sums = thin_ref[1]
            read_sum = dg_all[:CT] + dg_all[CT:] + dq_all
            col_rows = jnp.concatenate([dcol_all, jnp.zeros((120, 128), F32)], axis=0)
            ddecay = (
                jnp.dot(sums[:, :CT], read_sum, preferred_element_type=F32, precision=HIGH)
                - lax.dot_general(
                    sums, col_rows, (((1,), (1,)), ((), ())), preferred_element_type=F32, precision=HIGH
                )
                + dtail_all
            )
            dshift = ddecay * par_ref[s, 0:1, :] * sigm(shifted)
            acc[1 + s : 2 + s, :] += jnp.sum(dshift, axis=0, keepdims=True)
            acc[1 + nsq + s : 2 + nsq + s, :] += jnp.sum(ddecay * decay, axis=0, keepdims=True)
            dpre_ref[s, span, lay.r : lay.r + 128] = (dshift + dbeta_all).astype(BF)
    small_ref[...] = acc[...]


def shared_specs(square, thin, nsq):
    return [
        pl.BlockSpec((nsq, 2, 128), lambda i, _: (0, 0, 0)),
        pl.BlockSpec((1, HEAD), lambda i, _: (0, 0)),
        pl.BlockSpec(square.shape, lambda i, _: (0, 0, 0)),
        pl.BlockSpec(thin.shape, lambda i, _: (0, 0, 0)),
    ]


def part_chunk(step, place, per_part):
    return ((step // per_part) ^ place[0]) * per_part + step % per_part


def mixer_forward(place, parts, pre, params, gain, heads, nb=2):
    nsq, length, width = pre.shape
    lay = Layout(heads)
    square, thin = mixer_tables()
    nchunk = length // CT
    chains = nsq * heads
    span = nb * CT
    per_part = nchunk // nb // parts
    big = lambda: pl.BlockSpec((nb, chains, ROWS, HEAD), lambda i, _: (i, 0, 0, 0))
    rows = lambda w: pl.BlockSpec((nsq, span, w), lambda i, place: (0, part_chunk(i, place, per_part), 0))
    return pl.pallas_call(
        functools.partial(forward_kernel, lay, nsq, heads, nb),
        grid_spec=pltpu.PrefetchScalarGridSpec(
            num_scalar_prefetch=1,
            grid=(nchunk // nb,),
            in_specs=[rows(width)] + shared_specs(square, thin, nsq),
            out_specs=[rows(heads * HEAD), big(), big(), big(), rows(heads * HEAD)],
            scratch_shapes=[pltpu.VMEM((chains, HEAD, HEAD), F32)],
        ),
        out_shape=[
            jax.ShapeDtypeStruct((nsq, length, heads * HEAD), BF),
            jax.ShapeDtypeStruct((nchunk, chains, ROWS, ROWS), BF),
            jax.ShapeDtypeStruct((nchunk, chains, HEAD, HEAD), BF),
            jax.ShapeDtypeStruct((nchunk, chains, ROWS, HEAD), BF),
            jax.ShapeDtypeStruct((nsq, length, heads * HEAD), F32),
        ],
        compiler_params=pltpu.CompilerParams(vmem_limit_bytes=56 * 1024 * 1024),
        cost_estimate=pl.CostEstimate(
            flops=nchunk * chains * 20 * 2 * ROWS**3,
            bytes_accessed=nsq * length * (4 * width + 6 * heads * HEAD) + nchunk * chains * 6 * ROWS**2,
            transcendentals=0,
        ),
        name="mixer_forward",
    )(place, pre, params, gain, jnp.asarray(square), jnp.asarray(thin))


def mixer_backward(place, parts, pre, params, gain, tinv, states, deltas, outs, dmixed, heads, nb=2):
    nsq, length, width = pre.shape
    lay = Layout(heads)
    square, thin = mixer_tables()
    nchunk = length // CT
    chains = nsq * heads
    span = nb * CT
    per_part = nchunk // nb // parts
    last = nchunk // nb - 1
    big = lambda: pl.BlockSpec((nb, chains, ROWS, HEAD), lambda i, _: (last - i, 0, 0, 0))
    rows = lambda w: pl.BlockSpec(
        (nsq, span, w), lambda i, place: (0, part_chunk(last - i, place, per_part), 0)
    )
    return pl.pallas_call(
        functools.partial(backward_kernel, lay, nsq, heads, nb),
        grid_spec=pltpu.PrefetchScalarGridSpec(
            num_scalar_prefetch=1,
            grid=(nchunk // nb,),
            in_specs=[rows(width)]
            + shared_specs(square, thin, nsq)
            + [big(), big(), big(), rows(heads * HEAD), rows(heads * HEAD)],
            out_specs=[rows(width), pl.BlockSpec((8, 128), lambda i, _: (0, 0))],
            scratch_shapes=[
                pltpu.VMEM((chains, HEAD, HEAD), F32),
                pltpu.VMEM((8, 128), F32),
            ],
        ),
        out_shape=[
            jax.ShapeDtypeStruct((nsq, length, width), BF),
            jax.ShapeDtypeStruct((8, 128), F32),
        ],
        compiler_params=pltpu.CompilerParams(vmem_limit_bytes=56 * 1024 * 1024),
        cost_estimate=pl.CostEstimate(
            flops=nchunk * chains * 26 * 2 * ROWS**3,
            bytes_accessed=nsq * length * (6 * width + 6 * heads * HEAD) + nchunk * chains * 6 * ROWS**2,
            transcendentals=0,
        ),
        name="mixer_backward",
    )(place, pre, params, gain, jnp.asarray(square), jnp.asarray(thin), tinv, states, deltas, outs, dmixed)


def rms_parts(values):
    scale = lax.rsqrt(jnp.mean(values * values, axis=-1, keepdims=True) + EPS)
    return values * scale, scale


def rms_back(grad_out, values, scale, gain):
    gain_grad = jnp.sum(grad_out * values * scale, axis=0)
    scaled = grad_out * gain
    value_grad = scale * scaled - values * scale * scale * scale * jnp.mean(
        scaled * values, axis=-1, keepdims=True
    )
    return value_grad, gain_grad


def swap(values, which, parts):
    return lax.ppermute(values, "sub", [(i, i ^ which) for i in range(parts)])


def pick(options, wanted, keys):
    chosen = options[0]
    for option, key in zip(options[1:], keys[1:]):
        chosen = jnp.where(wanted == key, option, chosen)
    return chosen


def per_device(
    tokens, lengths, out_grad, ln1_gain, ln2_gain, onorm_gain, a_log, dt_bias,
    w_query, w_key, w_value, w_rates, w_outgate, w_out, w_gate, w_up, w_down,
):
    nsq, parts = lax.axis_size("sq"), lax.axis_size("sub")
    which_seq, place = lax.axis_index("sq"), lax.axis_index("sub")
    count = nsq * parts
    tok_dev, model = tokens.shape
    heads = a_log.shape[0] // count
    lay = Layout(heads)
    units = w_gate.shape[1]
    hw = heads * HEAD
    place_arr = place.astype(jnp.int32).reshape(1)

    rates_pad = jnp.zeros((w_rates.shape[0], 128 - w_rates.shape[1]), BF)
    mix_shard = jnp.concatenate([w_query, w_key, w_value, w_outgate, w_rates, rates_pad], axis=1)
    w_mix = lax.all_gather(mix_shard, ("sq", "dp"), axis=0, tiled=True).reshape(nsq, model, lay.width)

    def everywhere(shard):
        full = lax.all_gather(shard, ("sq", "sub", "dp"), axis=0, tiled=True)
        return full.reshape(count, model, shard.shape[1])

    resid_in = tokens.astype(F32)
    normed_one, scale_one = rms_parts(resid_in)
    first = (normed_one * ln1_gain).astype(BF)
    first_seq = jnp.concatenate([first] + [swap(first, r, parts) for r in range(1, parts)], axis=0)

    pre = jnp.stack([dot_nn(first_seq, w_mix[s]) for s in range(nsq)])
    hpos = [(s * parts + place) * heads for s in range(nsq)]
    lanes = 3 * np.arange(heads) + 2

    def spread(values, s):
        mine = lax.dynamic_slice_in_dim(values, hpos[s], heads)
        return jnp.zeros((128,), F32).at[lanes].set(mine)

    params = jnp.stack([jnp.stack([spread(-jnp.exp(a_log), s), spread(dt_bias, s)]) for s in range(nsq)])
    gain = onorm_gain.reshape(1, HEAD)
    mixed, tinv, states, deltas, outs = mixer_forward(place_arr, parts, pre, params, gain, heads)

    w_out_t = everywhere(w_out.T)
    w_gate_f = everywhere(w_gate)
    w_up_f = everywhere(w_up)
    w_down_t = everywhere(w_down.T)

    got = []
    for r in range(parts):
        mine = mixed[:, r * tok_dev : (r + 1) * tok_dev]
        got.append(mine if r == 0 else swap(mine, r, parts))
    keys = [place ^ r for r in range(parts)]
    mixed_of = {}
    for s in range(nsq):
        for j in range(parts):
            mixed_of[s * parts + j] = pick([g[s] for g in got], j, keys)
    attn = dot_nt(mixed_of[0], w_out_t[0])
    for p in range(1, count):
        attn = attn + dot_nt(mixed_of[p], w_out_t[p])

    position = place * tok_dev + jnp.arange(tok_dev)
    limit = jnp.sum(jnp.where(jnp.arange(nsq) == which_seq, lengths, 0))
    mask = (position < limit).astype(F32)[:, None]
    middle = resid_in + attn
    normed_two, scale_two = rms_parts(middle)
    second = (normed_two * ln2_gain).astype(BF)
    grad_low = (out_grad.astype(F32) * mask).astype(BF)
    grad_top = grad_low.astype(F32)
    mlp = None
    second_grad = None
    gate_grads, up_grads, down_grads = [], [], []
    for p in range(count):
        gate_pre = dot_nn(second, w_gate_f[p])
        up_pre = dot_nn(second, w_up_f[p])
        gate_sig = sigm(gate_pre)
        gate_act = gate_pre * gate_sig
        hidden = (gate_act * up_pre).astype(BF)
        part = dot_nt(hidden, w_down_t[p])
        mlp = part if mlp is None else mlp + part
        hidden_grad = dot_nn(grad_low, w_down_t[p])
        down_grads.append(dot_tn(grad_low, hidden))
        up_low = (hidden_grad * gate_act).astype(BF)
        gate_low = (hidden_grad * up_pre * silu_slope(gate_pre, gate_sig)).astype(BF)
        gate_grads.append(dot_tn(second, gate_low))
        up_grads.append(dot_tn(second, up_low))
        part = dot_nt(gate_low, w_gate_f[p]) + dot_nt(up_low, w_up_f[p])
        second_grad = part if second_grad is None else second_grad + part
    block_out = ((middle + mlp) * mask).astype(BF)

    def owned(grads):
        full = jnp.concatenate([g.astype(BF) for g in grads], axis=0)
        return lax.psum_scatter(full, ("sq", "sub", "dp"), scatter_dimension=0, tiled=True).astype(F32)

    gate_own, up_own, down_own = owned(gate_grads), owned(up_grads), owned(down_grads).T

    middle_back, ln2_grad = rms_back(second_grad, middle, scale_two, ln2_gain)
    middle_grad = grad_top + middle_back
    middle_low = middle_grad.astype(BF)
    out_own = owned([dot_tn(middle_low, mixed_of[p]) for p in range(count)]).T
    mixed_grad = [dot_nn(middle_low, w_out_t[p]).astype(BF) for p in range(count)]
    back = []
    for r in range(parts):
        piece_r = jnp.stack(
            [pick([mixed_grad[s * parts + j] for j in range(parts)], place ^ r, list(range(parts))) for s in range(nsq)]
        )
        back.append(piece_r if r == 0 else swap(piece_r, r, parts))
    dmixed = jnp.concatenate(back, axis=1)
    dpre, small = mixer_backward(
        place_arr, parts, pre, params, gain, tinv, states, deltas, outs, dmixed, heads
    )

    mix_grads = jnp.concatenate([dot_tn(first_seq, dpre[s]).astype(BF) for s in range(nsq)], axis=0)
    mix_own = lax.psum_scatter(mix_grads, ("sq", "dp"), scatter_dimension=0, tiled=True).astype(F32)
    first_all = dot_nt(dpre[0], w_mix[0])
    for s in range(1, nsq):
        first_all = first_all + dot_nt(dpre[s], w_mix[s])
    first_low = first_all.astype(BF)
    first_grad = first_all[:tok_dev]
    for r in range(1, parts):
        first_grad = first_grad + swap(first_low[r * tok_dev : (r + 1) * tok_dev], r, parts).astype(F32)
    input_back, ln1_grad = rms_back(first_grad, resid_in, scale_one, ln1_gain)
    tokens_grad = (middle_grad + input_back).astype(BF)

    def gather_heads(rows):
        full = jnp.zeros(a_log.shape, F32)
        for s in range(nsq):
            full = lax.dynamic_update_slice_in_dim(full, rows[s, lanes], hpos[s], 0)
        return full

    a_grad = gather_heads(small[1 + nsq : 1 + 2 * nsq])
    dt_grad = gather_heads(small[1 : 1 + nsq])
    total = lax.psum((ln1_grad, ln2_grad, small[0], a_grad, dt_grad), ("dp", "sq", "sub"))
    return (
        block_out, tokens_grad, total[0], total[1], total[2], total[3], total[4],
        mix_own[:, lay.q : lay.k], mix_own[:, lay.k : lay.v], mix_own[:, lay.v : lay.g],
        mix_own[:, lay.r : lay.r + w_rates.shape[1]], mix_own[:, lay.g : lay.r],
        out_own, gate_own, up_own, down_own,
    )


def solution(mesh):
    dp, tensor = mesh.shape["dp"], mesh.shape["tensor"]

    def run(*args):
        nsq = args[1].shape[0] // dp
        split = Mesh(mesh.devices.reshape(dp, nsq, tensor // nsq), ("dp", "sq", "sub"))
        rows = P(("dp", "sq", "sub"), None)
        down = P("dp", ("sq", "sub"))
        across = P(("sq", "sub"), "dp")
        in_specs = (rows, P("dp"), rows) + (P(),) * 5 + (down,) * 5 + (across, down, down, across)
        out_specs = (rows, rows) + (P(),) * 5 + (down,) * 5 + (across, down, down, across)
        return jax.shard_map(
            per_device, mesh=split, in_specs=in_specs, out_specs=out_specs, check_vma=False
        )(*args)

    return run
```

```python
import functools
import jax
import jax.numpy as jnp
import numpy as np
from jax import lax
from jax.experimental import pallas as pl
from jax.experimental.pallas import tpu as pltpu
from jax.sharding import Mesh
from jax.sharding import PartitionSpec as P

HEAD = 128
NH = 2
CT = 64
ROWS = CT * NH
EPS = 1e-06
HIGH = lax.Precision.HIGHEST
BF = jnp.bfloat16
F32 = jnp.float32


def dot_nn(left, right):
    return jnp.dot(left, right, preferred_element_type=F32)


def dot_nt(left, right):
    return lax.dot_general(left, right, (((1,), (1,)), ((), ())), preferred_element_type=F32)


def dot_tn(left, right):
    return lax.dot_general(left, right, (((0,), (0,)), ((), ())), preferred_element_type=F32)


def mixer_tables():
    row = np.arange(ROWS)
    tok, step = row % CT, row // CT
    order = tok * NH + step
    later = order[:, None] > order[None, :]
    barred = np.where(later, 0.0, -1e30).astype(np.float32)
    levels = []
    for size in (1, 4, 16):
        near = (tok[:, None] // (4 * size)) == (tok[None, :] // (4 * size))
        apart = (tok[:, None] // size) != (tok[None, :] // size)
        levels.append((near & apart).astype(np.float32))
    own = ((tok[:, None] == tok[None, :]) & later).astype(np.float32)
    eye = np.eye(ROWS, dtype=np.float32)
    read = np.zeros((CT, ROWS), np.float32)
    read[np.arange(CT), CT + np.arange(CT)] = 1.0
    sums = (np.arange(CT)[:, None] <= tok[None, :]).astype(np.float32)
    square = np.stack([barred, eye, own] + levels)
    thin = np.stack([read, sums])
    return square, thin


def sigm(values):
    return jax.nn.sigmoid(values)


class Layout:
    def __init__(self, heads):
        self.q = 0
        self.k = heads * HEAD
        self.v = self.k + heads * NH * HEAD
        self.g = self.v + heads * NH * HEAD
        self.r = self.g + heads * HEAD
        self.width = self.r + 128


def piece(refs, s, c, start):
    return refs[s][c * CT : (c + 1) * CT, start : start + HEAD]


def unit_silu(raw):
    sig = sigm(raw)
    act = raw * sig
    norm = lax.rsqrt(jnp.sum(act * act, axis=-1, keepdims=True) + EPS)
    return act * norm, norm, sig


def rates_of(pre_ref, par_ref, thin_ref, s, c, lay):
    raw = pre_ref[s][c * CT : (c + 1) * CT, lay.r : lay.r + 128]
    shifted = raw + par_ref[s, 1:2, :]
    soft = jnp.maximum(shifted, 0.0) + jnp.log1p(jnp.exp(-jnp.abs(shifted)))
    decay = par_ref[s, 0:1, :] * soft
    sums = thin_ref[1]
    cum_col = lax.dot_general(
        sums, decay, (((0,), (0,)), ((), ())), preferred_element_type=F32, precision=HIGH
    )
    cum_row = lax.dot_general(
        decay, sums, (((0,), (0,)), ((), ())), preferred_element_type=F32, precision=HIGH
    )
    return raw, shifted, decay, cum_col, cum_row


def chunk_parts(pre_ref, s, h, c, lay, raw, cum_col, cum_row, square_ref, thin_ref):
    query, nq, sq = unit_silu(piece(pre_ref, s, c, lay.q + h * HEAD))
    key0, nk0, sk0 = unit_silu(piece(pre_ref, s, c, lay.k + (2 * h) * HEAD))
    key1, nk1, sk1 = unit_silu(piece(pre_ref, s, c, lay.k + (2 * h + 1) * HEAD))
    keys = jnp.concatenate([key0, key1], axis=0)
    beta = jnp.concatenate([sigm(raw[:, 3 * h : 3 * h + 1]), sigm(raw[:, 3 * h + 1 : 3 * h + 2])], axis=0)
    scaled = keys * beta
    at = 3 * h + 2
    gcol = cum_col[:, at : at + 1]
    grow = cum_row[at : at + 1, :]
    weights = jnp.exp(gcol - grow + square_ref[0])
    tail = gcol[CT - 1 : CT, :]
    grown = jnp.exp(gcol)
    left = jnp.exp(tail - gcol)
    return dict(
        query=query, keys=keys, beta=beta, scaled=scaled, weights=weights, grown=grown, left=left,
        tail=jnp.exp(tail), nq=nq, sq=sq, nk=(nk0, nk1), sk=(sk0, sk1),
    )


def forward_kernel(lay, nsq, heads, nb, _, *refs):
    pre_ref = refs[:nsq]
    par_ref, gain_ref, square_ref, thin_ref = refs[nsq : nsq + 4]
    mixed_ref, tinv_ref, state_ref, delta_ref, o_ref, carry = refs[nsq + 4 :]

    @pl.when(pl.program_id(0) == 0)
    def _():
        carry[...] = jnp.zeros_like(carry)

    which = [(c, s, h) for c in range(nb) for s in range(nsq) for h in range(heads)]
    rates = {}
    for c in range(nb):
        for s in range(nsq):
            rates[c, s] = rates_of(pre_ref, par_ref, thin_ref, s, c, lay)
    parts = {}
    for c, s, h in which:
        raw, _, _, cum_col, cum_row = rates[c, s]
        parts[c, s, h] = chunk_parts(pre_ref, s, h, c, lay, raw, cum_col, cum_row, square_ref, thin_ref)
    lam, scores = {}, {}
    for key in which:
        p = parts[key]
        keys_low, scaled_low, query_low = p["keys"].astype(BF), p["scaled"].astype(BF), p["query"].astype(BF)
        both = dot_nt(jnp.concatenate([keys_low, query_low], axis=0), scaled_low)
        lam[key] = both[:ROWS] * p["weights"]
        scores[key] = (both[ROWS:] * (p["weights"][CT:] + thin_ref[0])).astype(BF)
    tinv = {key: square_ref[1] - lam[key] * square_ref[2] for key in which}
    for level in range(3):
        low = {key: tinv[key].astype(BF) for key in which}
        step = {key: dot_nn(low[key], (lam[key] * square_ref[3 + level]).astype(BF)).astype(BF) for key in which}
        twice = {key: dot_nn(step[key], step[key]).astype(BF) for key in which}
        half = {key: tinv[key] - dot_nn(step[key], low[key]) for key in which}
        tinv = {key: half[key] + dot_nn(twice[key], half[key].astype(BF)) for key in which}
    for c in range(nb):
        for s in range(nsq):
            for h in range(heads):
                p = parts[c, s, h]
                at = s * heads + h
                state = carry[at]
                state_low = state.astype(BF)
                t_low = tinv[c, s, h].astype(BF)
                tinv_ref[c, at] = t_low
                state_ref[c, at] = state_low
                kg = (p["keys"] * p["grown"]).astype(BF)
                qg = (p["query"] * p["grown"][:CT]).astype(BF)
                both = dot_nn(jnp.concatenate([kg, qg], axis=0), state_low)
                raw0 = piece(pre_ref, s, c, lay.v + (2 * h) * HEAD)
                raw1 = piece(pre_ref, s, c, lay.v + (2 * h + 1) * HEAD)
                values = jnp.concatenate([raw0 * sigm(raw0), raw1 * sigm(raw1)], axis=0)
                delta = dot_nn(t_low, (values - both[:ROWS]).astype(BF)).astype(BF)
                delta_ref[c, at] = delta
                kout = (p["scaled"] * p["left"]).astype(BF)
                carry[at] = p["tail"] * state + dot_tn(kout, delta)
                out = both[ROWS:] + dot_nn(scores[c, s, h], delta)
                o_ref[s, c * CT : (c + 1) * CT, h * HEAD : (h + 1) * HEAD] = out
                scale = lax.rsqrt(jnp.mean(out * out, axis=-1, keepdims=True) + EPS)
                gate = piece(pre_ref, s, c, lay.g + h * HEAD)
                mixed = out * scale * gain_ref[0:1, :] * (gate * sigm(gate))
                mixed_ref[s, c * CT : (c + 1) * CT, h * HEAD : (h + 1) * HEAD] = mixed.astype(BF)


def silu_slope(raw, sig):
    return sig * (1.0 + raw * (1.0 - sig))


def backward_kernel(lay, nsq, heads, nb, _, *refs):
    pre_ref = refs[:nsq]
    par_ref, gain_ref, square_ref, thin_ref = refs[nsq : nsq + 4]
    tinv_ref, state_ref, delta_ref, o_ref, dm_ref = refs[nsq + 4 : nsq + 9]
    dpre_ref = refs[nsq + 9 : 2 * nsq + 9]
    small_ref, carry, acc = refs[2 * nsq + 9 :]

    @pl.when(pl.program_id(0) == 0)
    def _():
        carry[...] = jnp.zeros_like(carry)
        acc[...] = jnp.zeros_like(acc)

    lane = lax.broadcasted_iota(jnp.int32, (CT, 128), 1)
    sub8 = lax.broadcasted_iota(jnp.int32, (8, 128), 0)
    lane_rows = lax.broadcasted_iota(jnp.int32, (ROWS, 128), 1)
    rates = {}
    for c in range(nb):
        for s in range(nsq):
            rates[c, s] = rates_of(pre_ref, par_ref, thin_ref, s, c, lay)
    for c in reversed(range(nb)):
        span = slice(c * CT, (c + 1) * CT)
        for s in range(nsq):
            raw, shifted, decay, cum_col, cum_row = rates[c, s]
            dg_all = jnp.zeros((ROWS, 128), F32)
            dq_all = jnp.zeros((CT, 128), F32)
            dtail_all = jnp.zeros((1, 128), F32)
            dbeta_all = jnp.zeros((CT, 128), F32)
            dcol_all = jnp.zeros((8, 128), F32)
            for h in range(heads):
                at = s * heads + h
                cols = slice(h * HEAD, (h + 1) * HEAD)
                p = chunk_parts(pre_ref, s, h, c, lay, raw, cum_col, cum_row, square_ref, thin_ref)
                out = o_ref[s, span, cols]
                dm = dm_ref[s, span, cols].astype(F32)
                graw = piece(pre_ref, s, c, lay.g + h * HEAD)
                gsig = sigm(graw)
                gate = graw * gsig
                scale = lax.rsqrt(jnp.mean(out * out, axis=-1, keepdims=True) + EPS)
                normed = out * scale
                gain = gain_ref[0:1, :]
                dgate = dm * normed * gain
                dpre_ref[s][span, lay.g + h * HEAD : lay.g + (h + 1) * HEAD] = (
                    dgate * silu_slope(graw, gsig)
                ).astype(BF)
                dn = dm * gate
                acc[0:1, :] += jnp.sum(dn * normed, axis=0, keepdims=True)
                scaled_dn = dn * gain
                dout = scale * (scaled_dn - normed * jnp.mean(scaled_dn * normed, axis=-1, keepdims=True))
                dout_low = dout.astype(BF)
                keys_low, scaled_low, query_low = p["keys"].astype(BF), p["scaled"].astype(BF), p["query"].astype(BF)
                read_w = p["weights"][CT:] + thin_ref[0]
                both_low = jnp.concatenate([keys_low, query_low], axis=0)
                w_all = jnp.concatenate([p["weights"], read_w], axis=0)
                weighted = dot_nt(both_low, scaled_low) * w_all
                scores = weighted[ROWS:].astype(BF)
                dstate = carry[at]
                dstate_low = dstate.astype(BF)
                kout = (p["scaled"] * p["left"]).astype(BF)
                ddelta = dot_tn(scores, dout_low) + dot_nn(kout, dstate_low)
                dpv = dot_tn(tinv_ref[c, at], ddelta.astype(BF))
                kg = (p["keys"] * p["grown"]).astype(BF)
                qg = (p["query"] * p["grown"][:CT]).astype(BF)
                joint = jnp.concatenate([(-dpv).astype(BF), dout_low], axis=0)
                carry[at] = p["tail"] * dstate + dot_tn(jnp.concatenate([kg, qg], axis=0), joint)
                delta = delta_ref[c, at]
                state_low = state_ref[c, at]
                inner = dot_nt(joint, delta)
                inner_low = (inner * w_all).astype(BF)
                pairs = inner * weighted
                grown_all = jnp.concatenate([p["grown"], p["grown"][:CT]], axis=0)
                entered = grown_all * dot_nt(joint, state_low)
                left_out = p["left"] * dot_nt(delta, dstate_low)
                direct = dot_nn(inner_low, scaled_low) + entered
                dscaled = dot_tn(inner_low, both_low) + left_out
                both_rows = jnp.concatenate([p["keys"], p["query"]], axis=0)
                row_part = jnp.sum(pairs + both_rows * entered, axis=-1, keepdims=True)
                col_part = jnp.sum(pairs, axis=0, keepdims=True)
                out_part = jnp.sum(p["scaled"] * left_out, axis=-1, keepdims=True)
                dtail = p["tail"] * jnp.sum(
                    jnp.sum(state_low.astype(F32) * dstate, axis=0, keepdims=True), axis=1, keepdims=True
                ) + jnp.sum(out_part, axis=0, keepdims=True)
                dkeys, dquery = direct[:ROWS], direct[ROWS:]
                dbeta = jnp.sum(p["keys"] * dscaled, axis=-1, keepdims=True)
                kdot = jnp.sum(p["keys"] * dkeys, axis=-1, keepdims=True)
                qdot = jnp.sum(p["query"] * dquery, axis=-1, keepdims=True)
                dg = row_part[:ROWS] - out_part
                kfull = kdot + p["beta"] * dbeta
                here = 3 * h + 2
                dg_all = jnp.where(lane_rows == here, dg, dg_all)
                dq_all = jnp.where(lane == here, row_part[ROWS:], dq_all)
                dcol_all = jnp.where(sub8 == here, col_part, dcol_all)
                dtail_all = jnp.where(lane[0:1] == here, dtail, dtail_all)
                dbp = dbeta * p["beta"] * (1.0 - p["beta"])
                dbeta_all = jnp.where(lane == 3 * h, dbp[:CT], dbeta_all)
                dbeta_all = jnp.where(lane == 3 * h + 1, dbp[CT:], dbeta_all)
                dk = dkeys + p["beta"] * dscaled
                dk = dk - p["keys"] * kfull
                for j in range(NH):
                    part = slice(j * CT, (j + 1) * CT)
                    start = lay.k + (2 * h + j) * HEAD
                    kraw = piece(pre_ref, s, c, start)
                    dpre_ref[s][span, start : start + HEAD] = (
                        dk[part] * p["nk"][j] * silu_slope(kraw, p["sk"][j])
                    ).astype(BF)
                    start = lay.v + (2 * h + j) * HEAD
                    vraw = piece(pre_ref, s, c, start)
                    dpre_ref[s][span, start : start + HEAD] = (
                        dpv[part] * silu_slope(vraw, sigm(vraw))
                    ).astype(BF)
                start = lay.q + h * HEAD
                qraw = piece(pre_ref, s, c, start)
                dq = (dquery - p["query"] * qdot) * p["nq"]
                dpre_ref[s][span, start : start + HEAD] = (dq * silu_slope(qraw, p["sq"])).astype(BF)
            sums = thin_ref[1]
            read_sum = dg_all[:CT] + dg_all[CT:] + dq_all
            col_rows = jnp.concatenate([dcol_all, jnp.zeros((120, 128), F32)], axis=0)
            ddecay = (
                jnp.dot(sums[:, :CT], read_sum, preferred_element_type=F32, precision=HIGH)
                - lax.dot_general(
                    sums, col_rows, (((1,), (1,)), ((), ())), preferred_element_type=F32, precision=HIGH
                )
                + dtail_all
            )
            dshift = ddecay * par_ref[s, 0:1, :] * sigm(shifted)
            acc[1 + s : 2 + s, :] += jnp.sum(dshift, axis=0, keepdims=True)
            acc[1 + nsq + s : 2 + nsq + s, :] += jnp.sum(ddecay * decay, axis=0, keepdims=True)
            dpre_ref[s][span, lay.r : lay.r + 128] = (dshift + dbeta_all).astype(BF)
    small_ref[...] = acc[...]


def shared_specs(square, thin, nsq):
    return [
        pl.BlockSpec((nsq, 2, 128), lambda i, _: (0, 0, 0)),
        pl.BlockSpec((1, HEAD), lambda i, _: (0, 0)),
        pl.BlockSpec(square.shape, lambda i, _: (0, 0, 0)),
        pl.BlockSpec(thin.shape, lambda i, _: (0, 0, 0)),
    ]


def part_chunk(step, place, per_part):
    return ((step // per_part) ^ place[0]) * per_part + step % per_part


def mixer_forward(place, parts, pre, params, gain, heads, nb=2):
    nsq, (length, width) = len(pre), pre[0].shape
    lay = Layout(heads)
    square, thin = mixer_tables()
    nchunk = length // CT
    chains = nsq * heads
    span = nb * CT
    per_part = nchunk // nb // parts
    big = lambda: pl.BlockSpec((nb, chains, ROWS, HEAD), lambda i, _: (i, 0, 0, 0))
    rows = lambda w: pl.BlockSpec((nsq, span, w), lambda i, place: (0, part_chunk(i, place, per_part), 0))
    wide = lambda: pl.BlockSpec((span, width), lambda i, place: (part_chunk(i, place, per_part), 0))
    return pl.pallas_call(
        functools.partial(forward_kernel, lay, nsq, heads, nb),
        grid_spec=pltpu.PrefetchScalarGridSpec(
            num_scalar_prefetch=1,
            grid=(nchunk // nb,),
            in_specs=[wide() for _ in pre] + shared_specs(square, thin, nsq),
            out_specs=[rows(heads * HEAD), big(), big(), big(), rows(heads * HEAD)],
            scratch_shapes=[pltpu.VMEM((chains, HEAD, HEAD), F32)],
        ),
        out_shape=[
            jax.ShapeDtypeStruct((nsq, length, heads * HEAD), BF),
            jax.ShapeDtypeStruct((nchunk, chains, ROWS, ROWS), BF),
            jax.ShapeDtypeStruct((nchunk, chains, HEAD, HEAD), BF),
            jax.ShapeDtypeStruct((nchunk, chains, ROWS, HEAD), BF),
            jax.ShapeDtypeStruct((nsq, length, heads * HEAD), F32),
        ],
        compiler_params=pltpu.CompilerParams(vmem_limit_bytes=56 * 1024 * 1024),
        cost_estimate=pl.CostEstimate(
            flops=nchunk * chains * 20 * 2 * ROWS**3,
            bytes_accessed=nsq * length * (4 * width + 6 * heads * HEAD) + nchunk * chains * 6 * ROWS**2,
            transcendentals=0,
        ),
        name="mixer_forward",
    )(place, *pre, params, gain, jnp.asarray(square), jnp.asarray(thin))


def mixer_backward(place, parts, pre, params, gain, tinv, states, deltas, outs, dmixed, heads, nb=2):
    nsq, (length, width) = len(pre), pre[0].shape
    lay = Layout(heads)
    square, thin = mixer_tables()
    nchunk = length // CT
    chains = nsq * heads
    span = nb * CT
    per_part = nchunk // nb // parts
    last = nchunk // nb - 1
    big = lambda: pl.BlockSpec((nb, chains, ROWS, HEAD), lambda i, _: (last - i, 0, 0, 0))
    rows = lambda w: pl.BlockSpec(
        (nsq, span, w), lambda i, place: (0, part_chunk(last - i, place, per_part), 0)
    )
    wide = lambda: pl.BlockSpec((span, width), lambda i, place: (part_chunk(last - i, place, per_part), 0))
    return pl.pallas_call(
        functools.partial(backward_kernel, lay, nsq, heads, nb),
        grid_spec=pltpu.PrefetchScalarGridSpec(
            num_scalar_prefetch=1,
            grid=(nchunk // nb,),
            in_specs=[wide() for _ in pre]
            + shared_specs(square, thin, nsq)
            + [big(), big(), big(), rows(heads * HEAD), rows(heads * HEAD)],
            out_specs=[wide() for _ in pre] + [pl.BlockSpec((8, 128), lambda i, _: (0, 0))],
            scratch_shapes=[
                pltpu.VMEM((chains, HEAD, HEAD), F32),
                pltpu.VMEM((8, 128), F32),
            ],
        ),
        out_shape=[jax.ShapeDtypeStruct((length, width), BF) for _ in pre]
        + [
            jax.ShapeDtypeStruct((8, 128), F32),
        ],
        compiler_params=pltpu.CompilerParams(vmem_limit_bytes=56 * 1024 * 1024),
        cost_estimate=pl.CostEstimate(
            flops=nchunk * chains * 26 * 2 * ROWS**3,
            bytes_accessed=nsq * length * (6 * width + 6 * heads * HEAD) + nchunk * chains * 6 * ROWS**2,
            transcendentals=0,
        ),
        name="mixer_backward",
    )(place, *pre, params, gain, jnp.asarray(square), jnp.asarray(thin), tinv, states, deltas, outs, dmixed)


TILE = 256


def token_mask(place, limit, tile, rows, base):
    position = place * rows + base + lax.broadcasted_iota(jnp.int32, (tile, 1), 0)
    return position < limit


def join_kernel(parts, nsq, tok, scalars, *refs):
    mixed_refs = refs[:parts]
    x_ref, og_ref, wout_ref, gain_ref = refs[parts : parts + 4]
    middle_ref, second_ref, grad_ref = refs[parts + 4 :]
    place, limit = scalars[0], scalars[1]
    total = x_ref[...].astype(F32)
    for r in range(parts):
        for s in range(nsq):
            total = total + dot_nt(mixed_refs[r][s], wout_ref[s * parts + (place ^ r)])
    middle_ref[...] = total
    scale = lax.rsqrt(jnp.mean(total * total, axis=-1, keepdims=True) + EPS)
    second_ref[...] = (total * scale * gain_ref[...]).astype(BF)
    keep = token_mask(place, limit, x_ref.shape[0], tok, pl.program_id(0) * x_ref.shape[0])
    grad_ref[...] = jnp.where(keep, og_ref[...].astype(F32), 0.0).astype(BF)


def join(scalars, mixed_parts, x, out_grad, wall, gain, parts, nsq, hw):
    tok, model = x.shape
    count = parts * nsq
    tile = min(TILE, tok)
    row = pl.BlockSpec((tile, model), lambda i, _: (i, 0))
    return pl.pallas_call(
        functools.partial(join_kernel, parts, nsq, tok),
        grid_spec=pltpu.PrefetchScalarGridSpec(
            num_scalar_prefetch=1,
            grid=(tok // tile,),
            in_specs=[pl.BlockSpec((nsq, tile, hw), lambda i, _: (0, i, 0)) for _ in mixed_parts]
            + [row, row, pl.BlockSpec((count, model, hw), lambda i, _: (0, 0, 0)),
               pl.BlockSpec((1, model), lambda i, _: (0, 0))],
            out_specs=[row, row, row],
        ),
        out_shape=[
            jax.ShapeDtypeStruct((tok, model), F32),
            jax.ShapeDtypeStruct((tok, model), BF),
            jax.ShapeDtypeStruct((tok, model), BF),
        ],
        compiler_params=pltpu.CompilerParams(vmem_limit_bytes=40 * 1024 * 1024),
        cost_estimate=pl.CostEstimate(
            flops=2 * tok * model * count * hw, bytes_accessed=14 * tok * model, transcendentals=0
        ),
        name="join",
    )(scalars, *mixed_parts, x, out_grad, wall, gain)


def ff_kernel(tile, hw, units, sec_ref, grad_ref, w_ref, mlp_ref, sg_ref, dw_ref, hid, both):
    tok, model = sec_ref.shape
    mid, end = hw + 2 * units, hw + 3 * units

    @pl.when(pl.program_id(0) == 0)
    def _():
        mlp_ref[...] = jnp.zeros_like(mlp_ref)
        sg_ref[...] = jnp.zeros_like(sg_ref)

    for m in range(tok // tile):
        rows = slice(m * tile, (m + 1) * tile)
        pre = dot_nn(sec_ref[rows, :], w_ref[0, :, hw:mid])
        gate_pre, up_pre = pre[:, :units], pre[:, units:]
        hidden_grad = dot_nn(grad_ref[rows, :], w_ref[0, :, mid:end])
        sig = sigm(gate_pre)
        act = gate_pre * sig
        hidden = (act * up_pre).astype(BF)
        hid[rows, :] = hidden
        gate_low = (hidden_grad * up_pre * (sig + act * (1.0 - sig))).astype(BF)
        up_low = (hidden_grad * act).astype(BF)
        both_low = jnp.concatenate([gate_low, up_low], axis=1)
        both[rows, :] = both_low
        mlp_ref[rows, :] += dot_nt(hidden, w_ref[0, :, mid:end])
        sg_ref[rows, :] += dot_nt(both_low, w_ref[0, :, hw:mid])
    step = min(256, model)
    for k in range(model // step):
        cols = slice(k * step, (k + 1) * step)
        dw_ref[0, cols, hw:mid] = dot_tn(sec_ref[:, cols], both[...]).astype(BF)
        dw_ref[0, cols, mid:end] = dot_tn(grad_ref[:, cols], hid[...]).astype(BF)


def feed_forward(second, grad_low, wall, hw, units):
    tok, model = second.shape
    count, _, width = wall.shape
    whole = pl.BlockSpec((tok, model), lambda p: (0, 0))
    weight = pl.BlockSpec((1, model, width), lambda p: (p, 0, 0))
    return pl.pallas_call(
        functools.partial(ff_kernel, min(TILE, tok), hw, units),
        grid=(count,),
        in_specs=[whole, whole, weight],
        out_specs=[whole, whole, weight],
        out_shape=[
            jax.ShapeDtypeStruct((tok, model), F32),
            jax.ShapeDtypeStruct((tok, model), F32),
            jax.ShapeDtypeStruct((count, model, width), BF),
        ],
        scratch_shapes=[pltpu.VMEM((tok, units), BF), pltpu.VMEM((tok, 2 * units), BF)],
        compiler_params=pltpu.CompilerParams(vmem_limit_bytes=62 * 1024 * 1024),
        cost_estimate=pl.CostEstimate(
            flops=18 * tok * model * units * count,
            bytes_accessed=count * model * width * 4 + 12 * tok * model,
            transcendentals=0,
        ),
        name="feed_forward",
    )(second, grad_low, wall)


def split_kernel(parts, nsq, tok, scalars, *refs):
    middle_ref, mlp_ref, sg_ref, grad_ref, wout_ref, gain_ref = refs[:6]
    out_ref, mg_ref, ml_ref, ln_ref = refs[6:10]
    back_refs = refs[10:]
    place, limit = scalars[0], scalars[1]
    tile = middle_ref.shape[0]
    middle = middle_ref[...]
    keep = token_mask(place, limit, tile, tok, pl.program_id(0) * tile)
    out_ref[...] = jnp.where(keep, middle + mlp_ref[...], 0.0).astype(BF)
    scale = lax.rsqrt(jnp.mean(middle * middle, axis=-1, keepdims=True) + EPS)
    normed = middle * scale
    sg = sg_ref[...]

    @pl.when(pl.program_id(0) == 0)
    def _():
        ln_ref[...] = jnp.zeros_like(ln_ref)

    ln_ref[...] += jnp.sum(sg * normed, axis=0, keepdims=True)
    scaled = sg * gain_ref[...]
    back = scale * (scaled - normed * jnp.mean(scaled * normed, axis=-1, keepdims=True))
    total = grad_ref[...].astype(F32) + back
    mg_ref[...] = total
    low = total.astype(BF)
    ml_ref[...] = low
    for r in range(parts):
        for s in range(nsq):
            back_refs[r][s] = dot_nn(low, wout_ref[s * parts + (place ^ r)]).astype(BF)


def split(scalars, middle, mlp, second_grad, grad_low, wall, gain, parts, nsq, hw):
    tok, model = middle.shape
    count = parts * nsq
    tile = min(TILE, tok)
    row = pl.BlockSpec((tile, model), lambda i, _: (i, 0))
    line = pl.BlockSpec((1, model), lambda i, _: (0, 0))
    return pl.pallas_call(
        functools.partial(split_kernel, parts, nsq, tok),
        grid_spec=pltpu.PrefetchScalarGridSpec(
            num_scalar_prefetch=1,
            grid=(tok // tile,),
            in_specs=[row, row, row, row, pl.BlockSpec((count, model, hw), lambda i, _: (0, 0, 0)), line],
            out_specs=[row, row, row, line]
            + [pl.BlockSpec((nsq, tile, hw), lambda i, _: (0, i, 0)) for _ in range(parts)],
        ),
        out_shape=[
            jax.ShapeDtypeStruct((tok, model), BF),
            jax.ShapeDtypeStruct((tok, model), F32),
            jax.ShapeDtypeStruct((tok, model), BF),
            jax.ShapeDtypeStruct((1, model), F32),
        ]
        + [jax.ShapeDtypeStruct((nsq, tok, hw), BF) for _ in range(parts)],
        compiler_params=pltpu.CompilerParams(vmem_limit_bytes=40 * 1024 * 1024),
        cost_estimate=pl.CostEstimate(
            flops=2 * tok * model * count * hw, bytes_accessed=26 * tok * model, transcendentals=0
        ),
        name="split",
    )(scalars, middle, mlp, second_grad, grad_low, wall, gain)


def out_grad_kernel(scalars, ml_ref, mixed_ref, full_ref, dw_ref):
    model = ml_ref.shape[1]
    step = min(256, model)
    for k in range(model // step):
        cols = slice(k * step, (k + 1) * step)
        dw_ref[0, cols, :] = dot_tn(ml_ref[:, cols], mixed_ref[0]).astype(BF)


def out_proj_grad(scalars, middle_low, mixed_part, full, r, parts, nsq, hw):
    tok, model = middle_low.shape
    return pl.pallas_call(
        out_grad_kernel,
        grid_spec=pltpu.PrefetchScalarGridSpec(
            num_scalar_prefetch=1,
            grid=(nsq,),
            in_specs=[
                pl.BlockSpec((tok, model), lambda s, _: (0, 0)),
                pl.BlockSpec((1, tok, hw), lambda s, _: (s, 0, 0)),
                pl.BlockSpec(memory_space=pl.ANY),
            ],
            out_specs=pl.BlockSpec((1, model, hw), lambda s, sc: (s * parts + (sc[0] ^ r), 0, 0)),
        ),
        out_shape=jax.ShapeDtypeStruct(full.shape, BF),
        input_output_aliases={3: 0},
        compiler_params=pltpu.CompilerParams(vmem_limit_bytes=40 * 1024 * 1024),
        cost_estimate=pl.CostEstimate(
            flops=2 * tok * model * nsq * hw, bytes_accessed=2 * tok * model * 2, transcendentals=0
        ),
        name="out_proj_grad",
    )(scalars, middle_low, mixed_part, full)


def pack_kernel(lay, q_ref, k_ref, v_ref, r_ref, g_ref, out_ref, gate_ref, up_ref, down_ref, mix_ref, all_ref):
    mix_ref[:, lay.q : lay.k] = q_ref[...]
    mix_ref[:, lay.k : lay.v] = k_ref[...]
    mix_ref[:, lay.v : lay.g] = v_ref[...]
    mix_ref[:, lay.g : lay.r] = g_ref[...]
    mix_ref[:, lay.r : lay.width] = jnp.zeros((mix_ref.shape[0], 128), BF)
    mix_ref[:, lay.r : lay.r + r_ref.shape[1]] = r_ref[...]
    hw, units = out_ref.shape[0], gate_ref.shape[1]
    all_ref[:, 0:hw] = out_ref[...].astype(F32).T.astype(BF)
    all_ref[:, hw : hw + units] = gate_ref[...]
    all_ref[:, hw + units : hw + 2 * units] = up_ref[...]
    all_ref[:, hw + 2 * units : hw + 3 * units] = down_ref[...].astype(F32).T.astype(BF)


def pack(lay, w_query, w_key, w_value, w_rates, w_outgate, w_out, w_gate, w_up, w_down):
    rows = w_query.shape[0]
    return pl.pallas_call(
        functools.partial(pack_kernel, lay),
        out_shape=[
            jax.ShapeDtypeStruct((rows, lay.width), BF),
            jax.ShapeDtypeStruct((rows, w_out.shape[0] + 3 * w_gate.shape[1]), BF),
        ],
        name="pack",
    )(w_query, w_key, w_value, w_rates, w_outgate, w_out, w_gate, w_up, w_down)
def rms_parts(values):
    scale = lax.rsqrt(jnp.mean(values * values, axis=-1, keepdims=True) + EPS)
    return values * scale, scale


def bits(axis):
    return [1 << k for k in range((lax.axis_size(axis) - 1).bit_length())]


def trade(values, axis, bit):
    return lax.ppermute(values, axis, [(i, i ^ bit) for i in range(lax.axis_size(axis))])


def everyone(values):
    for axis in ("sub", "sq", "dp"):
        for bit in bits(axis):
            values = values + trade(values, axis, bit)
    return values


def plus(left, right):
    return (left.astype(F32) + right.astype(F32)).astype(BF)


def scatter_mix(grads, which_seq):
    dp = lax.axis_size("dp")
    me = lax.axis_index("dp")
    nbits = len(bits("dp"))
    width = grads[0].shape[1]
    shaped = [g.reshape((2,) * nbits + (-1, width)) for g in grads]

    def halves(values, k):
        axis, mine = nbits - 1 - k, (me >> k) & 1
        part = lambda i: lax.dynamic_index_in_dim(values, i, axis, keepdims=True)
        return part(mine), part(1 - mine)

    kept = []
    for g in shaped:
        keep, send = halves(g, 0)
        kept.append(plus(keep, trade(send, "dp", 1)))
    if len(kept) == 2:
        keep = jnp.where(which_seq == 0, kept[0], kept[1])
        send = jnp.where(which_seq == 0, kept[1], kept[0])
        keep_near, keep_far = halves(keep, 1)
        send_near, send_far = halves(send, 1)
        far = plus(keep_far, trade(send_far, "sq", 1))
        near = plus(keep_near, trade(send_near, "sq", 1))
    else:
        near, far = halves(kept[0], 1)
    value = plus(near, trade(far, "dp", 2))
    for k in range(2, nbits):
        keep, send = halves(value, k)
        value = plus(keep, trade(send, "dp", 1 << k))
    return value.reshape(-1, width)


def swap(values, which, parts):
    return lax.ppermute(values, "sub", [(i, i ^ which) for i in range(parts)])


def pick(options, wanted, keys):
    chosen = options[0]
    for option, key in zip(options[1:], keys[1:]):
        chosen = jnp.where(wanted == key, option, chosen)
    return chosen


def per_device(
    tokens, lengths, out_grad, ln1_gain, ln2_gain, onorm_gain, a_log, dt_bias,
    w_query, w_key, w_value, w_rates, w_outgate, w_out, w_gate, w_up, w_down,
):
    nsq, parts = lax.axis_size("sq"), lax.axis_size("sub")
    which_seq, place = lax.axis_index("sq"), lax.axis_index("sub")
    count = nsq * parts
    tok_dev, model = tokens.shape
    heads = a_log.shape[0] // count
    lay = Layout(heads)
    units = w_gate.shape[1]
    hw = heads * HEAD
    place_arr = place.astype(jnp.int32).reshape(1)

    mix_shard, all_shard = pack(
        lay, w_query, w_key, w_value, w_rates, w_outgate, w_out, w_gate, w_up, w_down
    )
    w_mix = lax.all_gather(mix_shard, ("sq", "dp"), axis=0, tiled=True).reshape(nsq, model, lay.width)
    wall = lax.all_gather(all_shard, ("sq", "sub", "dp"), axis=0, tiled=True)
    wall = wall.reshape(count, model, all_shard.shape[1])

    resid_in = tokens.astype(F32)
    normed_one, scale_one = rms_parts(resid_in)
    first = (normed_one * ln1_gain).astype(BF)
    first_seq = jnp.concatenate([first] + [swap(first, r, parts) for r in range(1, parts)], axis=0)

    pre = [dot_nn(first_seq, w_mix[s]) for s in range(nsq)]
    hpos = [(s * parts + place) * heads for s in range(nsq)]
    lanes = 3 * np.arange(heads) + 2

    def spread(values, s):
        mine = lax.dynamic_slice_in_dim(values, hpos[s], heads)
        return jnp.zeros((128,), F32).at[lanes].set(mine)

    params = jnp.stack([jnp.stack([spread(-jnp.exp(a_log), s), spread(dt_bias, s)]) for s in range(nsq)])
    gain = onorm_gain.reshape(1, HEAD)
    mixed, tinv, states, deltas, outs = mixer_forward(place_arr, parts, pre, params, gain, heads)

    got = [mixed] + [swap(mixed[:, r * tok_dev : (r + 1) * tok_dev], r, parts) for r in range(1, parts)]

    limit = jnp.sum(jnp.where(jnp.arange(nsq) == which_seq, lengths, 0)).astype(jnp.int32)
    scalars = jnp.stack([place.astype(jnp.int32), limit])
    middle, second, grad_low = join(
        scalars, got, tokens, out_grad, wall, ln2_gain.reshape(1, model), parts, nsq, hw
    )
    mlp, second_grad, grads = feed_forward(second, grad_low, wall, hw, units)
    block_out, middle_grad, middle_low, ln2_grad, *back = split(
        scalars, middle, mlp, second_grad, grad_low, wall, ln2_gain.reshape(1, model), parts, nsq, hw
    )
    for r in range(parts):
        grads = out_proj_grad(scalars, middle_low, got[r], grads, r, parts, nsq, hw)
    dmixed = jnp.concatenate([back[0]] + [swap(back[r], r, parts) for r in range(1, parts)], axis=1)
    dmixed, grads = lax.optimization_barrier((dmixed, grads))
    own = lax.psum_scatter(
        grads.reshape(count * model, -1), ("sq", "sub", "dp"), scatter_dimension=0, tiled=True
    ).astype(F32)
    own_out, own_gate = own[:, :hw].T, own[:, hw : hw + units]
    own_up, own_down = own[:, hw + units : hw + 2 * units], own[:, hw + 2 * units :].T

    *dpre, small = mixer_backward(
        place_arr, parts, pre, params, gain, tinv, states, deltas, outs, dmixed, heads
    )

    mix_own = scatter_mix([dot_tn(first_seq, dpre[s]).astype(BF) for s in range(nsq)], which_seq).astype(F32)
    first_all = dot_nt(dpre[0], w_mix[0])
    for s in range(1, nsq):
        first_all = first_all + dot_nt(dpre[s], w_mix[s])
    first_low = first_all.astype(BF)
    ln1_grad = jnp.sum(first_all * first_seq.astype(F32), axis=0) / ln1_gain
    first_grad = first_all[:tok_dev]
    for r in range(1, parts):
        first_grad = first_grad + swap(first_low[r * tok_dev : (r + 1) * tok_dev], r, parts).astype(F32)
    scaled = first_grad * ln1_gain
    input_back = scale_one * (scaled - normed_one * jnp.mean(scaled * normed_one, axis=-1, keepdims=True))
    tokens_grad = (middle_grad + input_back).astype(BF)

    def gather_heads(rows):
        full = jnp.zeros(a_log.shape, F32)
        for s in range(nsq):
            full = lax.dynamic_update_slice_in_dim(full, rows[s, lanes], hpos[s], 0)
        return full

    a_grad = gather_heads(small[1 + nsq : 1 + 2 * nsq])
    dt_grad = gather_heads(small[1 : 1 + nsq])
    total = everyone(jnp.concatenate([ln1_grad, ln2_grad[0], small[0], a_grad, dt_grad]))
    marks = np.cumsum([0, model, model, HEAD, a_log.shape[0], a_log.shape[0]])
    return (
        block_out, tokens_grad, *[total[i:j] for i, j in zip(marks[:-1], marks[1:])],
        mix_own[:, lay.q : lay.k], mix_own[:, lay.k : lay.v], mix_own[:, lay.v : lay.g],
        mix_own[:, lay.r : lay.r + w_rates.shape[1]], mix_own[:, lay.g : lay.r],
        own_out, own_gate, own_up, own_down,
    )


def solution(mesh):
    dp, tensor = mesh.shape["dp"], mesh.shape["tensor"]

    def run(*args):
        nsq = args[1].shape[0] // dp
        split = Mesh(mesh.devices.reshape(dp, nsq, tensor // nsq), ("dp", "sq", "sub"))
        rows = P(("dp", "sq", "sub"), None)
        down = P("dp", ("sq", "sub"))
        across = P(("sq", "sub"), "dp")
        in_specs = (rows, P("dp"), rows) + (P(),) * 5 + (down,) * 5 + (across, down, down, across)
        out_specs = (rows, rows) + (P(),) * 5 + (down,) * 5 + (across, down, down, across)
        return jax.shard_map(
            per_device, mesh=split, in_specs=in_specs, out_specs=out_specs, check_vma=False
        )(*args)

    return run
```

```python
import functools
import jax
import jax.numpy as jnp
import numpy as np
from jax import lax
from jax.experimental import pallas as pl
from jax.experimental.pallas import tpu as pltpu
from jax.sharding import Mesh
from jax.sharding import PartitionSpec as P

HEAD = 128
NH = 2
CT = 64
ROWS = CT * NH
EPS = 1e-06
HIGH = lax.Precision.HIGHEST
BF = jnp.bfloat16
F32 = jnp.float32


def dot_nn(left, right):
    return jnp.dot(left, right, preferred_element_type=F32)


def dot_nt(left, right):
    return lax.dot_general(left, right, (((1,), (1,)), ((), ())), preferred_element_type=F32)


def dot_tn(left, right):
    return lax.dot_general(left, right, (((0,), (0,)), ((), ())), preferred_element_type=F32)


def mixer_tables():
    row = np.arange(ROWS)
    tok, step = row % CT, row // CT
    order = tok * NH + step
    later = order[:, None] > order[None, :]
    barred = np.where(later, 0.0, -1e30).astype(np.float32)
    levels = []
    for size in (1, 4, 16):
        near = (tok[:, None] // (4 * size)) == (tok[None, :] // (4 * size))
        apart = (tok[:, None] // size) != (tok[None, :] // size)
        levels.append((near & apart).astype(np.float32))
    own = ((tok[:, None] == tok[None, :]) & later).astype(np.float32)
    eye = np.eye(ROWS, dtype=np.float32)
    read = np.zeros((CT, ROWS), np.float32)
    read[np.arange(CT), CT + np.arange(CT)] = 1.0
    sums = (np.arange(CT)[:, None] <= tok[None, :]).astype(np.float32)
    square = np.stack([barred, eye, own] + levels)
    thin = np.stack([read, sums])
    return square, thin, np.concatenate([sums] * 3, axis=0)


def sigm(values):
    return jax.nn.sigmoid(values)


class Layout:
    def __init__(self, heads):
        self.q = 0
        self.k = heads * HEAD
        self.v = self.k + heads * NH * HEAD
        self.g = self.v + heads * NH * HEAD
        self.r = self.g + heads * HEAD
        self.width = self.r + 128


def piece(refs, s, c, start):
    return refs[s][c * CT : (c + 1) * CT, start : start + HEAD]


def unit_silu(raw):
    sig = sigm(raw)
    act = raw * sig
    norm = lax.rsqrt(jnp.sum(act * act, axis=-1, keepdims=True) + EPS)
    return act * norm, norm, sig


def thirds(values):
    high = values.astype(BF)
    rest = values - high.astype(F32)
    middle = rest.astype(BF)
    return high, middle, (rest - middle.astype(F32)).astype(BF)


def rates_of(pre_ref, par_ref, sums_ref, nb, nsq, lay):
    raw = None
    for c in range(nb):
        for s in range(nsq):
            here = pre_ref[s][c * CT : (c + 1) * CT, lay.r : lay.r + 128]
            if c + s > 0:
                here = pltpu.roll(here, 8 * (c * nsq + s), axis=1)
            raw = here if raw is None else raw + here
    shifted = raw + par_ref[1:2, :]
    soft = jnp.maximum(shifted, 0.0) + jnp.log1p(jnp.exp(-jnp.abs(shifted)))
    decay = par_ref[0:1, :] * soft
    stacked = jnp.concatenate(thirds(decay), axis=0)
    sums = sums_ref[...]
    return sigm(raw), shifted, decay, dot_tn(sums, stacked), dot_tn(stacked, sums)


def chunk_parts(pre_ref, s, h, c, nsq, lay, betas, cum_col, cum_row, square_ref):
    query, nq, sq = unit_silu(piece(pre_ref, s, c, lay.q + h * HEAD))
    key0, nk0, sk0 = unit_silu(piece(pre_ref, s, c, lay.k + (2 * h) * HEAD))
    key1, nk1, sk1 = unit_silu(piece(pre_ref, s, c, lay.k + (2 * h + 1) * HEAD))
    keys = jnp.concatenate([key0, key1], axis=0)
    base = 8 * (c * nsq + s) + 3 * h
    wide = lambda column: jnp.broadcast_to(column, (CT, HEAD))
    beta = jnp.concatenate([wide(betas[:, base : base + 1]), wide(betas[:, base + 1 : base + 2])], axis=0)
    scaled = keys * beta
    g = wide(cum_col[:CT, base + 2 : base + 3])
    grow = cum_row[base + 2 : base + 3, :]
    weights = jnp.exp(jnp.concatenate([g, g], axis=0) - grow + square_ref[0])
    tail = g[CT - 1 : CT, :]
    grown, left = jnp.exp(g), jnp.exp(tail - g)
    return dict(
        query=query, keys=keys, beta=beta, scaled=scaled, weights=weights, grown=jnp.concatenate([grown, grown], axis=0),
        left=jnp.concatenate([left, left], axis=0), tail=jnp.exp(tail), nq=nq, sq=sq, nk=(nk0, nk1), sk=(sk0, sk1),
    )


def forward_kernel(lay, nsq, heads, nb, _, *refs):
    pre_ref = refs[:nsq]
    par_ref, gain_ref, square_ref, thin_ref, sums_ref = refs[nsq : nsq + 5]
    mixed_ref, tinv_ref, wk_ref, state_ref, delta_ref, o_ref, carry = refs[nsq + 5 :]

    @pl.when(pl.program_id(0) == 0)
    def _():
        carry[...] = jnp.zeros_like(carry)

    which = [(c, s, h) for c in range(nb) for s in range(nsq) for h in range(heads)]
    betas, _, _, cum_col, cum_row = rates_of(pre_ref, par_ref, sums_ref, nb, nsq, lay)
    parts = {}
    for c, s, h in which:
        parts[c, s, h] = chunk_parts(pre_ref, s, h, c, nsq, lay, betas, cum_col, cum_row, square_ref)
    lam, scores = {}, {}
    for key in which:
        p = parts[key]
        keys_low, scaled_low, query_low = p["keys"].astype(BF), p["scaled"].astype(BF), p["query"].astype(BF)
        both = dot_nt(jnp.concatenate([keys_low, query_low], axis=0), scaled_low)
        lam[key] = both[:ROWS] * p["weights"]
        scores[key] = (both[ROWS:] * (p["weights"][CT:] + thin_ref[0])).astype(BF)
    tinv = {key: square_ref[1] - lam[key] * square_ref[2] for key in which}
    for level in range(3):
        low = {key: tinv[key].astype(BF) for key in which}
        step = {key: dot_nn(low[key], (lam[key] * square_ref[3 + level]).astype(BF)).astype(BF) for key in which}
        twice = {key: dot_nn(step[key], step[key]).astype(BF) for key in which}
        half = {key: tinv[key] - dot_nn(step[key], low[key]) for key in which}
        tinv = {key: half[key] + dot_nn(twice[key], half[key].astype(BF)) for key in which}
    chains = [(s, h) for s in range(nsq) for h in range(heads)]
    mixed_in = {}
    for key in which:
        c, s, h = key
        p = parts[key]
        t_low = tinv[key].astype(BF)
        tinv_ref[c, s * heads + h] = t_low
        raw0 = piece(pre_ref, s, c, lay.v + (2 * h) * HEAD)
        raw1 = piece(pre_ref, s, c, lay.v + (2 * h + 1) * HEAD)
        values = jnp.concatenate([raw0 * sigm(raw0), raw1 * sigm(raw1)], axis=0)
        kg = p["keys"] * p["grown"]
        solved = dot_nn(t_low, jnp.concatenate([values, kg], axis=1).astype(BF))
        wk = solved[:, HEAD:].astype(BF)
        wk_ref[c, s * heads + h] = wk
        qg = (p["query"] * p["grown"][:CT]).astype(BF)
        mixed_in[key] = (solved[:, :HEAD], jnp.concatenate([wk, qg], axis=0), (p["scaled"] * p["left"]).astype(BF))
    state = {k: carry[k[0] * heads + k[1]] for k in chains}
    read, deltas = {}, {}
    for c in range(nb):
        low = {k: state[k].astype(BF) for k in chains}
        for s, h in chains:
            state_ref[c, s * heads + h] = low[s, h]
        seen = {k: dot_nn(mixed_in[(c,) + k][1], low[k]) for k in chains}
        delta = {k: (mixed_in[(c,) + k][0] - seen[k][:ROWS]).astype(BF) for k in chains}
        state = {k: parts[(c,) + k]["tail"] * state[k] + dot_tn(mixed_in[(c,) + k][2], delta[k]) for k in chains}
        for k in chains:
            read[(c,) + k] = seen[k][ROWS:]
            deltas[(c,) + k] = delta[k]
    for s, h in chains:
        carry[s * heads + h] = state[s, h]
    for key in which:
        c, s, h = key
        delta_ref[c, s * heads + h] = deltas[key]
        out = read[key] + dot_nn(scores[key], deltas[key])
        o_ref[s, c * CT : (c + 1) * CT, h * HEAD : (h + 1) * HEAD] = out
        scale = lax.rsqrt(jnp.mean(out * out, axis=-1, keepdims=True) + EPS)
        gate = piece(pre_ref, s, c, lay.g + h * HEAD)
        mixed = out * scale * gain_ref[0:1, :] * (gate * sigm(gate))
        mixed_ref[s, c * CT : (c + 1) * CT, h * HEAD : (h + 1) * HEAD] = mixed.astype(BF)


def silu_slope(raw, sig):
    return sig * (1.0 + raw * (1.0 - sig))


def backward_kernel(lay, nsq, heads, nb, _, *refs):
    pre_ref = refs[:nsq]
    par_ref, gain_ref, square_ref, thin_ref, sums_ref = refs[nsq : nsq + 5]
    tinv_ref, wk_ref, state_ref, delta_ref, o_ref, dm_ref = refs[nsq + 5 : nsq + 11]
    carry_in, small_in = refs[nsq + 11 : nsq + 13]
    dpre_ref = refs[-nsq - 3 : -3]
    carry, acc, carried = refs[-3:]

    @pl.when(pl.program_id(0) == 0)
    def _():
        carried[...] = carry_in[...]
        acc[...] = small_in[...]

    lane = lax.broadcasted_iota(jnp.int32, (CT, 128), 1)
    sub8 = lax.broadcasted_iota(jnp.int32, (8, 128), 0)
    chains = [(s, h) for s in range(nsq) for h in range(heads)]
    spans = [slice(c * CT, (c + 1) * CT) for c in range(nb)]
    gain = gain_ref[0:1, :]
    gain_sum = jnp.zeros((1, HEAD), F32)
    work = {}
    betas, shifted, decay, cum_col, cum_row = rates_of(pre_ref, par_ref, sums_ref, nb, nsq, lay)
    for c in reversed(range(nb)):
        for s, h in chains:
            cols = slice(h * HEAD, (h + 1) * HEAD)
            p = chunk_parts(pre_ref, s, h, c, nsq, lay, betas, cum_col, cum_row, square_ref)
            out = o_ref[s, spans[c], cols]
            dm = dm_ref[s, spans[c], cols].astype(F32)
            graw = piece(pre_ref, s, c, lay.g + h * HEAD)
            gsig = sigm(graw)
            gate = graw * gsig
            scale = lax.rsqrt(jnp.mean(out * out, axis=-1, keepdims=True) + EPS)
            normed = out * scale
            dpre_ref[s][spans[c], lay.g + h * HEAD : lay.g + (h + 1) * HEAD] = (
                dm * normed * gain * (gsig + gate * (1.0 - gsig))
            ).astype(BF)
            dn = dm * gate
            gain_sum = gain_sum + jnp.sum(dn * normed, axis=0, keepdims=True)
            scaled_dn = dn * gain
            dout = scale * (scaled_dn - normed * jnp.mean(scaled_dn * normed, axis=-1, keepdims=True))
            dout_low = dout.astype(BF)
            keys_low, query_low = p["keys"].astype(BF), p["query"].astype(BF)
            scaled_low = p["scaled"].astype(BF)
            both_low = jnp.concatenate([keys_low, query_low], axis=0)
            w_all = jnp.concatenate([p["weights"], p["weights"][CT:] + thin_ref[0]], axis=0)
            weighted = dot_nt(both_low, scaled_low) * w_all
            p["w_all"], p["weighted"], p["both_low"], p["scaled_low"] = w_all, weighted, both_low, scaled_low
            p["dout_low"] = dout_low
            p["from_out"] = dot_tn(weighted[ROWS:].astype(BF), dout_low)
            qg = (p["query"] * p["grown"][:CT]).astype(BF)
            p["to_state"] = dot_tn(qg, dout_low)
            p["kout"] = (p["scaled"] * p["left"]).astype(BF)
            work[c, s, h] = p
    dstate = {k: carried[k[0] * heads + k[1]] for k in chains}
    for c in reversed(range(nb)):
        low = {k: dstate[k].astype(BF) for k in chains}
        ddelta = {
            k: (work[(c,) + k]["from_out"] + dot_nn(work[(c,) + k]["kout"], low[k])).astype(BF) for k in chains
        }
        for k in chains:
            p = work[(c,) + k]
            p["ddelta"], p["dstate"], p["dstate_low"] = ddelta[k], dstate[k], low[k]
        dstate = {
            k: work[(c,) + k]["tail"] * dstate[k]
            + work[(c,) + k]["to_state"]
            - dot_tn(wk_ref[c, k[0] * heads + k[1]], ddelta[k])
            for k in chains
        }
    for s, h in chains:
        carried[s * heads + h] = dstate[s, h]
        carry[s * heads + h] = dstate[s, h]
    read_all = jnp.zeros((CT, 128), F32)
    dtail_all = jnp.zeros((1, 128), F32)
    dbeta_all = jnp.zeros((CT, 128), F32)
    col_rows = {}
    for c in reversed(range(nb)):
        span = spans[c]
        for s in range(nsq):
            dcol_all = jnp.zeros((8, 128), F32)
            for h in range(heads):
                at = s * heads + h
                p = work[c, s, h]
                dpv = dot_tn(tinv_ref[c, at], p["ddelta"])
                joint = jnp.concatenate([(-dpv).astype(BF), p["dout_low"]], axis=0)
                delta = delta_ref[c, at]
                state_low = state_ref[c, at]
                inner = dot_nt(joint, delta)
                inner_low = (inner * p["w_all"]).astype(BF)
                pairs = inner * p["weighted"]
                grown_all = jnp.concatenate([p["grown"], p["grown"][:CT]], axis=0)
                base = 8 * (c * nsq + s) + 3 * h
                entered = grown_all * dot_nt(joint, state_low)
                left_out = p["left"] * dot_nt(delta, p["dstate_low"])
                direct = dot_nn(inner_low, p["scaled_low"]) + entered
                dscaled = dot_tn(inner_low, p["both_low"]) + left_out
                both_rows = jnp.concatenate([p["keys"], p["query"]], axis=0)
                row_part = jnp.sum(pairs + both_rows * entered, axis=-1, keepdims=True)
                col_part = jnp.sum(pairs, axis=0, keepdims=True)
                out_part = jnp.sum(p["scaled"] * left_out, axis=-1, keepdims=True)
                dtail = p["tail"] * jnp.sum(
                    jnp.sum(state_low.astype(F32) * p["dstate"], axis=0, keepdims=True), axis=1, keepdims=True
                ) + jnp.sum(out_part, axis=0, keepdims=True)
                dkeys, dquery = direct[:ROWS], direct[ROWS:]
                dbeta = jnp.sum(p["keys"] * dscaled, axis=-1, keepdims=True)
                kdot = jnp.sum(p["keys"] * dkeys, axis=-1, keepdims=True)
                qdot = jnp.sum(p["query"] * dquery, axis=-1, keepdims=True)
                kfull = kdot + p["beta"] * dbeta
                tokens = row_part[:CT] + row_part[CT:ROWS] + row_part[ROWS:] - out_part[:CT] - out_part[CT:]
                read_all = jnp.where(lane == base + 2, tokens, read_all)
                dcol_all = jnp.where(sub8 == 3 * h + 2, col_part, dcol_all)
                dtail_all = jnp.where(lane[0:1] == base + 2, dtail, dtail_all)
                dbeta_all = jnp.where(lane == base, dbeta[:CT], dbeta_all)
                dbeta_all = jnp.where(lane == base + 1, dbeta[CT:], dbeta_all)
                dk = dkeys + p["beta"] * dscaled
                dk = dk - p["keys"] * kfull
                for j in range(NH):
                    part = slice(j * CT, (j + 1) * CT)
                    start = lay.k + (2 * h + j) * HEAD
                    kraw = piece(pre_ref, s, c, start)
                    dpre_ref[s][span, start : start + HEAD] = (
                        dk[part] * p["nk"][j] * silu_slope(kraw, p["sk"][j])
                    ).astype(BF)
                    start = lay.v + (2 * h + j) * HEAD
                    vraw = piece(pre_ref, s, c, start)
                    dpre_ref[s][span, start : start + HEAD] = (
                        dpv[part] * silu_slope(vraw, sigm(vraw))
                    ).astype(BF)
                start = lay.q + h * HEAD
                qraw = piece(pre_ref, s, c, start)
                dq = (dquery - p["query"] * qdot) * p["nq"]
                dpre_ref[s][span, start : start + HEAD] = (dq * silu_slope(qraw, p["sq"])).astype(BF)
            col_rows[c * nsq + s] = dcol_all
    sums = sums_ref[0:CT, :]
    reads = jnp.concatenate(thirds(read_all), axis=0)
    padding = [jnp.zeros((128 - 8 * len(col_rows), 128), F32)] if len(col_rows) < 16 else []
    columns = jnp.concatenate([col_rows[k] for k in range(len(col_rows))] + padding, axis=0)
    ddecay = dot_nn(jnp.concatenate([sums[:, :CT]] * 3, axis=1), reads) + dtail_all
    for term in thirds(columns):
        ddecay = ddecay - dot_nt(sums, term)
    dshift = ddecay * par_ref[0:1, :] * sigm(shifted)
    acc[1:2, :] += jnp.sum(dshift, axis=0, keepdims=True)
    acc[2:3, :] += jnp.sum(ddecay * decay, axis=0, keepdims=True)
    drates = dshift + dbeta_all * betas * (1.0 - betas)
    for c in range(nb):
        for s in range(nsq):
            shift = 8 * (c * nsq + s)
            here = pltpu.roll(drates, 128 - shift, axis=1) if shift else drates
            dpre_ref[s][spans[c], lay.r : lay.r + 128] = jnp.where(lane < 8, here, 0.0).astype(BF)
    acc[0:1, :] += gain_sum


def shared_specs(square, thin, sums):
    return [
        pl.BlockSpec((2, 128), lambda i, _: (0, 0)),
        pl.BlockSpec((1, HEAD), lambda i, _: (0, 0)),
        pl.BlockSpec(square.shape, lambda i, _: (0, 0, 0)),
        pl.BlockSpec(thin.shape, lambda i, _: (0, 0, 0)),
        pl.BlockSpec(sums.shape, lambda i, _: (0, 0)),
    ]


def part_chunk(step, place, per_part):
    return ((step // per_part) ^ place[0]) * per_part + step % per_part


def mixer_forward(place, parts, pre, params, gain, heads, nb=2):
    nsq, (length, width) = len(pre), pre[0].shape
    lay = Layout(heads)
    square, thin, sums3 = mixer_tables()
    nchunk = length // CT
    chains = nsq * heads
    span = nb * CT
    per_part = nchunk // nb // parts
    big = lambda: pl.BlockSpec((nb, chains, ROWS, HEAD), lambda i, _: (i, 0, 0, 0))
    rows = lambda w: pl.BlockSpec((nsq, span, w), lambda i, place: (0, part_chunk(i, place, per_part), 0))
    wide = lambda: pl.BlockSpec((span, width), lambda i, place: (part_chunk(i, place, per_part), 0))
    return pl.pallas_call(
        functools.partial(forward_kernel, lay, nsq, heads, nb),
        grid_spec=pltpu.PrefetchScalarGridSpec(
            num_scalar_prefetch=1,
            grid=(nchunk // nb,),
            in_specs=[wide() for _ in pre] + shared_specs(square, thin, sums3),
            out_specs=[rows(heads * HEAD), big(), big(), big(), big(), rows(heads * HEAD)],
            scratch_shapes=[pltpu.VMEM((chains, HEAD, HEAD), F32)],
        ),
        out_shape=[
            jax.ShapeDtypeStruct((nsq, length, heads * HEAD), BF),
            jax.ShapeDtypeStruct((nchunk, chains, ROWS, ROWS), BF),
            jax.ShapeDtypeStruct((nchunk, chains, ROWS, HEAD), BF),
            jax.ShapeDtypeStruct((nchunk, chains, HEAD, HEAD), BF),
            jax.ShapeDtypeStruct((nchunk, chains, ROWS, HEAD), BF),
            jax.ShapeDtypeStruct((nsq, length, heads * HEAD), F32),
        ],
        compiler_params=pltpu.CompilerParams(vmem_limit_bytes=56 * 1024 * 1024),
        cost_estimate=pl.CostEstimate(
            flops=nchunk * chains * 20 * 2 * ROWS**3,
            bytes_accessed=nsq * length * (4 * width + 6 * heads * HEAD) + nchunk * chains * 6 * ROWS**2,
            transcendentals=0,
        ),
        name="mixer_forward",
    )(place, *pre, params, gain, jnp.asarray(square), jnp.asarray(thin), jnp.asarray(sums3, BF))


def mixer_backward(place, parts, pre, params, gain, tinv, wks, states, deltas, outs, dmixed, heads, nb, at, earlier):
    nsq, (length, width) = len(pre), pre[0].shape
    lay = Layout(heads)
    square, thin, sums3 = mixer_tables()
    nchunk = length // CT
    chains = nsq * heads
    span = nb * CT
    per_part = nchunk // nb // parts
    last = nchunk // nb - 1 - at * per_part
    big = lambda: pl.BlockSpec((nb, chains, ROWS, HEAD), lambda i, _: (last - i, 0, 0, 0))
    rows = lambda w: pl.BlockSpec(
        (nsq, span, w), lambda i, place: (0, part_chunk(last - i, place, per_part), 0)
    )
    wide = lambda: pl.BlockSpec((span, width), lambda i, place: (part_chunk(last - i, place, per_part), 0))
    held = pl.BlockSpec((chains, HEAD, HEAD), lambda i, _: (0, 0, 0))
    sums = pl.BlockSpec((8, 128), lambda i, _: (0, 0))
    carry, small, *done = earlier
    first_done = nsq + 14
    return pl.pallas_call(
        functools.partial(backward_kernel, lay, nsq, heads, nb),
        grid_spec=pltpu.PrefetchScalarGridSpec(
            num_scalar_prefetch=1,
            grid=(per_part,),
            in_specs=[wide() for _ in pre]
            + shared_specs(square, thin, sums3)
            + [big(), big(), big(), big(), rows(heads * HEAD), rows(heads * HEAD), held, sums]
            + [pl.BlockSpec(memory_space=pl.ANY) for _ in done],
            out_specs=[wide() for _ in pre] + [held, sums],
            scratch_shapes=[pltpu.VMEM((chains, HEAD, HEAD), F32)],
        ),
        out_shape=[jax.ShapeDtypeStruct((length, width), BF) for _ in pre]
        + [jax.ShapeDtypeStruct((chains, HEAD, HEAD), F32), jax.ShapeDtypeStruct((8, 128), F32)],
        input_output_aliases={first_done + k: k for k in range(len(done))},
        compiler_params=pltpu.CompilerParams(vmem_limit_bytes=56 * 1024 * 1024),
        cost_estimate=pl.CostEstimate(
            flops=nchunk // parts * chains * 26 * 2 * ROWS**3,
            bytes_accessed=(nsq * length * (6 * width + 6 * heads * HEAD) + nchunk * chains * 8 * ROWS**2) // parts,
            transcendentals=0,
        ),
        name="mixer_backward",
    )(
        place, *pre, params, gain, jnp.asarray(square), jnp.asarray(thin), jnp.asarray(sums3, BF),
        tinv, wks, states, deltas, outs, dmixed, carry, small, *done,
    )


TILE = 256


def token_mask(place, limit, tile, rows, base):
    position = place * rows + base + lax.broadcasted_iota(jnp.int32, (tile, 1), 0)
    return position < limit


def join_kernel(parts, nsq, tok, scalars, *refs):
    mixed_refs = refs[:parts]
    x_ref, og_ref, wout_ref, gain_ref = refs[parts : parts + 4]
    middle_ref, second_ref, grad_ref = refs[parts + 4 :]
    place, limit = scalars[0], scalars[1]
    total = x_ref[...].astype(F32)
    for r in range(parts):
        for s in range(nsq):
            total = total + dot_nt(mixed_refs[r][s], wout_ref[s * parts + (place ^ r)])
    middle_ref[...] = total
    scale = lax.rsqrt(jnp.mean(total * total, axis=-1, keepdims=True) + EPS)
    second_ref[...] = (total * scale * gain_ref[...]).astype(BF)
    keep = token_mask(place, limit, x_ref.shape[0], tok, pl.program_id(0) * x_ref.shape[0])
    grad_ref[...] = jnp.where(keep, og_ref[...].astype(F32), 0.0).astype(BF)


def join(scalars, mixed_parts, x, out_grad, wall, gain, parts, nsq, hw):
    tok, model = x.shape
    count = parts * nsq
    tile = min(TILE, tok)
    row = pl.BlockSpec((tile, model), lambda i, _: (i, 0))
    return pl.pallas_call(
        functools.partial(join_kernel, parts, nsq, tok),
        grid_spec=pltpu.PrefetchScalarGridSpec(
            num_scalar_prefetch=1,
            grid=(tok // tile,),
            in_specs=[pl.BlockSpec((nsq, tile, hw), lambda i, _: (0, i, 0)) for _ in mixed_parts]
            + [row, row, pl.BlockSpec((count, model, hw), lambda i, _: (0, 0, 0)),
               pl.BlockSpec((1, model), lambda i, _: (0, 0))],
            out_specs=[row, row, row],
        ),
        out_shape=[
            jax.ShapeDtypeStruct((tok, model), F32),
            jax.ShapeDtypeStruct((tok, model), BF),
            jax.ShapeDtypeStruct((tok, model), BF),
        ],
        compiler_params=pltpu.CompilerParams(vmem_limit_bytes=40 * 1024 * 1024),
        cost_estimate=pl.CostEstimate(
            flops=2 * tok * model * count * hw, bytes_accessed=14 * tok * model, transcendentals=0
        ),
        name="join",
    )(scalars, *mixed_parts, x, out_grad, wall, gain)


def core_halves(core, block, value):
    count = value.shape[0] // block
    pieces = [value[j * block : (j + 1) * block] for j in range(count)]
    join_all = lambda items: items[0] if len(items) == 1 else jnp.concatenate(items, axis=0)
    even, odd = join_all(pieces[0::2]), join_all(pieces[1::2])
    return jnp.where(core == 0, even, odd), jnp.where(core == 0, odd, even)


def ff_kernel(
    tile, block, lead, lead_out, units, scalars, sec_ref, grad_ref, w_ref, mlp_ref, sg_ref, keep_ref, send_ref, hid, both
):
    tok, model = sec_ref.shape
    mid, end = lead + 2 * units, lead + 3 * units
    mid_out, end_out = lead_out + 2 * units, lead_out + 3 * units

    @pl.when(pl.program_id(0) == 0)
    def _():
        mlp_ref[...] = jnp.zeros_like(mlp_ref)
        sg_ref[...] = jnp.zeros_like(sg_ref)

    for m in range(tok // tile):
        rows = slice(m * tile, (m + 1) * tile)
        pre = dot_nn(sec_ref[rows, :], w_ref[0, :, lead:mid])
        gate_pre, up_pre = pre[:, :units], pre[:, units:]
        hidden_grad = dot_nn(grad_ref[rows, :], w_ref[0, :, mid:end])
        sig = sigm(gate_pre)
        act = gate_pre * sig
        hidden = (act * up_pre).astype(BF)
        hid[rows, :] = hidden
        gate_low = (hidden_grad * up_pre * (sig + act * (1.0 - sig))).astype(BF)
        up_low = (hidden_grad * act).astype(BF)
        both_low = jnp.concatenate([gate_low, up_low], axis=1)
        both[rows, :] = both_low
        mlp_ref[rows, :] += dot_nt(hidden, w_ref[0, :, mid:end])
        sg_ref[rows, :] += dot_nt(both_low, w_ref[0, :, lead:mid])
    step = min(256, model)
    for k in range(model // step):
        cols = slice(k * step, (k + 1) * step)
        rows = slice(k * step // 2, (k + 1) * step // 2)
        value = core_halves(scalars[2], block, dot_tn(sec_ref[:, cols], both[...]))
        keep_ref[0, rows, lead_out:mid_out] = value[0].astype(BF)
        send_ref[0, rows, lead_out:mid_out] = value[1].astype(BF)
        value = core_halves(scalars[2], block, dot_tn(grad_ref[:, cols], hid[...]))
        keep_ref[0, rows, mid_out:end_out] = value[0].astype(BF)
        send_ref[0, rows, mid_out:end_out] = value[1].astype(BF)


def feed_forward(scalars, second, grad_low, wall, lead, lead_out, width_out, units, block):
    tok, model = second.shape
    count, _, width = wall.shape
    whole = pl.BlockSpec((tok, model), lambda p, _: (0, 0))
    weight = pl.BlockSpec((1, model, width), lambda p, _: (p, 0, 0))
    half = pl.BlockSpec((1, model // 2, width_out), lambda p, _: (p, 0, 0))
    return pl.pallas_call(
        functools.partial(ff_kernel, min(TILE, tok), block, lead, lead_out, units),
        grid_spec=pltpu.PrefetchScalarGridSpec(
            num_scalar_prefetch=1,
            grid=(count,),
            in_specs=[whole, whole, weight],
            out_specs=[whole, whole, half, half],
            scratch_shapes=[pltpu.VMEM((tok, units), BF), pltpu.VMEM((tok, 2 * units), BF)],
        ),
        out_shape=[
            jax.ShapeDtypeStruct((tok, model), F32),
            jax.ShapeDtypeStruct((tok, model), F32),
            jax.ShapeDtypeStruct((count, model // 2, width_out), BF),
            jax.ShapeDtypeStruct((count, model // 2, width_out), BF),
        ],
        compiler_params=pltpu.CompilerParams(vmem_limit_bytes=62 * 1024 * 1024),
        cost_estimate=pl.CostEstimate(
            flops=18 * tok * model * units * count,
            bytes_accessed=count * model * width * 4 + 12 * tok * model,
            transcendentals=0,
        ),
        name="feed_forward",
    )(scalars, second, grad_low, wall)


def split_kernel(parts, nsq, tok, scalars, *refs):
    middle_ref, mlp_ref, mlp2_ref, sg_ref, sg2_ref, grad_ref, wout_ref, gain_ref = refs[:8]
    out_ref, mg_ref, ml_ref, ln_ref = refs[8:12]
    back_refs = refs[12:]
    place, limit = scalars[0], scalars[1]
    tile = middle_ref.shape[0]
    middle = middle_ref[...]
    keep = token_mask(place, limit, tile, tok, pl.program_id(0) * tile)
    out_ref[...] = jnp.where(keep, middle + (mlp_ref[...] + mlp2_ref[...]), 0.0).astype(BF)
    scale = lax.rsqrt(jnp.mean(middle * middle, axis=-1, keepdims=True) + EPS)
    normed = middle * scale
    sg = sg_ref[...] + sg2_ref[...]

    @pl.when(pl.program_id(0) == 0)
    def _():
        ln_ref[...] = jnp.zeros_like(ln_ref)

    ln_ref[...] += jnp.sum(sg * normed, axis=0, keepdims=True)
    scaled = sg * gain_ref[...]
    back = scale * (scaled - normed * jnp.mean(scaled * normed, axis=-1, keepdims=True))
    total = grad_ref[...].astype(F32) + back
    mg_ref[...] = total
    low = total.astype(BF)
    ml_ref[...] = low
    for r in range(parts):
        for s in range(nsq):
            back_refs[r][s] = dot_nn(low, wout_ref[s * parts + (place ^ r)]).astype(BF)


def split(scalars, middle, mlps, second_grads, grad_low, wall, gain, parts, nsq, hw):
    tok, model = middle.shape
    count = parts * nsq
    tile = min(TILE, tok)
    row = pl.BlockSpec((tile, model), lambda i, _: (i, 0))
    line = pl.BlockSpec((1, model), lambda i, _: (0, 0))
    return pl.pallas_call(
        functools.partial(split_kernel, parts, nsq, tok),
        grid_spec=pltpu.PrefetchScalarGridSpec(
            num_scalar_prefetch=1,
            grid=(tok // tile,),
            in_specs=[row] * 6 + [pl.BlockSpec((count, model, hw), lambda i, _: (0, 0, 0)), line],
            out_specs=[row, row, row, line]
            + [pl.BlockSpec((nsq, tile, hw), lambda i, _: (0, i, 0)) for _ in range(parts)],
        ),
        out_shape=[
            jax.ShapeDtypeStruct((tok, model), BF),
            jax.ShapeDtypeStruct((tok, model), F32),
            jax.ShapeDtypeStruct((tok, model), BF),
            jax.ShapeDtypeStruct((1, model), F32),
        ]
        + [jax.ShapeDtypeStruct((nsq, tok, hw), BF) for _ in range(parts)],
        compiler_params=pltpu.CompilerParams(vmem_limit_bytes=40 * 1024 * 1024),
        cost_estimate=pl.CostEstimate(
            flops=2 * tok * model * count * hw, bytes_accessed=26 * tok * model, transcendentals=0
        ),
        name="split",
    )(scalars, middle, *mlps, *second_grads, grad_low, wall, gain)


def out_grad_kernel(block, scalars, ml_ref, mixed_ref, _, __, keep_ref, send_ref):
    model = ml_ref.shape[1]
    step = min(256, model)
    for k in range(model // step):
        rows = slice(k * step // 2, (k + 1) * step // 2)
        value = dot_tn(ml_ref[:, k * step : (k + 1) * step], mixed_ref[0])
        value = core_halves(scalars[2], block, value)
        keep_ref[0, rows, :] = value[0].astype(BF)
        send_ref[0, rows, :] = value[1].astype(BF)


def out_proj_grad(scalars, middle_low, mixed_part, halves, r, parts, nsq, hw, block):
    tok, model = middle_low.shape
    shape = halves[0].shape
    half = pl.BlockSpec((1, model // 2, hw), lambda s, sc: (s * parts + (sc[0] ^ r), 0, 0))
    return pl.pallas_call(
        functools.partial(out_grad_kernel, block),
        grid_spec=pltpu.PrefetchScalarGridSpec(
            num_scalar_prefetch=1,
            grid=(nsq,),
            in_specs=[
                pl.BlockSpec((tok, model), lambda s, _: (0, 0)),
                pl.BlockSpec((1, tok, hw), lambda s, _: (s, 0, 0)),
                pl.BlockSpec(memory_space=pl.ANY),
                pl.BlockSpec(memory_space=pl.ANY),
            ],
            out_specs=[half, half],
        ),
        out_shape=[jax.ShapeDtypeStruct(shape, BF)] * 2,
        input_output_aliases={3: 0, 4: 1},
        compiler_params=pltpu.CompilerParams(vmem_limit_bytes=40 * 1024 * 1024),
        cost_estimate=pl.CostEstimate(
            flops=2 * tok * model * nsq * hw, bytes_accessed=2 * tok * model * 2, transcendentals=0
        ),
        name="out_proj_grad",
    )(scalars, middle_low, mixed_part, *halves)


def rounded(size):
    return size + -size % 128


def unit_halves(units):
    first = rounded(units * 7 // 10)
    return first, units - first


def pack_kernel(lay, q_ref, k_ref, v_ref, r_ref, g_ref, out_ref, gate_ref, up_ref, down_ref, mix_ref, *all_refs):
    mix_ref[:, lay.q : lay.k] = q_ref[...]
    mix_ref[:, lay.k : lay.v] = k_ref[...]
    mix_ref[:, lay.v : lay.g] = v_ref[...]
    mix_ref[:, lay.g : lay.r] = g_ref[...]
    mix_ref[:, lay.r : lay.width] = jnp.zeros((mix_ref.shape[0], 128), BF)
    mix_ref[:, lay.r : lay.r + r_ref.shape[1]] = r_ref[...]
    hw, units = out_ref.shape[0], gate_ref.shape[1]
    all_refs[0][:, 0:hw] = out_ref[...].astype(F32).T.astype(BF)
    down = down_ref[...].astype(F32).T.astype(BF)
    start, lead = 0, hw
    for ref, size in zip(all_refs, unit_halves(units)):
        cols = slice(start, start + size)
        end = lead + 3 * size
        ref[:, lead : lead + size] = gate_ref[:, cols]
        ref[:, lead + size : lead + 2 * size] = up_ref[:, cols]
        ref[:, lead + 2 * size : end] = down[:, cols]
        if end < ref.shape[1]:
            ref[:, end:] = jnp.zeros((ref.shape[0], ref.shape[1] - end), BF)
        start, lead = start + size, 0


def pack(lay, w_query, w_key, w_value, w_rates, w_outgate, w_out, w_gate, w_up, w_down):
    rows = w_query.shape[0]
    one, two = unit_halves(w_gate.shape[1])
    return pl.pallas_call(
        functools.partial(pack_kernel, lay),
        out_shape=[
            jax.ShapeDtypeStruct((rows, lay.width), BF),
            jax.ShapeDtypeStruct((rows, rounded(w_out.shape[0] + 3 * one)), BF),
            jax.ShapeDtypeStruct((rows, rounded(3 * two)), BF),
        ],
        name="pack",
    )(w_query, w_key, w_value, w_rates, w_outgate, w_out, w_gate, w_up, w_down)


def unpack_kernel(hw, one, two, a_ref, b_ref, out_ref, gate_ref, up_ref, down_ref):
    a, b = a_ref[...].astype(F32), b_ref[...].astype(F32)
    out_ref[...] = b[:, :hw].T
    gate_ref[:, 0:one] = a[:, :one]
    gate_ref[:, one:] = b[:, hw : hw + two]
    up_ref[:, 0:one] = a[:, one : 2 * one]
    up_ref[:, one:] = b[:, hw + two : hw + 2 * two]
    down_ref[0:one, :] = a[:, 2 * one : 3 * one].T
    down_ref[one:, :] = b[:, hw + 2 * two : hw + 3 * two].T


def unpack(own_a, own_b, hw, units):
    one, two = unit_halves(units)
    rows = own_a.shape[0]
    shapes = [(hw, rows), (rows, units), (rows, units), (units, rows)]
    return pl.pallas_call(
        functools.partial(unpack_kernel, hw, one, two),
        out_shape=[jax.ShapeDtypeStruct(shape, F32) for shape in shapes],
        name="unpack",
    )(own_a, own_b)


def unpack_mix_kernel(lay, nrates, own_ref, q_ref, k_ref, v_ref, r_ref, g_ref):
    own = own_ref[...].astype(F32)
    q_ref[...] = own[:, lay.q : lay.k]
    k_ref[...] = own[:, lay.k : lay.v]
    v_ref[...] = own[:, lay.v : lay.g]
    r_ref[...] = own[:, lay.r : lay.r + nrates]
    g_ref[...] = own[:, lay.g : lay.r]


def unpack_mix(own, lay, nrates):
    rows = own.shape[0]
    widths = (lay.k - lay.q, lay.v - lay.k, lay.g - lay.v, nrates, lay.r - lay.g)
    return pl.pallas_call(
        functools.partial(unpack_mix_kernel, lay, nrates),
        out_shape=[jax.ShapeDtypeStruct((rows, width), F32) for width in widths],
        name="unpack_mix",
    )(own)
STEP = 4


def rms_parts(values):
    scale = lax.rsqrt(jnp.mean(values * values, axis=-1, keepdims=True) + EPS)
    return values * scale, scale


def bits(axis):
    return [1 << k for k in range((lax.axis_size(axis) - 1).bit_length())]


def trade(values, axis, bit):
    return lax.ppermute(values, axis, [(i, i ^ bit) for i in range(lax.axis_size(axis))])


def everyone(values):
    for axis in ("core", "dz", "sq", "sub"):
        for bit in bits(axis):
            values = values + trade(values, axis, bit)
    return values


def plus(left, right):
    return (left.astype(F32) + right.astype(F32)).astype(BF)


def swap(values, which, parts):
    return lax.ppermute(values, "sub", [(i, i ^ which) for i in range(parts)])


def per_device(
    tokens, lengths, out_grad, ln1_gain, ln2_gain, onorm_gain, a_log, dt_bias,
    w_query, w_key, w_value, w_rates, w_outgate, w_out, w_gate, w_up, w_down,
):
    nsq, parts = lax.axis_size("sq"), lax.axis_size("sub")
    which_seq, place = lax.axis_index("sq"), lax.axis_index("sub")
    count = nsq * parts
    tok_dev, model = tokens.shape
    heads = a_log.shape[0] // count
    lay = Layout(heads)
    units = w_gate.shape[1]
    hw = heads * HEAD
    place_arr = place.astype(jnp.int32).reshape(1)

    mix_shard, *ff_shards = pack(
        lay, w_query, w_key, w_value, w_rates, w_outgate, w_out, w_gate, w_up, w_down
    )
    w_mix = lax.all_gather(mix_shard, ("sq", "dz", "core"), axis=0, tiled=True)
    w_mix = w_mix.reshape(nsq, model, lay.width)
    walls = [
        lax.all_gather(shard, ("sq", "sub", "dz", "core"), axis=0, tiled=True).reshape(count, model, -1)
        for shard in ff_shards
    ]
    one, two = unit_halves(units)

    resid_in = tokens.astype(F32)
    normed_one, scale_one = rms_parts(resid_in)
    first = (normed_one * ln1_gain).astype(BF)
    first_seq = jnp.concatenate([first] + [swap(first, r, parts) for r in range(1, parts)], axis=0)

    pre = [dot_nn(first_seq, w_mix[s]) for s in range(nsq)]
    hpos = [(s * parts + place) * heads for s in range(nsq)]
    lanes = np.stack([8 * (c * nsq + s) + 3 * np.arange(heads) + 2 for c in range(STEP) for s in range(nsq)])

    def spread(values):
        mine = jnp.stack([lax.dynamic_slice_in_dim(values, hpos[s], heads) for s in range(nsq)])
        return jnp.zeros((128,), F32).at[lanes.ravel()].set(jnp.tile(mine.ravel(), STEP))

    params = jnp.stack([spread(-jnp.exp(a_log)), spread(dt_bias)])
    gain = onorm_gain.reshape(1, HEAD)
    mixed, *kept = mixer_forward(place_arr, parts, pre, params, gain, heads, STEP)

    got = [mixed] + [swap(mixed[:, r * tok_dev : (r + 1) * tok_dev], r, parts) for r in range(1, parts)]

    limit = jnp.sum(jnp.where(jnp.arange(nsq) == which_seq, lengths, 0)).astype(jnp.int32)
    scalars = jnp.stack([place.astype(jnp.int32), limit, lax.axis_index("core").astype(jnp.int32)])
    block = w_gate.shape[0]
    middle, second, grad_low = join(
        scalars, got, tokens, out_grad, walls[0], ln2_gain.reshape(1, model), parts, nsq, hw
    )
    def chips(pair):
        total = plus(pair[0], trade(pair[1], "core", 1))
        return total.reshape(count * model // 2, -1)

    def plane(values):
        return lax.psum_scatter(values, ("sq", "sub"), scatter_dimension=0, tiled=True)

    def column(values):
        return lax.psum_scatter(values, "dz", scatter_dimension=0, tiled=True)

    mlp_a, sg_a, *grads_a = feed_forward(
        scalars, second, grad_low, walls[0], hw, 0, rounded(3 * one), one, block
    )
    grads_a, wall_b = lax.optimization_barrier((chips(grads_a), walls[1]))
    grads_a = plane(grads_a)
    mlp_b, sg_b, *grads_b = feed_forward(
        scalars, second, grad_low, wall_b, 0, hw, hw + rounded(3 * two), two, block
    )
    block_out, middle_grad, middle_low, ln2_grad, *back = split(
        scalars, middle, (mlp_a, mlp_b), (sg_a, sg_b), grad_low, walls[0],
        ln2_gain.reshape(1, model), parts, nsq, hw,
    )
    for r in range(parts):
        grads_b = out_proj_grad(scalars, middle_low, got[r], grads_b, r, parts, nsq, hw, block)

    dmixed = jnp.concatenate([back[0]] + [swap(back[r], r, parts) for r in range(1, parts)], axis=1)
    dmixed, grads_b, grads_a = lax.optimization_barrier((dmixed, chips(grads_b), grads_a))
    own_a = column(grads_a)
    grads_b = plane(grads_b)
    chains = nsq * heads
    dpre = (jnp.zeros((chains, HEAD, HEAD), F32), jnp.zeros((8, 128), F32))
    for at in range(parts):
        *dpre, carry, small = mixer_backward(
            place_arr, parts, pre, params, gain, *kept, dmixed, heads, STEP, at, dpre
        )
        if at == 0:
            carry, grads_b = lax.optimization_barrier((carry, grads_b))
            own_b = column(grads_b)
        if at < parts - 1:
            dpre = (carry, small, *dpre)
    own_out, own_gate, own_up, own_down = unpack(own_a, own_b, hw, units)

    def back_rows(values, r):
        rows = slice(r * tok_dev, (r + 1) * tok_dev)
        total = dot_nt(values[0][rows], w_mix[0])
        for s in range(1, nsq):
            total = total + dot_nt(values[s][rows], w_mix[s])
        return total, jnp.sum(total * first_seq[rows].astype(F32), axis=0)

    mix_grads = jnp.concatenate([dot_tn(first_seq, dpre[s]).astype(BF) for s in range(nsq)], axis=0)
    dpre, mix_grads = lax.optimization_barrier((dpre, mix_grads))
    mix_own = lax.psum_scatter(mix_grads, ("sq", "dz", "core"), scatter_dimension=0, tiled=True)
    leaving = [back_rows(dpre, r) for r in range(1, parts)]
    arriving = [swap(leaving[r - 1][0].astype(BF), r, parts) for r in range(1, parts)]
    first_grad, ln1_grad = back_rows(dpre, 0)
    for r in range(1, parts):
        ln1_grad = ln1_grad + leaving[r - 1][1]
    ln1_grad = ln1_grad / ln1_gain
    first_grad, ln1_grad = lax.optimization_barrier((first_grad, ln1_grad))
    for r in range(1, parts):
        first_grad = first_grad + arriving[r - 1].astype(F32)
    scaled = first_grad * ln1_gain
    input_back = scale_one * (scaled - normed_one * jnp.mean(scaled * normed_one, axis=-1, keepdims=True))
    tokens_grad = (middle_grad + input_back).astype(BF)

    def gather_heads(row):
        mine = jnp.sum(row[lanes].reshape(STEP, nsq, heads), axis=0)
        full = jnp.zeros(a_log.shape, F32)
        for s in range(nsq):
            full = lax.dynamic_update_slice_in_dim(full, mine[s], hpos[s], 0)
        return full

    a_grad, dt_grad = gather_heads(small[2]), gather_heads(small[1])
    total = everyone(jnp.concatenate([ln1_grad, ln2_grad[0], small[0], a_grad, dt_grad]))
    marks = np.cumsum([0, model, model, HEAD, a_log.shape[0], a_log.shape[0]])
    return (
        block_out, tokens_grad, *[total[i:j] for i, j in zip(marks[:-1], marks[1:])],
        *unpack_mix(mix_own, lay, w_rates.shape[1]),
        own_out, own_gate, own_up, own_down,
    )


def solution(mesh):
    dp, tensor = mesh.shape["dp"], mesh.shape["tensor"]

    def run(*args):
        nsq = args[1].shape[0] // dp
        split = Mesh(
            mesh.devices.reshape(dp // 2, 2, nsq, tensor // nsq), ("dz", "core", "sq", "sub")
        )
        rows = P(("dz", "core", "sq", "sub"), None)
        down = P(("dz", "core"), ("sq", "sub"))
        across = P(("sq", "sub"), ("dz", "core"))
        in_specs = (rows, P(("dz", "core")), rows) + (P(),) * 5 + (down,) * 5 + (across, down, down, across)
        out_specs = (rows, rows) + (P(),) * 5 + (down,) * 5 + (across, down, down, across)
        return jax.shard_map(
            per_device, mesh=split, in_specs=in_specs, out_specs=out_specs, check_vma=False
        )(*args)

    return run
```

```python
import functools
import jax
import jax.numpy as jnp
import numpy as np
from jax import lax
from jax.experimental import pallas as pl
from jax.experimental.pallas import tpu as pltpu
from jax.sharding import Mesh
from jax.sharding import PartitionSpec as P

HEAD = 128
NH = 2
CT = 64
ROWS = CT * NH
EPS = 1e-06
HIGH = lax.Precision.HIGHEST
BF = jnp.bfloat16
F32 = jnp.float32


def dot_nn(left, right):
    return jnp.dot(left, right, preferred_element_type=F32)


def dot_nt(left, right):
    return lax.dot_general(left, right, (((1,), (1,)), ((), ())), preferred_element_type=F32)


def dot_tn(left, right):
    return lax.dot_general(left, right, (((0,), (0,)), ((), ())), preferred_element_type=F32)


def mixer_tables():
    row = np.arange(ROWS)
    tok, step = row % CT, row // CT
    order = tok * NH + step
    later = order[:, None] > order[None, :]
    barred = np.where(later, 0.0, -1e30).astype(np.float32)
    levels = []
    for size in (1, 4, 16):
        near = (tok[:, None] // (4 * size)) == (tok[None, :] // (4 * size))
        apart = (tok[:, None] // size) != (tok[None, :] // size)
        levels.append((near & apart).astype(np.float32))
    own = ((tok[:, None] == tok[None, :]) & later).astype(np.float32)
    eye = np.eye(ROWS, dtype=np.float32)
    read = np.zeros((CT, ROWS), np.float32)
    read[np.arange(CT), CT + np.arange(CT)] = 1.0
    sums = (np.arange(CT)[:, None] <= tok[None, :]).astype(np.float32)
    square = np.stack([barred, eye, own] + levels)
    thin = np.stack([read, sums])
    return square, thin, np.concatenate([sums] * 3, axis=0)


def sigm(values):
    return jax.nn.sigmoid(values)


class Layout:
    def __init__(self, heads):
        self.q = 0
        self.k = heads * HEAD
        self.v = self.k + heads * NH * HEAD
        self.g = self.v + heads * NH * HEAD
        self.r = self.g + heads * HEAD
        self.width = self.r + 128


def piece(refs, s, c, start):
    return refs[s][c * CT : (c + 1) * CT, start : start + HEAD]


def unit_silu(raw):
    sig = sigm(raw)
    act = raw * sig
    norm = lax.rsqrt(jnp.sum(act * act, axis=-1, keepdims=True) + EPS)
    return act * norm, norm, sig


def thirds(values):
    high = values.astype(BF)
    rest = values - high.astype(F32)
    middle = rest.astype(BF)
    return high, middle, (rest - middle.astype(F32)).astype(BF)


def rates_of(pre_ref, par_ref, sums_ref, nb, nsq, lay):
    raw = None
    for c in range(nb):
        for s in range(nsq):
            here = pre_ref[s][c * CT : (c + 1) * CT, lay.r : lay.r + 128]
            if c + s > 0:
                here = pltpu.roll(here, 8 * (c * nsq + s), axis=1)
            raw = here if raw is None else raw + here
    shifted = raw + par_ref[1:2, :]
    soft = jnp.maximum(shifted, 0.0) + jnp.log1p(jnp.exp(-jnp.abs(shifted)))
    decay = par_ref[0:1, :] * soft
    stacked = jnp.concatenate(thirds(decay), axis=0)
    sums = sums_ref[...]
    return sigm(raw), shifted, decay, dot_tn(sums, stacked), dot_tn(stacked, sums)


def chunk_parts(pre_ref, s, h, c, nsq, lay, betas, cum_col, cum_row, square_ref):
    query, nq, sq = unit_silu(piece(pre_ref, s, c, lay.q + h * HEAD))
    key0, nk0, sk0 = unit_silu(piece(pre_ref, s, c, lay.k + (2 * h) * HEAD))
    key1, nk1, sk1 = unit_silu(piece(pre_ref, s, c, lay.k + (2 * h + 1) * HEAD))
    keys = jnp.concatenate([key0, key1], axis=0)
    base = 8 * (c * nsq + s) + 3 * h
    wide = lambda column: jnp.broadcast_to(column, (CT, HEAD))
    beta = jnp.concatenate([wide(betas[:, base : base + 1]), wide(betas[:, base + 1 : base + 2])], axis=0)
    scaled = keys * beta
    g = wide(cum_col[:CT, base + 2 : base + 3])
    grow = cum_row[base + 2 : base + 3, :]
    weights = jnp.exp(jnp.concatenate([g, g], axis=0) - grow + square_ref[0])
    tail = g[CT - 1 : CT, :]
    grown, left = jnp.exp(g), jnp.exp(tail - g)
    return dict(
        query=query, keys=keys, beta=beta, scaled=scaled, weights=weights, grown=jnp.concatenate([grown, grown], axis=0),
        left=jnp.concatenate([left, left], axis=0), tail=jnp.exp(tail), nq=nq, sq=sq, nk=(nk0, nk1), sk=(sk0, sk1),
    )


def forward_kernel(lay, nsq, heads, nb, _, *refs):
    pre_ref = refs[:nsq]
    par_ref, gain_ref, square_ref, thin_ref, sums_ref = refs[nsq : nsq + 5]
    mixed_ref, tinv_ref, wk_ref, state_ref, delta_ref, o_ref, carry = refs[nsq + 5 :]

    @pl.when(pl.program_id(0) == 0)
    def _():
        carry[...] = jnp.zeros_like(carry)

    which = [(c, s, h) for c in range(nb) for s in range(nsq) for h in range(heads)]
    betas, _, _, cum_col, cum_row = rates_of(pre_ref, par_ref, sums_ref, nb, nsq, lay)
    parts = {}
    for c, s, h in which:
        parts[c, s, h] = chunk_parts(pre_ref, s, h, c, nsq, lay, betas, cum_col, cum_row, square_ref)
    lam, scores = {}, {}
    for key in which:
        p = parts[key]
        keys_low, scaled_low, query_low = p["keys"].astype(BF), p["scaled"].astype(BF), p["query"].astype(BF)
        both = dot_nt(jnp.concatenate([keys_low, query_low], axis=0), scaled_low)
        lam[key] = both[:ROWS] * p["weights"]
        scores[key] = (both[ROWS:] * (p["weights"][CT:] + thin_ref[0])).astype(BF)
    tinv = {key: square_ref[1] - lam[key] * square_ref[2] for key in which}
    for level in range(3):
        low = {key: tinv[key].astype(BF) for key in which}
        step = {key: dot_nn(low[key], (lam[key] * square_ref[3 + level]).astype(BF)).astype(BF) for key in which}
        twice = {key: dot_nn(step[key], step[key]).astype(BF) for key in which}
        half = {key: tinv[key] - dot_nn(step[key], low[key]) for key in which}
        tinv = {key: half[key] + dot_nn(twice[key], half[key].astype(BF)) for key in which}
    chains = [(s, h) for s in range(nsq) for h in range(heads)]
    mixed_in = {}
    for key in which:
        c, s, h = key
        p = parts[key]
        t_low = tinv[key].astype(BF)
        tinv_ref[c, s * heads + h] = t_low
        raw0 = piece(pre_ref, s, c, lay.v + (2 * h) * HEAD)
        raw1 = piece(pre_ref, s, c, lay.v + (2 * h + 1) * HEAD)
        values = jnp.concatenate([raw0 * sigm(raw0), raw1 * sigm(raw1)], axis=0)
        kg = p["keys"] * p["grown"]
        solved = dot_nn(t_low, jnp.concatenate([values, kg], axis=1).astype(BF))
        wk = solved[:, HEAD:].astype(BF)
        wk_ref[c, s * heads + h] = wk
        qg = (p["query"] * p["grown"][:CT]).astype(BF)
        mixed_in[key] = (solved[:, :HEAD], jnp.concatenate([wk, qg], axis=0), (p["scaled"] * p["left"]).astype(BF))
    state = {k: carry[k[0] * heads + k[1]] for k in chains}
    read, deltas = {}, {}
    for c in range(nb):
        low = {k: state[k].astype(BF) for k in chains}
        for s, h in chains:
            state_ref[c, s * heads + h] = low[s, h]
        seen = {k: dot_nn(mixed_in[(c,) + k][1], low[k]) for k in chains}
        delta = {k: (mixed_in[(c,) + k][0] - seen[k][:ROWS]).astype(BF) for k in chains}
        state = {k: parts[(c,) + k]["tail"] * state[k] + dot_tn(mixed_in[(c,) + k][2], delta[k]) for k in chains}
        for k in chains:
            read[(c,) + k] = seen[k][ROWS:]
            deltas[(c,) + k] = delta[k]
    for s, h in chains:
        carry[s * heads + h] = state[s, h]
    for key in which:
        c, s, h = key
        delta_ref[c, s * heads + h] = deltas[key]
        out = read[key] + dot_nn(scores[key], deltas[key])
        o_ref[s, c * CT : (c + 1) * CT, h * HEAD : (h + 1) * HEAD] = out
        scale = lax.rsqrt(jnp.mean(out * out, axis=-1, keepdims=True) + EPS)
        gate = piece(pre_ref, s, c, lay.g + h * HEAD)
        mixed = out * scale * gain_ref[0:1, :] * (gate * sigm(gate))
        mixed_ref[s, c * CT : (c + 1) * CT, h * HEAD : (h + 1) * HEAD] = mixed.astype(BF)


def silu_slope(raw, sig):
    return sig * (1.0 + raw * (1.0 - sig))


def backward_kernel(lay, nsq, heads, nb, _, *refs):
    pre_ref = refs[:nsq]
    par_ref, gain_ref, square_ref, thin_ref, sums_ref = refs[nsq : nsq + 5]
    tinv_ref, wk_ref, state_ref, delta_ref, o_ref, dm_ref = refs[nsq + 5 : nsq + 11]
    carry_in, small_in = refs[nsq + 11 : nsq + 13]
    dpre_ref = refs[-nsq - 3 : -3]
    carry, acc, carried = refs[-3:]

    @pl.when(pl.program_id(0) == 0)
    def _():
        carried[...] = carry_in[...]
        acc[...] = small_in[...]

    lane = lax.broadcasted_iota(jnp.int32, (CT, 128), 1)
    sub8 = lax.broadcasted_iota(jnp.int32, (8, 128), 0)
    chains = [(s, h) for s in range(nsq) for h in range(heads)]
    spans = [slice(c * CT, (c + 1) * CT) for c in range(nb)]
    gain = gain_ref[0:1, :]
    gain_sum = jnp.zeros((1, HEAD), F32)
    work = {}
    betas, shifted, decay, cum_col, cum_row = rates_of(pre_ref, par_ref, sums_ref, nb, nsq, lay)
    for c in reversed(range(nb)):
        for s, h in chains:
            cols = slice(h * HEAD, (h + 1) * HEAD)
            p = chunk_parts(pre_ref, s, h, c, nsq, lay, betas, cum_col, cum_row, square_ref)
            out = o_ref[s, spans[c], cols]
            dm = dm_ref[s, spans[c], cols].astype(F32)
            graw = piece(pre_ref, s, c, lay.g + h * HEAD)
            gsig = sigm(graw)
            gate = graw * gsig
            scale = lax.rsqrt(jnp.mean(out * out, axis=-1, keepdims=True) + EPS)
            normed = out * scale
            dpre_ref[s][spans[c], lay.g + h * HEAD : lay.g + (h + 1) * HEAD] = (
                dm * normed * gain * (gsig + gate * (1.0 - gsig))
            ).astype(BF)
            dn = dm * gate
            gain_sum = gain_sum + jnp.sum(dn * normed, axis=0, keepdims=True)
            scaled_dn = dn * gain
            dout = scale * (scaled_dn - normed * jnp.mean(scaled_dn * normed, axis=-1, keepdims=True))
            dout_low = dout.astype(BF)
            keys_low, query_low = p["keys"].astype(BF), p["query"].astype(BF)
            scaled_low = p["scaled"].astype(BF)
            both_low = jnp.concatenate([keys_low, query_low], axis=0)
            w_all = jnp.concatenate([p["weights"], p["weights"][CT:] + thin_ref[0]], axis=0)
            weighted = dot_nt(both_low, scaled_low) * w_all
            p["w_all"], p["weighted"], p["both_low"], p["scaled_low"] = w_all, weighted, both_low, scaled_low
            p["dout_low"] = dout_low
            p["from_out"] = dot_tn(weighted[ROWS:].astype(BF), dout_low)
            qg = (p["query"] * p["grown"][:CT]).astype(BF)
            p["to_state"] = dot_tn(qg, dout_low)
            p["kout"] = (p["scaled"] * p["left"]).astype(BF)
            work[c, s, h] = p
    dstate = {k: carried[k[0] * heads + k[1]] for k in chains}
    for c in reversed(range(nb)):
        low = {k: dstate[k].astype(BF) for k in chains}
        ddelta = {
            k: (work[(c,) + k]["from_out"] + dot_nn(work[(c,) + k]["kout"], low[k])).astype(BF) for k in chains
        }
        for k in chains:
            p = work[(c,) + k]
            p["ddelta"], p["dstate"], p["dstate_low"] = ddelta[k], dstate[k], low[k]
        dstate = {
            k: work[(c,) + k]["tail"] * dstate[k]
            + work[(c,) + k]["to_state"]
            - dot_tn(wk_ref[c, k[0] * heads + k[1]], ddelta[k])
            for k in chains
        }
    for s, h in chains:
        carried[s * heads + h] = dstate[s, h]
        carry[s * heads + h] = dstate[s, h]
    read_all = jnp.zeros((CT, 128), F32)
    dtail_all = jnp.zeros((1, 128), F32)
    dbeta_all = jnp.zeros((CT, 128), F32)
    col_rows = {}
    for c in reversed(range(nb)):
        span = spans[c]
        for s in range(nsq):
            dcol_all = jnp.zeros((8, 128), F32)
            for h in range(heads):
                at = s * heads + h
                p = work[c, s, h]
                dpv = dot_tn(tinv_ref[c, at], p["ddelta"])
                joint = jnp.concatenate([(-dpv).astype(BF), p["dout_low"]], axis=0)
                delta = delta_ref[c, at]
                state_low = state_ref[c, at]
                inner = dot_nt(joint, delta)
                inner_low = (inner * p["w_all"]).astype(BF)
                pairs = inner * p["weighted"]
                grown_all = jnp.concatenate([p["grown"], p["grown"][:CT]], axis=0)
                base = 8 * (c * nsq + s) + 3 * h
                entered = grown_all * dot_nt(joint, state_low)
                left_out = p["left"] * dot_nt(delta, p["dstate_low"])
                direct = dot_nn(inner_low, p["scaled_low"]) + entered
                dscaled = dot_tn(inner_low, p["both_low"]) + left_out
                both_rows = jnp.concatenate([p["keys"], p["query"]], axis=0)
                row_part = jnp.sum(pairs + both_rows * entered, axis=-1, keepdims=True)
                col_part = jnp.sum(pairs, axis=0, keepdims=True)
                out_part = jnp.sum(p["scaled"] * left_out, axis=-1, keepdims=True)
                dtail = p["tail"] * jnp.sum(
                    jnp.sum(state_low.astype(F32) * p["dstate"], axis=0, keepdims=True), axis=1, keepdims=True
                ) + jnp.sum(out_part, axis=0, keepdims=True)
                dkeys, dquery = direct[:ROWS], direct[ROWS:]
                dbeta = jnp.sum(p["keys"] * dscaled, axis=-1, keepdims=True)
                kdot = jnp.sum(p["keys"] * dkeys, axis=-1, keepdims=True)
                qdot = jnp.sum(p["query"] * dquery, axis=-1, keepdims=True)
                kfull = kdot + p["beta"] * dbeta
                tokens = row_part[:CT] + row_part[CT:ROWS] + row_part[ROWS:] - out_part[:CT] - out_part[CT:]
                read_all = jnp.where(lane == base + 2, tokens, read_all)
                dcol_all = jnp.where(sub8 == 3 * h + 2, col_part, dcol_all)
                dtail_all = jnp.where(lane[0:1] == base + 2, dtail, dtail_all)
                dbeta_all = jnp.where(lane == base, dbeta[:CT], dbeta_all)
                dbeta_all = jnp.where(lane == base + 1, dbeta[CT:], dbeta_all)
                dk = dkeys + p["beta"] * dscaled
                dk = dk - p["keys"] * kfull
                for j in range(NH):
                    part = slice(j * CT, (j + 1) * CT)
                    start = lay.k + (2 * h + j) * HEAD
                    kraw = piece(pre_ref, s, c, start)
                    dpre_ref[s][span, start : start + HEAD] = (
                        dk[part] * p["nk"][j] * silu_slope(kraw, p["sk"][j])
                    ).astype(BF)
                    start = lay.v + (2 * h + j) * HEAD
                    vraw = piece(pre_ref, s, c, start)
                    dpre_ref[s][span, start : start + HEAD] = (
                        dpv[part] * silu_slope(vraw, sigm(vraw))
                    ).astype(BF)
                start = lay.q + h * HEAD
                qraw = piece(pre_ref, s, c, start)
                dq = (dquery - p["query"] * qdot) * p["nq"]
                dpre_ref[s][span, start : start + HEAD] = (dq * silu_slope(qraw, p["sq"])).astype(BF)
            col_rows[c * nsq + s] = dcol_all
    sums = sums_ref[0:CT, :]
    reads = jnp.concatenate(thirds(read_all), axis=0)
    padding = [jnp.zeros((128 - 8 * len(col_rows), 128), F32)] if len(col_rows) < 16 else []
    columns = jnp.concatenate([col_rows[k] for k in range(len(col_rows))] + padding, axis=0)
    ddecay = dot_nn(jnp.concatenate([sums[:, :CT]] * 3, axis=1), reads) + dtail_all
    for term in thirds(columns):
        ddecay = ddecay - dot_nt(sums, term)
    dshift = ddecay * par_ref[0:1, :] * sigm(shifted)
    acc[1:2, :] += jnp.sum(dshift, axis=0, keepdims=True)
    acc[2:3, :] += jnp.sum(ddecay * decay, axis=0, keepdims=True)
    drates = dshift + dbeta_all * betas * (1.0 - betas)
    for c in range(nb):
        for s in range(nsq):
            shift = 8 * (c * nsq + s)
            here = pltpu.roll(drates, 128 - shift, axis=1) if shift else drates
            dpre_ref[s][spans[c], lay.r : lay.r + 128] = jnp.where(lane < 8, here, 0.0).astype(BF)
    acc[0:1, :] += gain_sum


def shared_specs(square, thin, sums):
    return [
        pl.BlockSpec((2, 128), lambda i, _: (0, 0)),
        pl.BlockSpec((1, HEAD), lambda i, _: (0, 0)),
        pl.BlockSpec(square.shape, lambda i, _: (0, 0, 0)),
        pl.BlockSpec(thin.shape, lambda i, _: (0, 0, 0)),
        pl.BlockSpec(sums.shape, lambda i, _: (0, 0)),
    ]


def part_chunk(step, place, per_part):
    return ((step // per_part) ^ place[0]) * per_part + step % per_part


def mixer_forward(place, parts, pre, params, gain, heads, nb=2):
    nsq, (length, width) = len(pre), pre[0].shape
    lay = Layout(heads)
    square, thin, sums3 = mixer_tables()
    nchunk = length // CT
    chains = nsq * heads
    span = nb * CT
    per_part = nchunk // nb // parts
    big = lambda: pl.BlockSpec((nb, chains, ROWS, HEAD), lambda i, _: (i, 0, 0, 0))
    rows = lambda w: pl.BlockSpec((nsq, span, w), lambda i, place: (0, part_chunk(i, place, per_part), 0))
    wide = lambda: pl.BlockSpec((span, width), lambda i, place: (part_chunk(i, place, per_part), 0))
    return pl.pallas_call(
        functools.partial(forward_kernel, lay, nsq, heads, nb),
        grid_spec=pltpu.PrefetchScalarGridSpec(
            num_scalar_prefetch=1,
            grid=(nchunk // nb,),
            in_specs=[wide() for _ in pre] + shared_specs(square, thin, sums3),
            out_specs=[rows(heads * HEAD), big(), big(), big(), big(), rows(heads * HEAD)],
            scratch_shapes=[pltpu.VMEM((chains, HEAD, HEAD), F32)],
        ),
        out_shape=[
            jax.ShapeDtypeStruct((nsq, length, heads * HEAD), BF),
            jax.ShapeDtypeStruct((nchunk, chains, ROWS, ROWS), BF),
            jax.ShapeDtypeStruct((nchunk, chains, ROWS, HEAD), BF),
            jax.ShapeDtypeStruct((nchunk, chains, HEAD, HEAD), BF),
            jax.ShapeDtypeStruct((nchunk, chains, ROWS, HEAD), BF),
            jax.ShapeDtypeStruct((nsq, length, heads * HEAD), F32),
        ],
        compiler_params=pltpu.CompilerParams(vmem_limit_bytes=56 * 1024 * 1024),
        cost_estimate=pl.CostEstimate(
            flops=nchunk * chains * 20 * 2 * ROWS**3,
            bytes_accessed=nsq * length * (4 * width + 6 * heads * HEAD) + nchunk * chains * 6 * ROWS**2,
            transcendentals=0,
        ),
        name="mixer_forward",
    )(place, *pre, params, gain, jnp.asarray(square), jnp.asarray(thin), jnp.asarray(sums3, BF))


def mixer_backward(place, parts, pre, params, gain, tinv, wks, states, deltas, outs, dmixed, heads, nb, skip, steps, earlier):
    nsq, (length, width) = len(pre), pre[0].shape
    lay = Layout(heads)
    square, thin, sums3 = mixer_tables()
    nchunk = length // CT
    chains = nsq * heads
    span = nb * CT
    per_part = nchunk // nb // parts
    last = nchunk // nb - 1 - skip
    big = lambda: pl.BlockSpec((nb, chains, ROWS, HEAD), lambda i, _: (last - i, 0, 0, 0))
    rows = lambda w: pl.BlockSpec(
        (nsq, span, w), lambda i, place: (0, part_chunk(last - i, place, per_part), 0)
    )
    wide = lambda: pl.BlockSpec((span, width), lambda i, place: (part_chunk(last - i, place, per_part), 0))
    held = pl.BlockSpec((chains, HEAD, HEAD), lambda i, _: (0, 0, 0))
    sums = pl.BlockSpec((8, 128), lambda i, _: (0, 0))
    carry, small, *done = earlier
    first_done = nsq + 14
    return pl.pallas_call(
        functools.partial(backward_kernel, lay, nsq, heads, nb),
        grid_spec=pltpu.PrefetchScalarGridSpec(
            num_scalar_prefetch=1,
            grid=(steps,),
            in_specs=[wide() for _ in pre]
            + shared_specs(square, thin, sums3)
            + [big(), big(), big(), big(), rows(heads * HEAD), rows(heads * HEAD), held, sums]
            + [pl.BlockSpec(memory_space=pl.ANY) for _ in done],
            out_specs=[wide() for _ in pre] + [held, sums],
            scratch_shapes=[pltpu.VMEM((chains, HEAD, HEAD), F32)],
        ),
        out_shape=[jax.ShapeDtypeStruct((length, width), BF) for _ in pre]
        + [jax.ShapeDtypeStruct((chains, HEAD, HEAD), F32), jax.ShapeDtypeStruct((8, 128), F32)],
        input_output_aliases={first_done + k: k for k in range(len(done))},
        compiler_params=pltpu.CompilerParams(vmem_limit_bytes=56 * 1024 * 1024),
        cost_estimate=pl.CostEstimate(
            flops=steps * nb * chains * 26 * 2 * ROWS**3,
            bytes_accessed=(nsq * length * (6 * width + 6 * heads * HEAD) + nchunk * chains * 8 * ROWS**2) * steps * nb // nchunk,
            transcendentals=0,
        ),
        name="mixer_backward",
    )(
        place, *pre, params, gain, jnp.asarray(square), jnp.asarray(thin), jnp.asarray(sums3, BF),
        tinv, wks, states, deltas, outs, dmixed, carry, small, *done,
    )


TILE = 256


def token_mask(place, limit, tile, rows, base):
    position = place * rows + base + lax.broadcasted_iota(jnp.int32, (tile, 1), 0)
    return position < limit


def join_kernel(parts, nsq, tok, scalars, *refs):
    mixed_refs = refs[:parts]
    x_ref, og_ref, wout_ref, gain_ref = refs[parts : parts + 4]
    middle_ref, second_ref, grad_ref = refs[parts + 4 :]
    place, limit = scalars[0], scalars[1]
    total = x_ref[...].astype(F32)
    for r in range(parts):
        for s in range(nsq):
            total = total + dot_nt(mixed_refs[r][s], wout_ref[s * parts + (place ^ r)])
    middle_ref[...] = total
    scale = lax.rsqrt(jnp.mean(total * total, axis=-1, keepdims=True) + EPS)
    second_ref[...] = (total * scale * gain_ref[...]).astype(BF)
    keep = token_mask(place, limit, x_ref.shape[0], tok, pl.program_id(0) * x_ref.shape[0])
    grad_ref[...] = jnp.where(keep, og_ref[...].astype(F32), 0.0).astype(BF)


def join(scalars, mixed_parts, x, out_grad, wall, gain, parts, nsq, hw):
    tok, model = x.shape
    count = parts * nsq
    tile = min(TILE, tok)
    row = pl.BlockSpec((tile, model), lambda i, _: (i, 0))
    return pl.pallas_call(
        functools.partial(join_kernel, parts, nsq, tok),
        grid_spec=pltpu.PrefetchScalarGridSpec(
            num_scalar_prefetch=1,
            grid=(tok // tile,),
            in_specs=[pl.BlockSpec((nsq, tile, hw), lambda i, _: (0, i, 0)) for _ in mixed_parts]
            + [row, row, pl.BlockSpec((count, model, hw), lambda i, _: (0, 0, 0)),
               pl.BlockSpec((1, model), lambda i, _: (0, 0))],
            out_specs=[row, row, row],
        ),
        out_shape=[
            jax.ShapeDtypeStruct((tok, model), F32),
            jax.ShapeDtypeStruct((tok, model), BF),
            jax.ShapeDtypeStruct((tok, model), BF),
        ],
        compiler_params=pltpu.CompilerParams(vmem_limit_bytes=40 * 1024 * 1024),
        cost_estimate=pl.CostEstimate(
            flops=2 * tok * model * count * hw, bytes_accessed=14 * tok * model, transcendentals=0
        ),
        name="join",
    )(scalars, *mixed_parts, x, out_grad, wall, gain)


def core_halves(core, block, value):
    count = value.shape[0] // block
    pieces = [value[j * block : (j + 1) * block] for j in range(count)]
    join_all = lambda items: items[0] if len(items) == 1 else jnp.concatenate(items, axis=0)
    even, odd = join_all(pieces[0::2]), join_all(pieces[1::2])
    return jnp.where(core == 0, even, odd), jnp.where(core == 0, odd, even)


def ff_tiles(tile, lead, units, sec_ref, grad_ref, w_ref, mlp_ref, sg_ref, store):
    tok, model = sec_ref.shape
    mid, end = lead + 2 * units, lead + 3 * units

    @pl.when(pl.program_id(0) == 0)
    def _():
        mlp_ref[...] = jnp.zeros_like(mlp_ref)
        sg_ref[...] = jnp.zeros_like(sg_ref)

    for m in range(tok // tile):
        rows = slice(m * tile, (m + 1) * tile)
        pre = dot_nn(sec_ref[rows, :], w_ref[0, :, lead:mid])
        gate_pre, up_pre = pre[:, :units], pre[:, units:]
        hidden_grad = dot_nn(grad_ref[rows, :], w_ref[0, :, mid:end])
        sig = sigm(gate_pre)
        act = gate_pre * sig
        hidden = (act * up_pre).astype(BF)
        gate_low = (hidden_grad * up_pre * (sig + act * (1.0 - sig))).astype(BF)
        up_low = (hidden_grad * act).astype(BF)
        both_low = jnp.concatenate([gate_low, up_low], axis=1)
        store(rows, hidden, both_low)
        mlp_ref[rows, :] += dot_nt(hidden, w_ref[0, :, mid:end])
        sg_ref[rows, :] += dot_nt(both_low, w_ref[0, :, lead:mid])


def weight_tiles(core, block, lead_out, sec_ref, grad_ref, hid, both, keep_ref, send_ref):
    model, units = sec_ref.shape[1], hid.shape[1]
    mid_out, end_out = lead_out + 2 * units, lead_out + 3 * units
    step = min(256, model)
    for k in range(model // step):
        cols = slice(k * step, (k + 1) * step)
        rows = slice(k * step // 2, (k + 1) * step // 2)
        value = core_halves(core, block, dot_tn(sec_ref[:, cols], both[...]))
        keep_ref[0, rows, lead_out:mid_out] = value[0].astype(BF)
        send_ref[0, rows, lead_out:mid_out] = value[1].astype(BF)
        value = core_halves(core, block, dot_tn(grad_ref[:, cols], hid[...]))
        keep_ref[0, rows, mid_out:end_out] = value[0].astype(BF)
        send_ref[0, rows, mid_out:end_out] = value[1].astype(BF)


def ff_kernel(tile, block, lead, units, scalars, sec_ref, grad_ref, w_ref, mlp_ref, sg_ref, keep_ref, send_ref, hid, both):
    def store(rows, hidden, both_low):
        hid[rows, :] = hidden
        both[rows, :] = both_low

    ff_tiles(tile, lead, units, sec_ref, grad_ref, w_ref, mlp_ref, sg_ref, store)
    weight_tiles(scalars[2], block, 0, sec_ref, grad_ref, hid, both, keep_ref, send_ref)


def feed_forward(scalars, second, grad_low, wall, lead, width_out, units, block):
    tok, model = second.shape
    count, _, width = wall.shape
    whole = pl.BlockSpec((tok, model), lambda p, _: (0, 0))
    weight = pl.BlockSpec((1, model, width), lambda p, _: (p, 0, 0))
    half = pl.BlockSpec((1, model // 2, width_out), lambda p, _: (p, 0, 0))
    return pl.pallas_call(
        functools.partial(ff_kernel, min(TILE, tok), block, lead, units),
        grid_spec=pltpu.PrefetchScalarGridSpec(
            num_scalar_prefetch=1,
            grid=(count,),
            in_specs=[whole, whole, weight],
            out_specs=[whole, whole, half, half],
            scratch_shapes=[pltpu.VMEM((tok, units), BF), pltpu.VMEM((tok, 2 * units), BF)],
        ),
        out_shape=[
            jax.ShapeDtypeStruct((tok, model), F32),
            jax.ShapeDtypeStruct((tok, model), F32),
            jax.ShapeDtypeStruct((count, model // 2, width_out), BF),
            jax.ShapeDtypeStruct((count, model // 2, width_out), BF),
        ],
        compiler_params=pltpu.CompilerParams(vmem_limit_bytes=62 * 1024 * 1024),
        cost_estimate=pl.CostEstimate(
            flops=18 * tok * model * units * count,
            bytes_accessed=count * model * width * 4 + 12 * tok * model,
            transcendentals=0,
        ),
        name="feed_forward",
    )(scalars, second, grad_low, wall)


def ff_rest_kernel(tile, units, sec_ref, grad_ref, w_ref, mlp_ref, sg_ref, hid_ref, both_ref):
    def store(rows, hidden, both_low):
        hid_ref[0, rows, :] = hidden
        both_ref[0, rows, :] = both_low

    ff_tiles(tile, 0, units, sec_ref, grad_ref, w_ref, mlp_ref, sg_ref, store)


def feed_forward_rest(second, grad_low, wall, units):
    tok, model = second.shape
    count, _, width = wall.shape
    whole = pl.BlockSpec((tok, model), lambda p: (0, 0))
    part = lambda w: pl.BlockSpec((1, tok, w), lambda p: (p, 0, 0))
    return pl.pallas_call(
        functools.partial(ff_rest_kernel, min(TILE, tok), units),
        grid=(count,),
        in_specs=[whole, whole, pl.BlockSpec((1, model, width), lambda p: (p, 0, 0))],
        out_specs=[whole, whole, part(units), part(2 * units)],
        out_shape=[
            jax.ShapeDtypeStruct((tok, model), F32),
            jax.ShapeDtypeStruct((tok, model), F32),
            jax.ShapeDtypeStruct((count, tok, units), BF),
            jax.ShapeDtypeStruct((count, tok, 2 * units), BF),
        ],
        compiler_params=pltpu.CompilerParams(vmem_limit_bytes=62 * 1024 * 1024),
        cost_estimate=pl.CostEstimate(
            flops=12 * tok * model * units * count,
            bytes_accessed=count * model * width * 2 + 12 * tok * model,
            transcendentals=0,
        ),
        name="feed_forward_rest",
    )(second, grad_low, wall)


def rest_grad_kernel(block, parts, hw, scalars, sec_ref, grad_ref, ml_ref, hid_ref, both_ref, *refs):
    mixed_refs, (keep_ref, send_ref) = refs[:-2], refs[-2:]
    model = sec_ref.shape[1]
    weight_tiles(scalars[2], block, hw, sec_ref, grad_ref, hid_ref.at[0], both_ref.at[0], keep_ref, send_ref)
    wanted = scalars[0] ^ (pl.program_id(0) % parts)
    mixed = mixed_refs[0][0]
    for r in range(1, parts):
        mixed = jnp.where(wanted == r, mixed_refs[r][0], mixed)
    step = min(256, model)
    for k in range(model // step):
        rows = slice(k * step // 2, (k + 1) * step // 2)
        value = core_halves(scalars[2], block, dot_tn(ml_ref[:, k * step : (k + 1) * step], mixed))
        keep_ref[0, rows, 0:hw] = value[0].astype(BF)
        send_ref[0, rows, 0:hw] = value[1].astype(BF)


def rest_grad(scalars, second, grad_low, middle_low, hidden, both, mixed_parts, width_out, parts, nsq, hw, block):
    tok, model = second.shape
    count, _, units = hidden.shape
    whole = pl.BlockSpec((tok, model), lambda p, _: (0, 0))
    part = lambda w: pl.BlockSpec((1, tok, w), lambda p, _: (p, 0, 0))
    half = pl.BlockSpec((1, model // 2, width_out), lambda p, _: (p, 0, 0))
    return pl.pallas_call(
        functools.partial(rest_grad_kernel, block, parts, hw),
        grid_spec=pltpu.PrefetchScalarGridSpec(
            num_scalar_prefetch=1,
            grid=(count,),
            in_specs=[whole, whole, whole, part(units), part(2 * units)]
            + [pl.BlockSpec((1, tok, hw), lambda p, _: (p // parts, 0, 0)) for _ in mixed_parts],
            out_specs=[half, half],
        ),
        out_shape=[jax.ShapeDtypeStruct((count, model // 2, width_out), BF)] * 2,
        compiler_params=pltpu.CompilerParams(vmem_limit_bytes=50 * 1024 * 1024),
        cost_estimate=pl.CostEstimate(
            flops=2 * tok * model * (3 * units + hw) * count,
            bytes_accessed=count * model * width_out * 2 + 6 * tok * model,
            transcendentals=0,
        ),
        name="rest_grad",
    )(scalars, second, grad_low, middle_low, hidden, both, *mixed_parts)


def split_kernel(parts, nsq, tok, scalars, *refs):
    middle_ref, mlp_ref, mlp2_ref, sg_ref, sg2_ref, grad_ref, wout_ref, gain_ref = refs[:8]
    out_ref, mg_ref, ml_ref, ln_ref = refs[8:12]
    back_refs = refs[12:]
    place, limit = scalars[0], scalars[1]
    tile = middle_ref.shape[0]
    middle = middle_ref[...]
    keep = token_mask(place, limit, tile, tok, pl.program_id(0) * tile)
    out_ref[...] = jnp.where(keep, middle + (mlp_ref[...] + mlp2_ref[...]), 0.0).astype(BF)
    scale = lax.rsqrt(jnp.mean(middle * middle, axis=-1, keepdims=True) + EPS)
    normed = middle * scale
    sg = sg_ref[...] + sg2_ref[...]

    @pl.when(pl.program_id(0) == 0)
    def _():
        ln_ref[...] = jnp.zeros_like(ln_ref)

    ln_ref[...] += jnp.sum(sg * normed, axis=0, keepdims=True)
    scaled = sg * gain_ref[...]
    back = scale * (scaled - normed * jnp.mean(scaled * normed, axis=-1, keepdims=True))
    total = grad_ref[...].astype(F32) + back
    mg_ref[...] = total
    low = total.astype(BF)
    ml_ref[...] = low
    for r in range(parts):
        for s in range(nsq):
            back_refs[r][s] = dot_nn(low, wout_ref[s * parts + (place ^ r)]).astype(BF)


def split(scalars, middle, mlps, second_grads, grad_low, wall, gain, parts, nsq, hw):
    tok, model = middle.shape
    count = parts * nsq
    tile = min(TILE, tok)
    row = pl.BlockSpec((tile, model), lambda i, _: (i, 0))
    line = pl.BlockSpec((1, model), lambda i, _: (0, 0))
    return pl.pallas_call(
        functools.partial(split_kernel, parts, nsq, tok),
        grid_spec=pltpu.PrefetchScalarGridSpec(
            num_scalar_prefetch=1,
            grid=(tok // tile,),
            in_specs=[row] * 6 + [pl.BlockSpec((count, model, hw), lambda i, _: (0, 0, 0)), line],
            out_specs=[row, row, row, line]
            + [pl.BlockSpec((nsq, tile, hw), lambda i, _: (0, i, 0)) for _ in range(parts)],
        ),
        out_shape=[
            jax.ShapeDtypeStruct((tok, model), BF),
            jax.ShapeDtypeStruct((tok, model), F32),
            jax.ShapeDtypeStruct((tok, model), BF),
            jax.ShapeDtypeStruct((1, model), F32),
        ]
        + [jax.ShapeDtypeStruct((nsq, tok, hw), BF) for _ in range(parts)],
        compiler_params=pltpu.CompilerParams(vmem_limit_bytes=40 * 1024 * 1024),
        cost_estimate=pl.CostEstimate(
            flops=2 * tok * model * count * hw, bytes_accessed=26 * tok * model, transcendentals=0
        ),
        name="split",
    )(scalars, middle, *mlps, *second_grads, grad_low, wall, gain)


def rounded(size):
    return size + -size % 128


def unit_halves(units):
    first = rounded((units + 1) // 2)
    return first, units - first


def turn(values):
    return values.astype(F32).T.astype(BF)


def pack_mix_kernel(lay, q_ref, k_ref, v_ref, r_ref, g_ref, mix_ref):
    mix_ref[:, lay.q : lay.k] = q_ref[...]
    mix_ref[:, lay.k : lay.v] = k_ref[...]
    mix_ref[:, lay.v : lay.g] = v_ref[...]
    mix_ref[:, lay.g : lay.r] = g_ref[...]
    mix_ref[:, lay.r : lay.width] = jnp.zeros((mix_ref.shape[0], 128), BF)
    mix_ref[:, lay.r : lay.r + r_ref.shape[1]] = r_ref[...]


def pack_mix(lay, w_query, w_key, w_value, w_rates, w_outgate):
    return pl.pallas_call(
        functools.partial(pack_mix_kernel, lay),
        out_shape=jax.ShapeDtypeStruct((w_query.shape[0], lay.width), BF),
        name="pack_mix",
    )(w_query, w_key, w_value, w_rates, w_outgate)


def pack_kernel(out_ref, gate_ref, up_ref, down_ref, *all_refs):
    hw, units = out_ref.shape[0], gate_ref.shape[0]
    all_refs[0][:, 0:hw] = turn(out_ref[...])
    whole = [turn(ref[...]) for ref in (gate_ref, up_ref, down_ref)]
    start, lead = 0, hw
    for ref, size in zip(all_refs, unit_halves(units)):
        for k in range(3):
            ref[:, lead + k * size : lead + (k + 1) * size] = whole[k][:, start : start + size]
        end = lead + 3 * size
        if end < ref.shape[1]:
            ref[:, end:] = jnp.zeros((ref.shape[0], ref.shape[1] - end), BF)
        start, lead = start + size, 0


def pack(w_out, w_gate, w_up, w_down):
    rows = w_out.shape[1]
    one, two = unit_halves(w_down.shape[0])
    return pl.pallas_call(
        pack_kernel,
        out_shape=[
            jax.ShapeDtypeStruct((rows, rounded(w_out.shape[0] + 3 * one)), BF),
            jax.ShapeDtypeStruct((rows, rounded(3 * two)), BF),
        ],
        name="pack",
    )(w_out, w_gate.T, w_up.T, w_down)


def project_kernel(x_ref, w_ref, *out_refs):
    step = min(256, x_ref.shape[0])
    for m in range(x_ref.shape[0] // step):
        rows = slice(m * step, (m + 1) * step)
        for s, out_ref in enumerate(out_refs):
            out_ref[rows, :] = dot_nn(x_ref[rows, :], w_ref[s])


def project(values, weights):
    nsq, model, width = weights.shape
    rows = values.shape[0]
    tile = min(512, rows)
    return pl.pallas_call(
        project_kernel,
        grid=(rows // tile,),
        in_specs=[
            pl.BlockSpec((tile, model), lambda i: (i, 0)),
            pl.BlockSpec((nsq, model, width), lambda i: (0, 0, 0)),
        ],
        out_specs=[pl.BlockSpec((tile, width), lambda i: (i, 0))] * nsq,
        out_shape=[jax.ShapeDtypeStruct((rows, width), F32)] * nsq,
        compiler_params=pltpu.CompilerParams(vmem_limit_bytes=50 * 1024 * 1024),
        cost_estimate=pl.CostEstimate(
            flops=2 * rows * model * width * nsq, bytes_accessed=4 * rows * width * nsq, transcendentals=0
        ),
        name="project",
    )(values, weights)


def unpack_kernel(hw, one, two, a_ref, b_ref, out_ref, gate_ref, up_ref, down_ref):
    a, b = a_ref[...].astype(F32), b_ref[...].astype(F32)
    out_ref[...] = b[:, :hw].T
    gate_ref[0:one, :] = a[:, :one].T
    gate_ref[one:, :] = b[:, hw : hw + two].T
    up_ref[0:one, :] = a[:, one : 2 * one].T
    up_ref[one:, :] = b[:, hw + two : hw + 2 * two].T
    down_ref[0:one, :] = a[:, 2 * one : 3 * one].T
    down_ref[one:, :] = b[:, hw + 2 * two : hw + 3 * two].T


def unpack(own_a, own_b, hw, units):
    one, two = unit_halves(units)
    rows = own_a.shape[0]
    shapes = [(hw, rows), (units, rows), (units, rows), (units, rows)]
    out, gate, up, down = pl.pallas_call(
        functools.partial(unpack_kernel, hw, one, two),
        out_shape=[jax.ShapeDtypeStruct(shape, F32) for shape in shapes],
        name="unpack",
    )(own_a, own_b)
    return out, gate.T, up.T, down


def unpack_mix_kernel(lay, nrates, own_ref, q_ref, k_ref, v_ref, r_ref, g_ref):
    own = own_ref[...].astype(F32)
    q_ref[...] = own[:, lay.q : lay.k]
    k_ref[...] = own[:, lay.k : lay.v]
    v_ref[...] = own[:, lay.v : lay.g]
    r_ref[...] = own[:, lay.r : lay.r + nrates]
    g_ref[...] = own[:, lay.g : lay.r]


def unpack_mix(own, lay, nrates):
    rows = own.shape[0]
    widths = (lay.k - lay.q, lay.v - lay.k, lay.g - lay.v, nrates, lay.r - lay.g)
    return pl.pallas_call(
        functools.partial(unpack_mix_kernel, lay, nrates),
        out_shape=[jax.ShapeDtypeStruct((rows, width), F32) for width in widths],
        name="unpack_mix",
    )(own)
STEP = 4


def rms_parts(values):
    scale = lax.rsqrt(jnp.mean(values * values, axis=-1, keepdims=True) + EPS)
    return values * scale, scale


def bits(axis):
    return [1 << k for k in range((lax.axis_size(axis) - 1).bit_length())]


def trade(values, axis, bit):
    return lax.ppermute(values, axis, [(i, i ^ bit) for i in range(lax.axis_size(axis))])


def everyone(values):
    for axis in ("core", "dz", "sq", "sub"):
        for bit in bits(axis):
            values = values + trade(values, axis, bit)
    return values


def plus(left, right):
    return (left.astype(F32) + right.astype(F32)).astype(BF)


def column_step(values, k):
    rows, width = values.shape
    mine = (lax.axis_index("dz") >> k) & 1
    blocks = values.reshape(-1, 2, rows // (lax.axis_size("dz") >> k), width)
    part = lambda i: lax.dynamic_index_in_dim(blocks, i, 1, keepdims=False).reshape(-1, width)
    return plus(part(mine), trade(part(1 - mine), "dz", 1 << k))


def swap(values, which, parts):
    return lax.ppermute(values, "sub", [(i, i ^ which) for i in range(parts)])


def per_device(
    tokens, lengths, out_grad, ln1_gain, ln2_gain, onorm_gain, a_log, dt_bias,
    w_query, w_key, w_value, w_rates, w_outgate, w_out, w_gate, w_up, w_down,
):
    nsq, parts = lax.axis_size("sq"), lax.axis_size("sub")
    which_seq, place = lax.axis_index("sq"), lax.axis_index("sub")
    count = nsq * parts
    tok_dev, model = tokens.shape
    heads = a_log.shape[0] // count
    lay = Layout(heads)
    units = w_gate.shape[1]
    hw = heads * HEAD
    place_arr = place.astype(jnp.int32).reshape(1)

    mix_shard = pack_mix(lay, w_query, w_key, w_value, w_rates, w_outgate)
    ff_shards = pack(w_out, w_gate, w_up, w_down)
    w_mix = lax.all_gather(mix_shard, ("sq", "dz", "core"), axis=0, tiled=True)
    w_mix = w_mix.reshape(nsq, model, lay.width)
    walls = [
        lax.all_gather(shard, ("sq", "sub", "dz", "core"), axis=0, tiled=True).reshape(count, model, -1)
        for shard in ff_shards
    ]
    one, two = unit_halves(units)

    resid_in = tokens.astype(F32)
    normed_one, scale_one = rms_parts(resid_in)
    first = (normed_one * ln1_gain).astype(BF)
    first_seq = jnp.concatenate([first] + [swap(first, r, parts) for r in range(1, parts)], axis=0)

    pre = project(first_seq, w_mix)
    hpos = [(s * parts + place) * heads for s in range(nsq)]
    lanes = np.stack([8 * (c * nsq + s) + 3 * np.arange(heads) + 2 for c in range(STEP) for s in range(nsq)])

    def spread(values):
        mine = jnp.stack([lax.dynamic_slice_in_dim(values, hpos[s], heads) for s in range(nsq)])
        return jnp.zeros((128,), F32).at[lanes.ravel()].set(jnp.tile(mine.ravel(), STEP))

    params = jnp.stack([spread(-jnp.exp(a_log)), spread(dt_bias)])
    gain = onorm_gain.reshape(1, HEAD)
    mixed, *kept = mixer_forward(place_arr, parts, pre, params, gain, heads, STEP)

    got = [mixed] + [swap(mixed[:, r * tok_dev : (r + 1) * tok_dev], r, parts) for r in range(1, parts)]

    limit = jnp.sum(jnp.where(jnp.arange(nsq) == which_seq, lengths, 0)).astype(jnp.int32)
    scalars = jnp.stack([place.astype(jnp.int32), limit, lax.axis_index("core").astype(jnp.int32)])
    block = w_gate.shape[0]
    middle, second, grad_low = join(
        scalars, got, tokens, out_grad, walls[0], ln2_gain.reshape(1, model), parts, nsq, hw
    )
    def chips(pair):
        total = plus(pair[0], trade(pair[1], "core", 1))
        return total.reshape(count * model // 2, -1)

    def plane(values):
        return lax.psum_scatter(values, ("sq", "sub"), scatter_dimension=0, tiled=True)

    mlp_a, sg_a, *grads_a = feed_forward(
        scalars, second, grad_low, walls[0], hw, rounded(3 * one), one, block
    )
    grads_a, wall_b = lax.optimization_barrier((chips(grads_a), walls[1]))
    grads_a = plane(grads_a)
    mlp_b, sg_b, *acts_b = feed_forward_rest(second, grad_low, wall_b, two)
    block_out, middle_grad, middle_low, ln2_grad, *back = split(
        scalars, middle, (mlp_a, mlp_b), (sg_a, sg_b), grad_low, walls[0],
        ln2_gain.reshape(1, model), parts, nsq, hw,
    )
    arrived = [swap(back[r], r, parts) for r in range(1, parts)]
    grads_b = rest_grad(
        scalars, second, grad_low, middle_low, *acts_b, got, hw + rounded(3 * two), parts, nsq, hw, block
    )
    arrived, grads_b = lax.optimization_barrier((arrived, grads_b))
    dmixed = jnp.concatenate([back[0], *arrived], axis=1)
    dmixed, grads_b = lax.optimization_barrier((dmixed, chips(grads_b)))
    grads_b = plane(grads_b)
    steps = dmixed.shape[1] // CT // STEP
    head_steps = steps * 3 // 4
    dpre = (jnp.zeros((nsq * heads, HEAD, HEAD), F32), jnp.zeros((8, 128), F32))
    back_args = (place_arr, parts, pre, params, gain, *kept, dmixed, heads, STEP)
    *dpre, carry, small = mixer_backward(*back_args, 0, head_steps, dpre)
    carry, grads_b, grads_a = lax.optimization_barrier((carry, grads_b, grads_a))
    own_a = lax.psum_scatter(grads_a, "dz", scatter_dimension=0, tiled=True)
    grads_b = column_step(grads_b, 0)
    *dpre, carry, small = mixer_backward(*back_args, head_steps, steps - head_steps, (carry, small, *dpre))

    def back_rows(values, r):
        rows = slice(r * tok_dev, (r + 1) * tok_dev)
        total = dot_nt(values[0][rows], w_mix[0])
        for s in range(1, nsq):
            total = total + dot_nt(values[s][rows], w_mix[s])
        return total, jnp.sum(total * first_seq[rows].astype(F32), axis=0)

    mix_grads = jnp.concatenate([dot_tn(first_seq, dpre[s]).astype(BF) for s in range(nsq)], axis=0)
    dpre, mix_grads, grads_b = lax.optimization_barrier((dpre, mix_grads, grads_b))
    own_b = grads_b
    for k in range(1, len(bits("dz"))):
        own_b = column_step(own_b, k)
    own_out, own_gate, own_up, own_down = unpack(own_a, own_b, hw, units)
    mix_own = lax.psum_scatter(mix_grads, ("sq", "dz", "core"), scatter_dimension=0, tiled=True)
    leaving = [back_rows(dpre, r) for r in range(1, parts)]
    arriving = [swap(leaving[r - 1][0].astype(BF), r, parts) for r in range(1, parts)]
    first_grad, ln1_grad = back_rows(dpre, 0)
    for r in range(1, parts):
        ln1_grad = ln1_grad + leaving[r - 1][1]
    ln1_grad = ln1_grad / ln1_gain
    first_grad, ln1_grad = lax.optimization_barrier((first_grad, ln1_grad))
    for r in range(1, parts):
        first_grad = first_grad + arriving[r - 1].astype(F32)
    scaled = first_grad * ln1_gain
    input_back = scale_one * (scaled - normed_one * jnp.mean(scaled * normed_one, axis=-1, keepdims=True))
    tokens_grad = (middle_grad + input_back).astype(BF)

    def gather_heads(row):
        mine = jnp.sum(row[lanes].reshape(STEP, nsq, heads), axis=0)
        full = jnp.zeros(a_log.shape, F32)
        for s in range(nsq):
            full = lax.dynamic_update_slice_in_dim(full, mine[s], hpos[s], 0)
        return full

    a_grad, dt_grad = gather_heads(small[2]), gather_heads(small[1])
    total = everyone(jnp.concatenate([ln1_grad, ln2_grad[0], small[0], a_grad, dt_grad]))
    marks = np.cumsum([0, model, model, HEAD, a_log.shape[0], a_log.shape[0]])
    return (
        block_out, tokens_grad, *[total[i:j] for i, j in zip(marks[:-1], marks[1:])],
        *unpack_mix(mix_own, lay, w_rates.shape[1]),
        own_out, own_gate, own_up, own_down,
    )


def solution(mesh):
    dp, tensor = mesh.shape["dp"], mesh.shape["tensor"]

    def run(*args):
        nsq = args[1].shape[0] // dp
        split = Mesh(
            mesh.devices.reshape(dp // 2, 2, nsq, tensor // nsq), ("dz", "core", "sq", "sub")
        )
        rows = P(("dz", "core", "sq", "sub"), None)
        down = P(("dz", "core"), ("sq", "sub"))
        across = P(("sq", "sub"), ("dz", "core"))
        in_specs = (rows, P(("dz", "core")), rows) + (P(),) * 5 + (down,) * 5 + (across, down, down, across)
        out_specs = (rows, rows) + (P(),) * 5 + (down,) * 5 + (across, down, down, across)
        return jax.shard_map(
            per_device, mesh=split, in_specs=in_specs, out_specs=out_specs, check_vma=False
        )(*args)

    return run
```

```python
import functools
import jax
import jax.numpy as jnp
import numpy as np
from jax import lax
from jax.experimental import pallas as pl
from jax.experimental.pallas import tpu as pltpu
from jax.sharding import Mesh
from jax.sharding import PartitionSpec as P

HEAD = 128
NH = 2
CT = 64
ROWS = CT * NH
EPS = 1e-06
HIGH = lax.Precision.HIGHEST
BF = jnp.bfloat16
F32 = jnp.float32


def dot_nn(left, right):
    return jnp.dot(left, right, preferred_element_type=F32)


def dot_nt(left, right):
    return lax.dot_general(left, right, (((1,), (1,)), ((), ())), preferred_element_type=F32)


def dot_tn(left, right):
    return lax.dot_general(left, right, (((0,), (0,)), ((), ())), preferred_element_type=F32)


def mixer_tables():
    row = np.arange(ROWS)
    tok, step = row % CT, row // CT
    order = tok * NH + step
    later = order[:, None] > order[None, :]
    barred = np.where(later, 0.0, -1e30).astype(np.float32)
    levels = []
    for size in (1, 4, 16):
        near = (tok[:, None] // (4 * size)) == (tok[None, :] // (4 * size))
        apart = (tok[:, None] // size) != (tok[None, :] // size)
        levels.append((near & apart).astype(np.float32))
    own = ((tok[:, None] == tok[None, :]) & later).astype(np.float32)
    eye = np.eye(ROWS, dtype=np.float32)
    read = np.zeros((CT, ROWS), np.float32)
    read[np.arange(CT), CT + np.arange(CT)] = 1.0
    sums = (np.arange(CT)[:, None] <= tok[None, :]).astype(np.float32)
    square = np.stack([barred, eye, own] + levels)
    thin = np.stack([read, sums])
    return square, thin, np.concatenate([sums] * 3, axis=0)


def sigm(values):
    return jax.nn.sigmoid(values)


class Layout:
    def __init__(self, heads):
        self.q = 0
        self.k = heads * HEAD
        self.v = self.k + heads * NH * HEAD
        self.g = self.v + heads * NH * HEAD
        self.r = self.g + heads * HEAD
        self.width = self.r + 128


def piece(refs, s, c, start):
    return refs[s][c * CT : (c + 1) * CT, start : start + HEAD]


def unit_silu(raw):
    sig = sigm(raw)
    act = raw * sig
    norm = lax.rsqrt(jnp.sum(act * act, axis=-1, keepdims=True) + EPS)
    return act * norm, norm, sig


def thirds(values):
    high = values.astype(BF)
    rest = values - high.astype(F32)
    middle = rest.astype(BF)
    return high, middle, (rest - middle.astype(F32)).astype(BF)


def rates_of(pre_ref, par_ref, sums_ref, nb, nsq, lay):
    raw = None
    for c in range(nb):
        for s in range(nsq):
            here = pre_ref[s][c * CT : (c + 1) * CT, lay.r : lay.r + 128]
            if c + s > 0:
                here = pltpu.roll(here, 8 * (c * nsq + s), axis=1)
            raw = here if raw is None else raw + here
    shifted = raw + par_ref[1:2, :]
    soft = jnp.maximum(shifted, 0.0) + jnp.log1p(jnp.exp(-jnp.abs(shifted)))
    decay = par_ref[0:1, :] * soft
    stacked = jnp.concatenate(thirds(decay), axis=0)
    sums = sums_ref[...]
    return sigm(raw), shifted, decay, dot_tn(sums, stacked), dot_tn(stacked, sums)


def chunk_parts(pre_ref, s, h, c, nsq, lay, betas, cum_col, cum_row, square_ref):
    query, nq, sq = unit_silu(piece(pre_ref, s, c, lay.q + h * HEAD))
    key0, nk0, sk0 = unit_silu(piece(pre_ref, s, c, lay.k + (2 * h) * HEAD))
    key1, nk1, sk1 = unit_silu(piece(pre_ref, s, c, lay.k + (2 * h + 1) * HEAD))
    keys = jnp.concatenate([key0, key1], axis=0)
    base = 8 * (c * nsq + s) + 3 * h
    wide = lambda column: jnp.broadcast_to(column, (CT, HEAD))
    beta = jnp.concatenate([wide(betas[:, base : base + 1]), wide(betas[:, base + 1 : base + 2])], axis=0)
    scaled = keys * beta
    g = wide(cum_col[:CT, base + 2 : base + 3])
    grow = cum_row[base + 2 : base + 3, :]
    weights = jnp.exp(jnp.concatenate([g, g], axis=0) - grow + square_ref[0])
    tail = g[CT - 1 : CT, :]
    grown, left = jnp.exp(g), jnp.exp(tail - g)
    return dict(
        query=query, keys=keys, beta=beta, scaled=scaled, weights=weights, grown=jnp.concatenate([grown, grown], axis=0),
        left=jnp.concatenate([left, left], axis=0), tail=jnp.exp(tail), nq=nq, sq=sq, nk=(nk0, nk1), sk=(sk0, sk1),
    )


def forward_kernel(lay, nsq, heads, nb, _, *refs):
    pre_ref = refs[:nsq]
    par_ref, gain_ref, square_ref, thin_ref, sums_ref = refs[nsq : nsq + 5]
    mixed_ref, tinv_ref, wk_ref, state_ref, delta_ref, o_ref, carry = refs[nsq + 5 :]

    @pl.when(pl.program_id(0) == 0)
    def _():
        carry[...] = jnp.zeros_like(carry)

    which = [(c, s, h) for c in range(nb) for s in range(nsq) for h in range(heads)]
    betas, _, _, cum_col, cum_row = rates_of(pre_ref, par_ref, sums_ref, nb, nsq, lay)
    parts = {}
    for c, s, h in which:
        parts[c, s, h] = chunk_parts(pre_ref, s, h, c, nsq, lay, betas, cum_col, cum_row, square_ref)
    lam, scores = {}, {}
    for key in which:
        p = parts[key]
        keys_low, scaled_low, query_low = p["keys"].astype(BF), p["scaled"].astype(BF), p["query"].astype(BF)
        both = dot_nt(jnp.concatenate([keys_low, query_low], axis=0), scaled_low)
        lam[key] = both[:ROWS] * p["weights"]
        scores[key] = (both[ROWS:] * (p["weights"][CT:] + thin_ref[0])).astype(BF)
    tinv = {key: square_ref[1] - lam[key] * square_ref[2] for key in which}
    for level in range(3):
        low = {key: tinv[key].astype(BF) for key in which}
        step = {key: dot_nn(low[key], (lam[key] * square_ref[3 + level]).astype(BF)).astype(BF) for key in which}
        twice = {key: dot_nn(step[key], step[key]).astype(BF) for key in which}
        half = {key: tinv[key] - dot_nn(step[key], low[key]) for key in which}
        tinv = {key: half[key] + dot_nn(twice[key], half[key].astype(BF)) for key in which}
    chains = [(s, h) for s in range(nsq) for h in range(heads)]
    mixed_in = {}
    for key in which:
        c, s, h = key
        p = parts[key]
        t_low = tinv[key].astype(BF)
        tinv_ref[c, s * heads + h] = t_low
        raw0 = piece(pre_ref, s, c, lay.v + (2 * h) * HEAD)
        raw1 = piece(pre_ref, s, c, lay.v + (2 * h + 1) * HEAD)
        values = jnp.concatenate([raw0 * sigm(raw0), raw1 * sigm(raw1)], axis=0)
        kg = p["keys"] * p["grown"]
        solved = dot_nn(t_low, jnp.concatenate([values, kg], axis=1).astype(BF))
        wk = solved[:, HEAD:].astype(BF)
        wk_ref[c, s * heads + h] = wk
        qg = (p["query"] * p["grown"][:CT]).astype(BF)
        mixed_in[key] = (solved[:, :HEAD], jnp.concatenate([wk, qg], axis=0), (p["scaled"] * p["left"]).astype(BF))
    state = {k: carry[k[0] * heads + k[1]] for k in chains}
    read, deltas = {}, {}
    for c in range(nb):
        low = {k: state[k].astype(BF) for k in chains}
        for s, h in chains:
            state_ref[c, s * heads + h] = low[s, h]
        seen = {k: dot_nn(mixed_in[(c,) + k][1], low[k]) for k in chains}
        delta = {k: (mixed_in[(c,) + k][0] - seen[k][:ROWS]).astype(BF) for k in chains}
        state = {k: parts[(c,) + k]["tail"] * state[k] + dot_tn(mixed_in[(c,) + k][2], delta[k]) for k in chains}
        for k in chains:
            read[(c,) + k] = seen[k][ROWS:]
            deltas[(c,) + k] = delta[k]
    for s, h in chains:
        carry[s * heads + h] = state[s, h]
    for key in which:
        c, s, h = key
        delta_ref[c, s * heads + h] = deltas[key]
        out = read[key] + dot_nn(scores[key], deltas[key])
        o_ref[s, c * CT : (c + 1) * CT, h * HEAD : (h + 1) * HEAD] = out
        scale = lax.rsqrt(jnp.mean(out * out, axis=-1, keepdims=True) + EPS)
        gate = piece(pre_ref, s, c, lay.g + h * HEAD)
        mixed = out * scale * gain_ref[0:1, :] * (gate * sigm(gate))
        mixed_ref[s, c * CT : (c + 1) * CT, h * HEAD : (h + 1) * HEAD] = mixed.astype(BF)


def silu_slope(raw, sig):
    return sig * (1.0 + raw * (1.0 - sig))


def backward_kernel(lay, nsq, heads, nb, _, *refs):
    pre_ref = refs[:nsq]
    par_ref, gain_ref, square_ref, thin_ref, sums_ref = refs[nsq : nsq + 5]
    tinv_ref, wk_ref, state_ref, delta_ref, o_ref, dm_ref = refs[nsq + 5 : nsq + 11]
    carry_in, small_in = refs[nsq + 11 : nsq + 13]
    dpre_ref = refs[-nsq - 3 : -3]
    carry, acc, carried = refs[-3:]

    @pl.when(pl.program_id(0) == 0)
    def _():
        carried[...] = carry_in[...]
        acc[...] = small_in[...]

    lane = lax.broadcasted_iota(jnp.int32, (CT, 128), 1)
    sub8 = lax.broadcasted_iota(jnp.int32, (8, 128), 0)
    chains = [(s, h) for s in range(nsq) for h in range(heads)]
    spans = [slice(c * CT, (c + 1) * CT) for c in range(nb)]
    gain = gain_ref[0:1, :]
    gain_sum = jnp.zeros((1, HEAD), F32)
    work = {}
    betas, shifted, decay, cum_col, cum_row = rates_of(pre_ref, par_ref, sums_ref, nb, nsq, lay)
    for c in reversed(range(nb)):
        for s, h in chains:
            cols = slice(h * HEAD, (h + 1) * HEAD)
            p = chunk_parts(pre_ref, s, h, c, nsq, lay, betas, cum_col, cum_row, square_ref)
            out = o_ref[s, spans[c], cols]
            dm = dm_ref[s, spans[c], cols].astype(F32)
            graw = piece(pre_ref, s, c, lay.g + h * HEAD)
            gsig = sigm(graw)
            gate = graw * gsig
            scale = lax.rsqrt(jnp.mean(out * out, axis=-1, keepdims=True) + EPS)
            normed = out * scale
            dpre_ref[s][spans[c], lay.g + h * HEAD : lay.g + (h + 1) * HEAD] = (
                dm * normed * gain * (gsig + gate * (1.0 - gsig))
            ).astype(BF)
            dn = dm * gate
            gain_sum = gain_sum + jnp.sum(dn * normed, axis=0, keepdims=True)
            scaled_dn = dn * gain
            dout = scale * (scaled_dn - normed * jnp.mean(scaled_dn * normed, axis=-1, keepdims=True))
            dout_low = dout.astype(BF)
            keys_low, query_low = p["keys"].astype(BF), p["query"].astype(BF)
            scaled_low = p["scaled"].astype(BF)
            both_low = jnp.concatenate([keys_low, query_low], axis=0)
            w_all = jnp.concatenate([p["weights"], p["weights"][CT:] + thin_ref[0]], axis=0)
            weighted = dot_nt(both_low, scaled_low) * w_all
            p["w_all"], p["weighted"], p["both_low"], p["scaled_low"] = w_all, weighted, both_low, scaled_low
            p["dout_low"] = dout_low
            p["from_out"] = dot_tn(weighted[ROWS:].astype(BF), dout_low)
            qg = (p["query"] * p["grown"][:CT]).astype(BF)
            p["to_state"] = dot_tn(qg, dout_low)
            p["kout"] = (p["scaled"] * p["left"]).astype(BF)
            work[c, s, h] = p
    dstate = {k: carried[k[0] * heads + k[1]] for k in chains}
    for c in reversed(range(nb)):
        low = {k: dstate[k].astype(BF) for k in chains}
        ddelta = {
            k: (work[(c,) + k]["from_out"] + dot_nn(work[(c,) + k]["kout"], low[k])).astype(BF) for k in chains
        }
        for k in chains:
            p = work[(c,) + k]
            p["ddelta"], p["dstate"], p["dstate_low"] = ddelta[k], dstate[k], low[k]
        dstate = {
            k: work[(c,) + k]["tail"] * dstate[k]
            + work[(c,) + k]["to_state"]
            - dot_tn(wk_ref[c, k[0] * heads + k[1]], ddelta[k])
            for k in chains
        }
    for s, h in chains:
        carried[s * heads + h] = dstate[s, h]
        carry[s * heads + h] = dstate[s, h]
    read_all = jnp.zeros((CT, 128), F32)
    dtail_all = jnp.zeros((1, 128), F32)
    dbeta_all = jnp.zeros((CT, 128), F32)
    col_rows = {}
    for c in reversed(range(nb)):
        span = spans[c]
        for s in range(nsq):
            dcol_all = jnp.zeros((8, 128), F32)
            for h in range(heads):
                at = s * heads + h
                p = work[c, s, h]
                dpv = dot_tn(tinv_ref[c, at], p["ddelta"])
                joint = jnp.concatenate([(-dpv).astype(BF), p["dout_low"]], axis=0)
                delta = delta_ref[c, at]
                state_low = state_ref[c, at]
                inner = dot_nt(joint, delta)
                inner_low = (inner * p["w_all"]).astype(BF)
                pairs = inner * p["weighted"]
                grown_all = jnp.concatenate([p["grown"], p["grown"][:CT]], axis=0)
                base = 8 * (c * nsq + s) + 3 * h
                entered = grown_all * dot_nt(joint, state_low)
                left_out = p["left"] * dot_nt(delta, p["dstate_low"])
                direct = dot_nn(inner_low, p["scaled_low"]) + entered
                dscaled = dot_tn(inner_low, p["both_low"]) + left_out
                both_rows = jnp.concatenate([p["keys"], p["query"]], axis=0)
                row_part = jnp.sum(pairs + both_rows * entered, axis=-1, keepdims=True)
                col_part = jnp.sum(pairs, axis=0, keepdims=True)
                out_part = jnp.sum(p["scaled"] * left_out, axis=-1, keepdims=True)
                dtail = p["tail"] * jnp.sum(
                    jnp.sum(state_low.astype(F32) * p["dstate"], axis=0, keepdims=True), axis=1, keepdims=True
                ) + jnp.sum(out_part, axis=0, keepdims=True)
                dkeys, dquery = direct[:ROWS], direct[ROWS:]
                dbeta = jnp.sum(p["keys"] * dscaled, axis=-1, keepdims=True)
                kdot = jnp.sum(p["keys"] * dkeys, axis=-1, keepdims=True)
                qdot = jnp.sum(p["query"] * dquery, axis=-1, keepdims=True)
                kfull = kdot + p["beta"] * dbeta
                tokens = row_part[:CT] + row_part[CT:ROWS] + row_part[ROWS:] - out_part[:CT] - out_part[CT:]
                read_all = jnp.where(lane == base + 2, tokens, read_all)
                dcol_all = jnp.where(sub8 == 3 * h + 2, col_part, dcol_all)
                dtail_all = jnp.where(lane[0:1] == base + 2, dtail, dtail_all)
                dbeta_all = jnp.where(lane == base, dbeta[:CT], dbeta_all)
                dbeta_all = jnp.where(lane == base + 1, dbeta[CT:], dbeta_all)
                dk = dkeys + p["beta"] * dscaled
                dk = dk - p["keys"] * kfull
                for j in range(NH):
                    part = slice(j * CT, (j + 1) * CT)
                    start = lay.k + (2 * h + j) * HEAD
                    kraw = piece(pre_ref, s, c, start)
                    dpre_ref[s][span, start : start + HEAD] = (
                        dk[part] * p["nk"][j] * silu_slope(kraw, p["sk"][j])
                    ).astype(BF)
                    start = lay.v + (2 * h + j) * HEAD
                    vraw = piece(pre_ref, s, c, start)
                    dpre_ref[s][span, start : start + HEAD] = (
                        dpv[part] * silu_slope(vraw, sigm(vraw))
                    ).astype(BF)
                start = lay.q + h * HEAD
                qraw = piece(pre_ref, s, c, start)
                dq = (dquery - p["query"] * qdot) * p["nq"]
                dpre_ref[s][span, start : start + HEAD] = (dq * silu_slope(qraw, p["sq"])).astype(BF)
            col_rows[c * nsq + s] = dcol_all
    sums = sums_ref[0:CT, :]
    reads = jnp.concatenate(thirds(read_all), axis=0)
    padding = [jnp.zeros((128 - 8 * len(col_rows), 128), F32)] if len(col_rows) < 16 else []
    columns = jnp.concatenate([col_rows[k] for k in range(len(col_rows))] + padding, axis=0)
    ddecay = dot_nn(jnp.concatenate([sums[:, :CT]] * 3, axis=1), reads) + dtail_all
    for term in thirds(columns):
        ddecay = ddecay - dot_nt(sums, term)
    dshift = ddecay * par_ref[0:1, :] * sigm(shifted)
    acc[1:2, :] += jnp.sum(dshift, axis=0, keepdims=True)
    acc[2:3, :] += jnp.sum(ddecay * decay, axis=0, keepdims=True)
    drates = dshift + dbeta_all * betas * (1.0 - betas)
    for c in range(nb):
        for s in range(nsq):
            shift = 8 * (c * nsq + s)
            here = pltpu.roll(drates, 128 - shift, axis=1) if shift else drates
            dpre_ref[s][spans[c], lay.r : lay.r + 128] = jnp.where(lane < 8, here, 0.0).astype(BF)
    acc[0:1, :] += gain_sum


def shared_specs(square, thin, sums):
    return [
        pl.BlockSpec((2, 128), lambda i, _: (0, 0)),
        pl.BlockSpec((1, HEAD), lambda i, _: (0, 0)),
        pl.BlockSpec(square.shape, lambda i, _: (0, 0, 0)),
        pl.BlockSpec(thin.shape, lambda i, _: (0, 0, 0)),
        pl.BlockSpec(sums.shape, lambda i, _: (0, 0)),
    ]


def part_chunk(step, place, per_part):
    return ((step // per_part) ^ place[0]) * per_part + step % per_part


def mixer_forward(place, parts, pre, params, gain, heads, nb=2):
    nsq, (length, width) = len(pre), pre[0].shape
    lay = Layout(heads)
    square, thin, sums3 = mixer_tables()
    nchunk = length // CT
    chains = nsq * heads
    span = nb * CT
    per_part = nchunk // nb // parts
    big = lambda: pl.BlockSpec((nb, chains, ROWS, HEAD), lambda i, _: (i, 0, 0, 0))
    rows = lambda w: pl.BlockSpec((nsq, span, w), lambda i, place: (0, part_chunk(i, place, per_part), 0))
    wide = lambda: pl.BlockSpec((span, width), lambda i, place: (part_chunk(i, place, per_part), 0))
    return pl.pallas_call(
        functools.partial(forward_kernel, lay, nsq, heads, nb),
        grid_spec=pltpu.PrefetchScalarGridSpec(
            num_scalar_prefetch=1,
            grid=(nchunk // nb,),
            in_specs=[wide() for _ in pre] + shared_specs(square, thin, sums3),
            out_specs=[rows(heads * HEAD), big(), big(), big(), big(), rows(heads * HEAD)],
            scratch_shapes=[pltpu.VMEM((chains, HEAD, HEAD), F32)],
        ),
        out_shape=[
            jax.ShapeDtypeStruct((nsq, length, heads * HEAD), BF),
            jax.ShapeDtypeStruct((nchunk, chains, ROWS, ROWS), BF),
            jax.ShapeDtypeStruct((nchunk, chains, ROWS, HEAD), BF),
            jax.ShapeDtypeStruct((nchunk, chains, HEAD, HEAD), BF),
            jax.ShapeDtypeStruct((nchunk, chains, ROWS, HEAD), BF),
            jax.ShapeDtypeStruct((nsq, length, heads * HEAD), F32),
        ],
        compiler_params=pltpu.CompilerParams(vmem_limit_bytes=56 * 1024 * 1024),
        cost_estimate=pl.CostEstimate(
            flops=nchunk * chains * 20 * 2 * ROWS**3,
            bytes_accessed=nsq * length * (4 * width + 6 * heads * HEAD) + nchunk * chains * 6 * ROWS**2,
            transcendentals=0,
        ),
        name="mixer_forward",
    )(place, *pre, params, gain, jnp.asarray(square), jnp.asarray(thin), jnp.asarray(sums3, BF))


def mixer_backward(place, parts, pre, params, gain, tinv, wks, states, deltas, outs, dmixed, heads, nb, skip, steps, earlier):
    nsq, (length, width) = len(pre), pre[0].shape
    lay = Layout(heads)
    square, thin, sums3 = mixer_tables()
    nchunk = length // CT
    chains = nsq * heads
    span = nb * CT
    per_part = nchunk // nb // parts
    last = nchunk // nb - 1 - skip
    big = lambda: pl.BlockSpec((nb, chains, ROWS, HEAD), lambda i, _: (last - i, 0, 0, 0))
    rows = lambda w: pl.BlockSpec(
        (nsq, span, w), lambda i, place: (0, part_chunk(last - i, place, per_part), 0)
    )
    wide = lambda: pl.BlockSpec((span, width), lambda i, place: (part_chunk(last - i, place, per_part), 0))
    held = pl.BlockSpec((chains, HEAD, HEAD), lambda i, _: (0, 0, 0))
    sums = pl.BlockSpec((8, 128), lambda i, _: (0, 0))
    carry, small, *done = earlier
    first_done = nsq + 14
    return pl.pallas_call(
        functools.partial(backward_kernel, lay, nsq, heads, nb),
        grid_spec=pltpu.PrefetchScalarGridSpec(
            num_scalar_prefetch=1,
            grid=(steps,),
            in_specs=[wide() for _ in pre]
            + shared_specs(square, thin, sums3)
            + [big(), big(), big(), big(), rows(heads * HEAD), rows(heads * HEAD), held, sums]
            + [pl.BlockSpec(memory_space=pl.ANY) for _ in done],
            out_specs=[wide() for _ in pre] + [held, sums],
            scratch_shapes=[pltpu.VMEM((chains, HEAD, HEAD), F32)],
        ),
        out_shape=[jax.ShapeDtypeStruct((length, width), BF) for _ in pre]
        + [jax.ShapeDtypeStruct((chains, HEAD, HEAD), F32), jax.ShapeDtypeStruct((8, 128), F32)],
        input_output_aliases={first_done + k: k for k in range(len(done))},
        compiler_params=pltpu.CompilerParams(vmem_limit_bytes=56 * 1024 * 1024),
        cost_estimate=pl.CostEstimate(
            flops=steps * nb * chains * 26 * 2 * ROWS**3,
            bytes_accessed=(nsq * length * (6 * width + 6 * heads * HEAD) + nchunk * chains * 8 * ROWS**2) * steps * nb // nchunk,
            transcendentals=0,
        ),
        name="mixer_backward",
    )(
        place, *pre, params, gain, jnp.asarray(square), jnp.asarray(thin), jnp.asarray(sums3, BF),
        tinv, wks, states, deltas, outs, dmixed, carry, small, *done,
    )


TILE = 256


def token_mask(place, limit, tile, rows, base):
    position = place * rows + base + lax.broadcasted_iota(jnp.int32, (tile, 1), 0)
    return position < limit


def join_kernel(parts, nsq, tok, scalars, *refs):
    mixed_refs = refs[:parts]
    x_ref, og_ref, wout_ref, gain_ref = refs[parts : parts + 4]
    middle_ref, second_ref, grad_ref = refs[parts + 4 :]
    place, limit = scalars[0], scalars[1]
    total = x_ref[...].astype(F32)
    for r in range(parts):
        for s in range(nsq):
            total = total + dot_nt(mixed_refs[r][s], wout_ref[s * parts + (place ^ r)])
    middle_ref[...] = total
    scale = lax.rsqrt(jnp.mean(total * total, axis=-1, keepdims=True) + EPS)
    second_ref[...] = (total * scale * gain_ref[...]).astype(BF)
    keep = token_mask(place, limit, x_ref.shape[0], tok, pl.program_id(0) * x_ref.shape[0])
    grad_ref[...] = jnp.where(keep, og_ref[...].astype(F32), 0.0).astype(BF)


def join(scalars, mixed_parts, x, out_grad, wall, gain, parts, nsq, hw):
    tok, model = x.shape
    count = parts * nsq
    tile = min(TILE, tok)
    row = pl.BlockSpec((tile, model), lambda i, _: (i, 0))
    return pl.pallas_call(
        functools.partial(join_kernel, parts, nsq, tok),
        grid_spec=pltpu.PrefetchScalarGridSpec(
            num_scalar_prefetch=1,
            grid=(tok // tile,),
            in_specs=[pl.BlockSpec((nsq, tile, hw), lambda i, _: (0, i, 0)) for _ in mixed_parts]
            + [row, row, pl.BlockSpec((count, model, hw), lambda i, _: (0, 0, 0)),
               pl.BlockSpec((1, model), lambda i, _: (0, 0))],
            out_specs=[row, row, row],
        ),
        out_shape=[
            jax.ShapeDtypeStruct((tok, model), F32),
            jax.ShapeDtypeStruct((tok, model), BF),
            jax.ShapeDtypeStruct((tok, model), BF),
        ],
        compiler_params=pltpu.CompilerParams(vmem_limit_bytes=40 * 1024 * 1024),
        cost_estimate=pl.CostEstimate(
            flops=2 * tok * model * count * hw, bytes_accessed=14 * tok * model, transcendentals=0
        ),
        name="join",
    )(scalars, *mixed_parts, x, out_grad, wall, gain)


def core_halves(core, block, value):
    count = value.shape[0] // block
    pieces = [value[j * block : (j + 1) * block] for j in range(count)]
    join_all = lambda items: items[0] if len(items) == 1 else jnp.concatenate(items, axis=0)
    even, odd = join_all(pieces[0::2]), join_all(pieces[1::2])
    return jnp.where(core == 0, even, odd), jnp.where(core == 0, odd, even)


def ff_tiles(tile, lead, units, sec_ref, grad_ref, w_ref, mlp_ref, sg_ref, store):
    tok, model = sec_ref.shape
    mid, end = lead + 2 * units, lead + 3 * units

    @pl.when(pl.program_id(0) == 0)
    def _():
        mlp_ref[...] = jnp.zeros_like(mlp_ref)
        sg_ref[...] = jnp.zeros_like(sg_ref)

    for m in range(tok // tile):
        rows = slice(m * tile, (m + 1) * tile)
        pre = dot_nn(sec_ref[rows, :], w_ref[0, :, lead:mid])
        gate_pre, up_pre = pre[:, :units], pre[:, units:]
        hidden_grad = dot_nn(grad_ref[rows, :], w_ref[0, :, mid:end])
        sig = sigm(gate_pre)
        act = gate_pre * sig
        hidden = (act * up_pre).astype(BF)
        gate_low = (hidden_grad * up_pre * (sig + act * (1.0 - sig))).astype(BF)
        up_low = (hidden_grad * act).astype(BF)
        both_low = jnp.concatenate([gate_low, up_low], axis=1)
        store(rows, hidden, both_low)
        mlp_ref[rows, :] += dot_nt(hidden, w_ref[0, :, mid:end])
        sg_ref[rows, :] += dot_nt(both_low, w_ref[0, :, lead:mid])


def weight_tiles(core, block, lead_out, sec_ref, grad_ref, hid, both, keep_ref, send_ref):
    model, units = sec_ref.shape[1], hid.shape[1]
    mid_out, end_out = lead_out + 2 * units, lead_out + 3 * units
    step = min(256, model)
    for k in range(model // step):
        cols = slice(k * step, (k + 1) * step)
        rows = slice(k * step // 2, (k + 1) * step // 2)
        value = core_halves(core, block, dot_tn(sec_ref[:, cols], both[...]))
        keep_ref[0, rows, lead_out:mid_out] = value[0].astype(BF)
        send_ref[0, rows, lead_out:mid_out] = value[1].astype(BF)
        value = core_halves(core, block, dot_tn(grad_ref[:, cols], hid[...]))
        keep_ref[0, rows, mid_out:end_out] = value[0].astype(BF)
        send_ref[0, rows, mid_out:end_out] = value[1].astype(BF)


def ff_kernel(tile, block, lead, units, scalars, sec_ref, grad_ref, w_ref, mlp_ref, sg_ref, keep_ref, send_ref, hid, both):
    def store(rows, hidden, both_low):
        hid[rows, :] = hidden
        both[rows, :] = both_low

    ff_tiles(tile, lead, units, sec_ref, grad_ref, w_ref, mlp_ref, sg_ref, store)
    weight_tiles(scalars[2], block, 0, sec_ref, grad_ref, hid, both, keep_ref, send_ref)


def feed_forward(scalars, second, grad_low, wall, lead, width_out, units, block):
    tok, model = second.shape
    count, _, width = wall.shape
    whole = pl.BlockSpec((tok, model), lambda p, _: (0, 0))
    weight = pl.BlockSpec((1, model, width), lambda p, _: (p, 0, 0))
    half = pl.BlockSpec((1, model // 2, width_out), lambda p, _: (p, 0, 0))
    return pl.pallas_call(
        functools.partial(ff_kernel, min(TILE, tok), block, lead, units),
        grid_spec=pltpu.PrefetchScalarGridSpec(
            num_scalar_prefetch=1,
            grid=(count,),
            in_specs=[whole, whole, weight],
            out_specs=[whole, whole, half, half],
            scratch_shapes=[pltpu.VMEM((tok, units), BF), pltpu.VMEM((tok, 2 * units), BF)],
        ),
        out_shape=[
            jax.ShapeDtypeStruct((tok, model), F32),
            jax.ShapeDtypeStruct((tok, model), F32),
            jax.ShapeDtypeStruct((count, model // 2, width_out), BF),
            jax.ShapeDtypeStruct((count, model // 2, width_out), BF),
        ],
        compiler_params=pltpu.CompilerParams(vmem_limit_bytes=62 * 1024 * 1024),
        cost_estimate=pl.CostEstimate(
            flops=18 * tok * model * units * count,
            bytes_accessed=count * model * width * 4 + 12 * tok * model,
            transcendentals=0,
        ),
        name="feed_forward",
    )(scalars, second, grad_low, wall)


def ff_rest_kernel(tile, units, sec_ref, grad_ref, w_ref, mlp_ref, sg_ref, hid_ref, both_ref):
    def store(rows, hidden, both_low):
        hid_ref[0, rows, :] = hidden
        both_ref[0, rows, :] = both_low

    ff_tiles(tile, 0, units, sec_ref, grad_ref, w_ref, mlp_ref, sg_ref, store)


def feed_forward_rest(second, grad_low, wall, units):
    tok, model = second.shape
    count, _, width = wall.shape
    whole = pl.BlockSpec((tok, model), lambda p: (0, 0))
    part = lambda w: pl.BlockSpec((1, tok, w), lambda p: (p, 0, 0))
    return pl.pallas_call(
        functools.partial(ff_rest_kernel, min(TILE, tok), units),
        grid=(count,),
        in_specs=[whole, whole, pl.BlockSpec((1, model, width), lambda p: (p, 0, 0))],
        out_specs=[whole, whole, part(units), part(2 * units)],
        out_shape=[
            jax.ShapeDtypeStruct((tok, model), F32),
            jax.ShapeDtypeStruct((tok, model), F32),
            jax.ShapeDtypeStruct((count, tok, units), BF),
            jax.ShapeDtypeStruct((count, tok, 2 * units), BF),
        ],
        compiler_params=pltpu.CompilerParams(vmem_limit_bytes=62 * 1024 * 1024),
        cost_estimate=pl.CostEstimate(
            flops=12 * tok * model * units * count,
            bytes_accessed=count * model * width * 2 + 12 * tok * model,
            transcendentals=0,
        ),
        name="feed_forward_rest",
    )(second, grad_low, wall)


def rest_grad_kernel(block, parts, hw, scalars, sec_ref, grad_ref, ml_ref, hid_ref, both_ref, *refs):
    mixed_refs, (keep_ref, send_ref) = refs[:-2], refs[-2:]
    model = sec_ref.shape[1]
    weight_tiles(scalars[2], block, hw, sec_ref, grad_ref, hid_ref.at[0], both_ref.at[0], keep_ref, send_ref)
    wanted = scalars[0] ^ (pl.program_id(0) % parts)
    mixed = mixed_refs[0][0]
    for r in range(1, parts):
        mixed = jnp.where(wanted == r, mixed_refs[r][0], mixed)
    step = min(256, model)
    for k in range(model // step):
        rows = slice(k * step // 2, (k + 1) * step // 2)
        value = core_halves(scalars[2], block, dot_tn(ml_ref[:, k * step : (k + 1) * step], mixed))
        keep_ref[0, rows, 0:hw] = value[0].astype(BF)
        send_ref[0, rows, 0:hw] = value[1].astype(BF)


def rest_grad(scalars, second, grad_low, middle_low, hidden, both, mixed_parts, width_out, parts, nsq, hw, block):
    tok, model = second.shape
    count, _, units = hidden.shape
    whole = pl.BlockSpec((tok, model), lambda p, _: (0, 0))
    part = lambda w: pl.BlockSpec((1, tok, w), lambda p, _: (p, 0, 0))
    half = pl.BlockSpec((1, model // 2, width_out), lambda p, _: (p, 0, 0))
    return pl.pallas_call(
        functools.partial(rest_grad_kernel, block, parts, hw),
        grid_spec=pltpu.PrefetchScalarGridSpec(
            num_scalar_prefetch=1,
            grid=(count,),
            in_specs=[whole, whole, whole, part(units), part(2 * units)]
            + [pl.BlockSpec((1, tok, hw), lambda p, _: (p // parts, 0, 0)) for _ in mixed_parts],
            out_specs=[half, half],
        ),
        out_shape=[jax.ShapeDtypeStruct((count, model // 2, width_out), BF)] * 2,
        compiler_params=pltpu.CompilerParams(vmem_limit_bytes=50 * 1024 * 1024),
        cost_estimate=pl.CostEstimate(
            flops=2 * tok * model * (3 * units + hw) * count,
            bytes_accessed=count * model * width_out * 2 + 6 * tok * model,
            transcendentals=0,
        ),
        name="rest_grad",
    )(scalars, second, grad_low, middle_low, hidden, both, *mixed_parts)


def split_kernel(parts, nsq, tok, scalars, *refs):
    middle_ref, mlp_ref, mlp2_ref, sg_ref, sg2_ref, grad_ref, wout_ref, gain_ref = refs[:8]
    out_ref, mg_ref, ml_ref, ln_ref = refs[8:12]
    back_refs = refs[12:]
    place, limit = scalars[0], scalars[1]
    tile = middle_ref.shape[0]
    middle = middle_ref[...]
    keep = token_mask(place, limit, tile, tok, pl.program_id(0) * tile)
    out_ref[...] = jnp.where(keep, middle + (mlp_ref[...] + mlp2_ref[...]), 0.0).astype(BF)
    scale = lax.rsqrt(jnp.mean(middle * middle, axis=-1, keepdims=True) + EPS)
    normed = middle * scale
    sg = sg_ref[...] + sg2_ref[...]

    @pl.when(pl.program_id(0) == 0)
    def _():
        ln_ref[...] = jnp.zeros_like(ln_ref)

    ln_ref[...] += jnp.sum(sg * normed, axis=0, keepdims=True)
    scaled = sg * gain_ref[...]
    back = scale * (scaled - normed * jnp.mean(scaled * normed, axis=-1, keepdims=True))
    total = grad_ref[...].astype(F32) + back
    mg_ref[...] = total
    low = total.astype(BF)
    ml_ref[...] = low
    for r in range(parts):
        for s in range(nsq):
            back_refs[r][s] = dot_nn(low, wout_ref[s * parts + (place ^ r)]).astype(BF)


def split(scalars, middle, mlps, second_grads, grad_low, wall, gain, parts, nsq, hw):
    tok, model = middle.shape
    count = parts * nsq
    tile = min(TILE, tok)
    row = pl.BlockSpec((tile, model), lambda i, _: (i, 0))
    line = pl.BlockSpec((1, model), lambda i, _: (0, 0))
    return pl.pallas_call(
        functools.partial(split_kernel, parts, nsq, tok),
        grid_spec=pltpu.PrefetchScalarGridSpec(
            num_scalar_prefetch=1,
            grid=(tok // tile,),
            in_specs=[row] * 6 + [pl.BlockSpec((count, model, hw), lambda i, _: (0, 0, 0)), line],
            out_specs=[row, row, row, line]
            + [pl.BlockSpec((nsq, tile, hw), lambda i, _: (0, i, 0)) for _ in range(parts)],
        ),
        out_shape=[
            jax.ShapeDtypeStruct((tok, model), BF),
            jax.ShapeDtypeStruct((tok, model), F32),
            jax.ShapeDtypeStruct((tok, model), BF),
            jax.ShapeDtypeStruct((1, model), F32),
        ]
        + [jax.ShapeDtypeStruct((nsq, tok, hw), BF) for _ in range(parts)],
        compiler_params=pltpu.CompilerParams(vmem_limit_bytes=40 * 1024 * 1024),
        cost_estimate=pl.CostEstimate(
            flops=2 * tok * model * count * hw, bytes_accessed=26 * tok * model, transcendentals=0
        ),
        name="split",
    )(scalars, middle, *mlps, *second_grads, grad_low, wall, gain)


def rounded(size):
    return size + -size % 128


def unit_halves(units):
    first = rounded((units + 1) // 2)
    return first, units - first


def turn(values):
    return values.astype(F32).T.astype(BF)


def pack_mix_kernel(lay, q_ref, k_ref, v_ref, r_ref, g_ref, mix_ref):
    mix_ref[:, lay.q : lay.k] = q_ref[...]
    mix_ref[:, lay.k : lay.v] = k_ref[...]
    mix_ref[:, lay.v : lay.g] = v_ref[...]
    mix_ref[:, lay.g : lay.r] = g_ref[...]
    mix_ref[:, lay.r : lay.width] = jnp.zeros((mix_ref.shape[0], 128), BF)
    mix_ref[:, lay.r : lay.r + r_ref.shape[0]] = turn(r_ref[...])


def pack_mix(lay, w_query, w_key, w_value, w_rates, w_outgate):
    return pl.pallas_call(
        functools.partial(pack_mix_kernel, lay),
        out_shape=jax.ShapeDtypeStruct((w_query.shape[0], lay.width), BF),
        name="pack_mix",
    )(w_query, w_key, w_value, w_rates.T, w_outgate)


def pack_kernel(out_ref, gate_ref, up_ref, down_ref, *all_refs):
    hw, units = out_ref.shape[0], gate_ref.shape[0]
    all_refs[0][:, 0:hw] = turn(out_ref[...])
    whole = [turn(ref[...]) for ref in (gate_ref, up_ref, down_ref)]
    start, lead = 0, hw
    for ref, size in zip(all_refs, unit_halves(units)):
        for k in range(3):
            ref[:, lead + k * size : lead + (k + 1) * size] = whole[k][:, start : start + size]
        end = lead + 3 * size
        if end < ref.shape[1]:
            ref[:, end:] = jnp.zeros((ref.shape[0], ref.shape[1] - end), BF)
        start, lead = start + size, 0


def pack(w_out, w_gate, w_up, w_down):
    rows = w_out.shape[1]
    one, two = unit_halves(w_down.shape[0])
    return pl.pallas_call(
        pack_kernel,
        out_shape=[
            jax.ShapeDtypeStruct((rows, rounded(w_out.shape[0] + 3 * one)), BF),
            jax.ShapeDtypeStruct((rows, rounded(3 * two)), BF),
        ],
        name="pack",
    )(w_out, w_gate.T, w_up.T, w_down)


def project_kernel(x_ref, w_ref, *out_refs):
    step = min(256, x_ref.shape[0])
    for m in range(x_ref.shape[0] // step):
        rows = slice(m * step, (m + 1) * step)
        for s, out_ref in enumerate(out_refs):
            out_ref[rows, :] = dot_nn(x_ref[rows, :], w_ref[s])


def project(values, weights):
    nsq, model, width = weights.shape
    rows = values.shape[0]
    tile = min(512, rows)
    return pl.pallas_call(
        project_kernel,
        grid=(rows // tile,),
        in_specs=[
            pl.BlockSpec((tile, model), lambda i: (i, 0)),
            pl.BlockSpec((nsq, model, width), lambda i: (0, 0, 0)),
        ],
        out_specs=[pl.BlockSpec((tile, width), lambda i: (i, 0))] * nsq,
        out_shape=[jax.ShapeDtypeStruct((rows, width), F32)] * nsq,
        compiler_params=pltpu.CompilerParams(vmem_limit_bytes=50 * 1024 * 1024),
        cost_estimate=pl.CostEstimate(
            flops=2 * rows * model * width * nsq, bytes_accessed=4 * rows * width * nsq, transcendentals=0
        ),
        name="project",
    )(values, weights)


def unpack_kernel(hw, one, two, a_ref, b_ref, out_ref, gate_ref, up_ref, down_ref):
    a, b = a_ref[...].astype(F32), b_ref[...].astype(F32)
    out_ref[...] = b[:, :hw].T
    gate_ref[0:one, :] = a[:, :one].T
    gate_ref[one:, :] = b[:, hw : hw + two].T
    up_ref[0:one, :] = a[:, one : 2 * one].T
    up_ref[one:, :] = b[:, hw + two : hw + 2 * two].T
    down_ref[0:one, :] = a[:, 2 * one : 3 * one].T
    down_ref[one:, :] = b[:, hw + 2 * two : hw + 3 * two].T


def unpack(own_a, own_b, hw, units):
    one, two = unit_halves(units)
    rows = own_a.shape[0]
    shapes = [(hw, rows), (units, rows), (units, rows), (units, rows)]
    out, gate, up, down = pl.pallas_call(
        functools.partial(unpack_kernel, hw, one, two),
        out_shape=[jax.ShapeDtypeStruct(shape, F32) for shape in shapes],
        name="unpack",
    )(own_a, own_b)
    return out, gate.T, up.T, down


def unpack_mix_kernel(lay, nrates, own_ref, q_ref, k_ref, v_ref, r_ref, g_ref):
    own = own_ref[...].astype(F32)
    q_ref[...] = own[:, lay.q : lay.k]
    k_ref[...] = own[:, lay.k : lay.v]
    v_ref[...] = own[:, lay.v : lay.g]
    r_ref[...] = own[:, lay.r : lay.width].T[:nrates]
    g_ref[...] = own[:, lay.g : lay.r]


def unpack_mix(own, lay, nrates):
    rows = own.shape[0]
    widths = (lay.k - lay.q, lay.v - lay.k, lay.g - lay.v, nrates, lay.r - lay.g)
    shapes = [(nrates, rows) if k == 3 else (rows, width) for k, width in enumerate(widths)]
    query, key, value, rates, outgate = pl.pallas_call(
        functools.partial(unpack_mix_kernel, lay, nrates),
        out_shape=[jax.ShapeDtypeStruct(shape, F32) for shape in shapes],
        name="unpack_mix",
    )(own)
    return query, key, value, rates.T, outgate
STEP = 4


def rms_parts(values):
    scale = lax.rsqrt(jnp.mean(values * values, axis=-1, keepdims=True) + EPS)
    return values * scale, scale


def bits(axis):
    return [1 << k for k in range((lax.axis_size(axis) - 1).bit_length())]


def trade(values, axis, bit):
    return lax.ppermute(values, axis, [(i, i ^ bit) for i in range(lax.axis_size(axis))])


def everyone(values):
    for axis in ("core", "dz", "sq", "sub"):
        for bit in bits(axis):
            values = values + trade(values, axis, bit)
    return values


def plus(left, right):
    return (left.astype(F32) + right.astype(F32)).astype(BF)


def column_step(values, k):
    rows, width = values.shape
    mine = (lax.axis_index("dz") >> k) & 1
    blocks = values.reshape(-1, 2, rows // (lax.axis_size("dz") >> k), width)
    part = lambda i: lax.dynamic_index_in_dim(blocks, i, 1, keepdims=False).reshape(-1, width)
    return plus(part(mine), trade(part(1 - mine), "dz", 1 << k))


def swap(values, which, parts):
    return lax.ppermute(values, "sub", [(i, i ^ which) for i in range(parts)])


def per_device(
    tokens, lengths, out_grad, ln1_gain, ln2_gain, onorm_gain, a_log, dt_bias,
    w_query, w_key, w_value, w_rates, w_outgate, w_out, w_gate, w_up, w_down,
):
    nsq, parts = lax.axis_size("sq"), lax.axis_size("sub")
    which_seq, place = lax.axis_index("sq"), lax.axis_index("sub")
    count = nsq * parts
    tok_dev, model = tokens.shape
    heads = a_log.shape[0] // count
    lay = Layout(heads)
    units = w_gate.shape[1]
    hw = heads * HEAD
    place_arr = place.astype(jnp.int32).reshape(1)

    mix_shard = pack_mix(lay, w_query, w_key, w_value, w_rates, w_outgate)
    ff_shards = pack(w_out, w_gate, w_up, w_down)
    w_mix = lax.all_gather(mix_shard, ("sq", "dz", "core"), axis=0, tiled=True)
    w_mix = w_mix.reshape(nsq, model, lay.width)
    walls = [
        lax.all_gather(shard, ("sq", "sub", "dz", "core"), axis=0, tiled=True).reshape(count, model, -1)
        for shard in ff_shards
    ]
    one, two = unit_halves(units)

    resid_in = tokens.astype(F32)
    normed_one, scale_one = rms_parts(resid_in)
    first = (normed_one * ln1_gain).astype(BF)
    first_seq = jnp.concatenate([first] + [swap(first, r, parts) for r in range(1, parts)], axis=0)

    pre = project(first_seq, w_mix)
    hpos = [(s * parts + place) * heads for s in range(nsq)]
    lanes = np.stack([8 * (c * nsq + s) + 3 * np.arange(heads) + 2 for c in range(STEP) for s in range(nsq)])

    def spread(values):
        mine = jnp.stack([lax.dynamic_slice_in_dim(values, hpos[s], heads) for s in range(nsq)])
        return jnp.zeros((128,), F32).at[lanes.ravel()].set(jnp.tile(mine.ravel(), STEP))

    params = jnp.stack([spread(-jnp.exp(a_log)), spread(dt_bias)])
    gain = onorm_gain.reshape(1, HEAD)
    mixed, *kept = mixer_forward(place_arr, parts, pre, params, gain, heads, STEP)

    got = [mixed] + [swap(mixed[:, r * tok_dev : (r + 1) * tok_dev], r, parts) for r in range(1, parts)]

    limit = jnp.sum(jnp.where(jnp.arange(nsq) == which_seq, lengths, 0)).astype(jnp.int32)
    scalars = jnp.stack([place.astype(jnp.int32), limit, lax.axis_index("core").astype(jnp.int32)])
    block = w_gate.shape[0]
    middle, second, grad_low = join(
        scalars, got, tokens, out_grad, walls[0], ln2_gain.reshape(1, model), parts, nsq, hw
    )
    def chips(pair):
        total = plus(pair[0], trade(pair[1], "core", 1))
        return total.reshape(count * model // 2, -1)

    def plane(values):
        return lax.psum_scatter(values, ("sq", "sub"), scatter_dimension=0, tiled=True)

    mlp_a, sg_a, *grads_a = feed_forward(
        scalars, second, grad_low, walls[0], hw, rounded(3 * one), one, block
    )
    grads_a, wall_b = lax.optimization_barrier((chips(grads_a), walls[1]))
    grads_a = plane(grads_a)
    mlp_b, sg_b, *acts_b = feed_forward_rest(second, grad_low, wall_b, two)
    block_out, middle_grad, middle_low, ln2_grad, *back = split(
        scalars, middle, (mlp_a, mlp_b), (sg_a, sg_b), grad_low, walls[0],
        ln2_gain.reshape(1, model), parts, nsq, hw,
    )
    arrived = [swap(back[r], r, parts) for r in range(1, parts)]
    grads_b = rest_grad(
        scalars, second, grad_low, middle_low, *acts_b, got, hw + rounded(3 * two), parts, nsq, hw, block
    )
    arrived, grads_b = lax.optimization_barrier((arrived, grads_b))
    dmixed = jnp.concatenate([back[0], *arrived], axis=1)
    dmixed, grads_b = lax.optimization_barrier((dmixed, chips(grads_b)))
    grads_b = plane(grads_b)
    steps = dmixed.shape[1] // CT // STEP
    head_steps = steps * 3 // 4
    dpre = (jnp.zeros((nsq * heads, HEAD, HEAD), F32), jnp.zeros((8, 128), F32))
    back_args = (place_arr, parts, pre, params, gain, *kept, dmixed, heads, STEP)
    *dpre, carry, small = mixer_backward(*back_args, 0, head_steps, dpre)
    grads_a = column_step(grads_a, 0)
    carry, grads_b, grads_a = lax.optimization_barrier((carry, grads_b, grads_a))
    own_b = lax.psum_scatter(grads_b, "dz", scatter_dimension=0, tiled=True)
    own_a = column_step(grads_a, 1)
    for k in range(2, len(bits("dz"))):
        own_a = column_step(own_a, k)
    *dpre, carry, small = mixer_backward(*back_args, head_steps, steps - head_steps, (carry, small, *dpre))

    def back_rows(values, r):
        rows = slice(r * tok_dev, (r + 1) * tok_dev)
        total = dot_nt(values[0][rows], w_mix[0])
        for s in range(1, nsq):
            total = total + dot_nt(values[s][rows], w_mix[s])
        return total, jnp.sum(total * first_seq[rows].astype(F32), axis=0)

    mix_grads = jnp.concatenate([dot_tn(first_seq, dpre[s]).astype(BF) for s in range(nsq)], axis=0)
    dpre, mix_grads, own_a = lax.optimization_barrier((dpre, mix_grads, own_a))
    own_out, own_gate, own_up, own_down = unpack(own_a, own_b, hw, units)
    mix_own = lax.psum_scatter(mix_grads, ("sq", "dz", "core"), scatter_dimension=0, tiled=True)
    leaving = [back_rows(dpre, r) for r in range(1, parts)]
    arriving = [swap(leaving[r - 1][0].astype(BF), r, parts) for r in range(1, parts)]
    first_grad, ln1_grad = back_rows(dpre, 0)
    for r in range(1, parts):
        ln1_grad = ln1_grad + leaving[r - 1][1]
    ln1_grad = ln1_grad / ln1_gain
    first_grad, ln1_grad = lax.optimization_barrier((first_grad, ln1_grad))
    for r in range(1, parts):
        first_grad = first_grad + arriving[r - 1].astype(F32)
    scaled = first_grad * ln1_gain
    input_back = scale_one * (scaled - normed_one * jnp.mean(scaled * normed_one, axis=-1, keepdims=True))
    tokens_grad = (middle_grad + input_back).astype(BF)

    def gather_heads(row):
        mine = jnp.sum(row[lanes].reshape(STEP, nsq, heads), axis=0)
        full = jnp.zeros(a_log.shape, F32)
        for s in range(nsq):
            full = lax.dynamic_update_slice_in_dim(full, mine[s], hpos[s], 0)
        return full

    a_grad, dt_grad = gather_heads(small[2]), gather_heads(small[1])
    total = everyone(jnp.concatenate([ln1_grad, ln2_grad[0], small[0], a_grad, dt_grad]))
    marks = np.cumsum([0, model, model, HEAD, a_log.shape[0], a_log.shape[0]])
    return (
        block_out, tokens_grad, *[total[i:j] for i, j in zip(marks[:-1], marks[1:])],
        *unpack_mix(mix_own, lay, w_rates.shape[1]),
        own_out, own_gate, own_up, own_down,
    )


def solution(mesh):
    dp, tensor = mesh.shape["dp"], mesh.shape["tensor"]

    def run(*args):
        nsq = args[1].shape[0] // dp
        split = Mesh(
            mesh.devices.reshape(dp // 2, 2, nsq, tensor // nsq), ("dz", "core", "sq", "sub")
        )
        rows = P(("dz", "core", "sq", "sub"), None)
        down = P(("dz", "core"), ("sq", "sub"))
        across = P(("sq", "sub"), ("dz", "core"))
        in_specs = (rows, P(("dz", "core")), rows) + (P(),) * 5 + (down,) * 5 + (across, down, down, across)
        out_specs = (rows, rows) + (P(),) * 5 + (down,) * 5 + (across, down, down, across)
        return jax.shard_map(
            per_device, mesh=split, in_specs=in_specs, out_specs=out_specs, check_vma=False
        )(*args)

    return run
```
